512 devices in a mesh: slab: 128 (over y_lo, x, z), cross: 4 (over y_hi, core).
Axes of the slice: x: 4, y: 4 (y_hi: 2, y_lo: 2; y = y_hi * 2 + y_lo), z: 16, core: 2. Of those that a mesh axis runs over, the one named last changes fastest.
Arguments:
- gas_state: float32 [16, 1024, 8192], P(None, 'slab', 'cross'), may hold values from -4 to 4, as said below
- parcel_record: float32 [5, 2097152], P(None, ('slab', 'cross')), may hold values from -4 to 4, as said below
- condensed_shares: float32 [12, 2097152], P(None, ('slab', 'cross')), may hold values from 0.02 to 0.2
- surface_steam_factor: float32 [12], replicated, may hold values from 0.2 to 2
- fine_cell: int32 [2097152], P(('slab', 'cross')), may hold values from 0 to 20479, as said below
- block_counts: int32 [16384], P(('slab', 'cross')), may hold values from 16 to 128, as said below
Outputs:
- parcel_next: float32 [5, 2097152], P(None, ('slab', 'cross'))
- fine_source: float32 [16, 1024, 8192], P(None, 'slab', 'cross')
- correction: float32 [64, 4096], replicated
The draws below stay inside these ranges and needn't reach their ends.
Inputs may be any that keep to these rules, and one draw needn't show every extreme that they name: fine_cell is plane * 2048 + k, with plane 0 and 9 the neighbouring slabs' last and first planes; it never points outside the gas mesh, and is non-decreasing over each device's 4096 slots. The live parcels of each aligned block of 128 slots are its first block_counts slots; the last block of each device's 4096 slots is full. `gas_state`: rows 0 to 2 velocity, row 3 temperature from 1 to 2, rows 4 on vapour fractions from 0 to 0.1. `parcel_record`: rows 0 to 2 velocity, row 3 temperature from 0.6 to 0.9, row 4 mass from 0.5 to 3.
All inputs are finite; a program needn't handle non-finite values.
Results may differ from the reference program's by a relative error of at most 0.00002.
Values sent between devices are 32-bit elements; how exact they have to be, the bound alone decides.
A program may use at most 64 MiB of HBM per device.

```python
import math
import jax
import jax.numpy as jnp

SPECIES = 12
PLANES = 8
CROSS_CELLS = 2048
PAR_DEV = 4096
BLOCK = 128
COARSE = 64
SWEEPS = 4
PTOT = 2097152
N_SLAB = 128
N_CROSS = 4


def draw_gas_state(key, part):
    domain_layer_sequence = PLANES * N_SLAB
    traversed_mesh_sites_whole = CROSS_CELLS * N_CROSS
    key_velocity = jax.random.fold_in(key, 11)
    thermal_noise_seed = jax.random.fold_in(key, 12)
    key_vapour = jax.random.fold_in(key, 13)
    motion_components = jnp.clip(jax.random.normal(key_velocity, (3, domain_layer_sequence, traversed_mesh_sites_whole), jnp.float32), -4.0, 4.0)
    thermal_reading = jax.random.uniform(thermal_noise_seed, (1, domain_layer_sequence, traversed_mesh_sites_whole), jnp.float32, 1.0, 2.0)
    steam_share = jax.random.uniform(key_vapour, (SPECIES, domain_layer_sequence, traversed_mesh_sites_whole), jnp.float32, 0.0, 0.1)
    return jnp.concatenate([motion_components, thermal_reading, steam_share], axis=0)


def draw_parcel_record(key, part):
    position_number_whole = PAR_DEV * N_SLAB * N_CROSS
    key_velocity = jax.random.fold_in(key, 21)
    thermal_noise_seed = jax.random.fold_in(key, 22)
    key_weight = jax.random.fold_in(key, 23)
    motion_components = jnp.clip(jax.random.normal(key_velocity, (3, position_number_whole), jnp.float32), -4.0, 4.0)
    thermal_reading = jax.random.uniform(thermal_noise_seed, (1, position_number_whole), jnp.float32, 0.6, 0.9)
    natural_log_weight = jax.random.uniform(key_weight, (1, position_number_whole), jnp.float32, jnp.log(0.5), jnp.log(3.0))
    return jnp.concatenate([motion_components, thermal_reading, jnp.exp(natural_log_weight)], axis=0)


def draw_fine_cell(key, part):
    devices_all = N_SLAB * N_CROSS
    slab_ids = jnp.arange(devices_all, dtype=jnp.int32) // N_CROSS
    lowest = jnp.where(slab_ids == 0, 1, 0).astype(jnp.int32)
    highest = jnp.where(slab_ids == N_SLAB - 1, PLANES, PLANES + 1).astype(jnp.int32)
    key_plane = jax.random.fold_in(key, 31)
    key_column = jax.random.fold_in(key, 32)
    plane_drawn = jax.random.randint(key_plane, (devices_all, PAR_DEV), lowest[:, None], highest[:, None] + 1, jnp.int32)
    column_drawn = jax.random.randint(key_column, (devices_all, PAR_DEV), 0, CROSS_CELLS, jnp.int32)
    cells = jnp.sort(plane_drawn * CROSS_CELLS + column_drawn, axis=1)
    return cells.reshape(-1).astype(jnp.int32)


def draw_block_counts(key, part):
    blocks_all = PAR_DEV * N_SLAB * N_CROSS // BLOCK
    blocks_device = PAR_DEV // BLOCK
    block_ids = jnp.arange(blocks_all, dtype=jnp.int32)
    slab_ids = block_ids // blocks_device // N_CROSS
    last_block = block_ids % blocks_device == blocks_device - 1
    dense_slabs = max(1, N_SLAB // 4)
    lowest = jnp.where((slab_ids < dense_slabs) | last_block, BLOCK, 16).astype(jnp.int32)
    return jax.random.randint(jax.random.fold_in(key, 41), (blocks_all,), lowest, BLOCK + 1, jnp.int32)


def block_levels(stream_key, shape, cuts, low, top_value):
    factor_of, own = 1.0, jax.random.fold_in(stream_key, 6)
    for axis_at, parts in cuts:
        heights = jnp.exp(jax.random.uniform(jax.random.fold_in(own, axis_at), (parts,), jnp.float32, low / len(cuts), top_value / len(cuts)))
        factor_of = factor_of * jnp.repeat(heights, shape[axis_at] // parts).reshape([-1 if axis == axis_at else 1 for axis in range(len(shape))])
    return factor_of


def setup_inputs(seed: int = 0) -> dict:
    splits = jax.random.split(jax.random.key(seed), 7)
    gas_state = draw_gas_state(jax.random.fold_in(splits[6], 71), 0)
    parcel_record = draw_parcel_record(jax.random.fold_in(splits[6], 71), 0)
    condensed_shares = jnp.clip(0.02 + 0.18 * jax.random.uniform(splits[2], (SPECIES, PTOT), jnp.float32) ** block_levels(splits[2], (SPECIES, PTOT), ((1, 512),), -0.2, 0.2), 0.02, 0.2)
    surface_steam_factor = jnp.clip(jnp.exp(jax.random.uniform(splits[3], (SPECIES,), jnp.float32, math.log(0.2), math.log(2.0))), 0.2, 2.0)
    fine_cell = draw_fine_cell(jax.random.fold_in(splits[6], 71), 0)
    block_counts = draw_block_counts(jax.random.fold_in(splits[6], 71), 0)
    return {"gas_state": gas_state, "parcel_record": parcel_record, "condensed_shares": condensed_shares, "surface_steam_factor": surface_steam_factor, "fine_cell": fine_cell, "block_counts": block_counts}


drag_rate = 0.5
evap_rate = 0.08
warming_speed = 0.3
latent_boiling_energy = 0.5
vapour_heat = 1.5
volume_inverse = 4.0


def advance(ambient_layer_fields, parcel_record, condensed_shares, surface_steam_factor, alive_mask):
    gas_velocity = ambient_layer_fields[0:3]
    ambient_thermal_level = ambient_layer_fields[3]
    gas_vapour = ambient_layer_fields[4:]
    parcel_velocity = parcel_record[0:3]
    parcel_thermal_level = parcel_record[3]
    parcel_weight_amount = parcel_record[4]
    slip_velocity = gas_velocity - parcel_velocity
    slip_squared = jnp.sum(slip_velocity * slip_velocity, axis=0)
    drag_factor = drag_rate * jnp.power(parcel_weight_amount, -2.0 / 3.0) * (1.0 + 0.15 * jnp.power(slip_squared + 1.0, 0.3435))
    following_motion = (parcel_velocity + drag_factor * gas_velocity) / (1.0 + drag_factor)
    surface_steam_share = condensed_shares * surface_steam_factor[:, None] * jnp.exp(2.0 * (parcel_thermal_level - 0.75))
    species_rates = evap_rate * parcel_weight_amount * (surface_steam_share - gas_vapour)
    evaporated_weight = jnp.sum(species_rates, axis=0)
    thermal_exchange = warming_speed * (ambient_thermal_level - parcel_thermal_level) * jnp.power(parcel_weight_amount, 1.0 / 3.0)
    following_thermal_level = parcel_thermal_level + (thermal_exchange - latent_boiling_energy * evaporated_weight) / parcel_weight_amount
    following_weight = parcel_weight_amount - evaporated_weight
    momentum_terms = parcel_weight_amount * (parcel_velocity - following_motion) + evaporated_weight * following_motion
    energy_terms = vapour_heat * evaporated_weight - thermal_exchange
    source_terms = jnp.concatenate([momentum_terms, energy_terms[None], species_rates], axis=0)
    source_terms = source_terms * (alive_mask * volume_inverse)
    updated_parcel_record = jnp.concatenate([following_motion, following_thermal_level[None], following_weight[None]], axis=0)
    parcel_next = jnp.where(alive_mask[None] > 0.5, updated_parcel_record, parcel_record)
    return source_terms, parcel_next, evaporated_weight * alive_mask


def neighbours(values_grid):
    edge = values_grid.shape[0]
    padded_x = jnp.pad(values_grid, ((1, 1), (0, 0)))
    summed = padded_x[2:] + padded_x[:-2]
    padded_y = jnp.pad(values_grid, ((0, 0), (edge, edge)))
    summed = summed + padded_y[:, 2 * edge:] + padded_y[:, :-2 * edge]
    padded_z = jnp.pad(values_grid, ((0, 0), (1, 1)))
    depth = jnp.arange(values_grid.shape[1], dtype=jnp.int32) % edge
    upper_mask = (depth < edge - 1).astype(values_grid.dtype)
    lower_mask = (depth > 0).astype(values_grid.dtype)
    return summed + padded_z[:, 2:] * upper_mask + padded_z[:, :-2] * lower_mask


def relax(coarse_source):
    solution = jnp.zeros_like(coarse_source)
    for sweep in range(SWEEPS):
        solution = (neighbours(solution) + coarse_source) / 6.0
    return solution


def reference(gas_state, parcel_record, condensed_shares, surface_steam_factor, fine_cell, block_counts):
    position_number_whole = parcel_record.shape[1]
    per_device = position_number_whole // (N_SLAB * N_CROSS)
    slot_ids = jnp.arange(position_number_whole, dtype=jnp.int32)
    device_ids = slot_ids // per_device
    slab_ids = device_ids // N_CROSS
    cross_ids = device_ids % N_CROSS
    alive_mask = ((slot_ids % BLOCK) < block_counts[slot_ids // BLOCK]).astype(jnp.float32)
    plane_ext = fine_cell // CROSS_CELLS
    column = fine_cell % CROSS_CELLS
    global_plane = slab_ids * PLANES + plane_ext - 1
    global_cross = cross_ids * CROSS_CELLS + column
    domain_layer_sequence = PLANES * N_SLAB
    traversed_mesh_sites_whole = CROSS_CELLS * N_CROSS
    global_index = (global_plane * traversed_mesh_sites_whole + global_cross).astype(jnp.int32)
    fields = gas_state.shape[0]
    gas_flat = gas_state.reshape(fields, domain_layer_sequence * traversed_mesh_sites_whole)
    ambient_layer_fields = jnp.take(gas_flat, global_index, axis=1)
    source_terms, parcel_next, evaporated_weight = advance(ambient_layer_fields, parcel_record, condensed_shares, surface_steam_factor, alive_mask)
    fine_source = jnp.zeros((fields, domain_layer_sequence * traversed_mesh_sites_whole), jnp.float32).at[:, global_index].add(source_terms)
    fine_source = fine_source.reshape(fields, domain_layer_sequence, traversed_mesh_sites_whole)
    squared = COARSE * COARSE
    fine_per_coarse = domain_layer_sequence // COARSE
    cross_per_coarse = traversed_mesh_sites_whole // squared
    coarse_index = ((global_plane // fine_per_coarse) * squared + global_cross // cross_per_coarse).astype(jnp.int32)
    coarse_source = jnp.zeros((COARSE * squared,), jnp.float32).at[coarse_index].add(evaporated_weight)
    coarse_source = coarse_source.reshape(COARSE, squared)
    correction = relax(coarse_source)
    return (parcel_next, fine_source, correction)
```

```python
import jax
import jax.numpy as jnp
from jax import lax
from jax.sharding import PartitionSpec as P

BLOCK = 128
COARSE = 64
SWEEPS = 4


drag_rate = 0.5
evap_rate = 0.08
warming_speed = 0.3
latent_boiling_energy = 0.5
vapour_heat = 1.5
volume_inverse = 4.0


def with_halo(shard, sides, width):
    for axis, dim in sides:
        devices, length = (lax.axis_size(axis), shard.shape[dim])
        up = [(i, (i + 1) % devices) for i in range(devices - 1)]
        down = [(j, i) for i, j in up]
        last = lax.slice_in_dim(shard, length - width, length, axis=dim)
        leading = lax.slice_in_dim(shard, 0, width, axis=dim)
        before = lax.ppermute(last, axis, up)
        after = lax.ppermute(leading, axis, down)
        shard = jnp.concatenate([before, shard, after], axis=dim)
    return shard


def shifted(shard, axis, by):
    devices = lax.axis_size(axis)
    pairs = [(i, i + by) for i in range(devices) if 0 <= i + by < devices]
    return lax.ppermute(shard, axis, pairs)


def advance(
    ambient_layer_fields, parcel_record, condensed_shares, surface_steam_factor, alive_mask
):
    gas_velocity = ambient_layer_fields[0:3]
    ambient_thermal_level = ambient_layer_fields[3]
    gas_vapour = ambient_layer_fields[4:]
    parcel_velocity = parcel_record[0:3]
    parcel_thermal_level = parcel_record[3]
    parcel_weight_amount = parcel_record[4]
    slip_velocity = gas_velocity - parcel_velocity
    slip_squared = jnp.sum(slip_velocity * slip_velocity, axis=0)
    drag_factor = (
        drag_rate
        * jnp.power(parcel_weight_amount, -2.0 / 3.0)
        * (1.0 + 0.15 * jnp.power(slip_squared + 1.0, 0.3435))
    )
    following_motion = (parcel_velocity + drag_factor * gas_velocity) / (1.0 + drag_factor)
    surface_steam_share = (
        condensed_shares
        * surface_steam_factor[:, None]
        * jnp.exp(2.0 * (parcel_thermal_level - 0.75))
    )
    species_rates = evap_rate * parcel_weight_amount * (surface_steam_share - gas_vapour)
    evaporated_weight = jnp.sum(species_rates, axis=0)
    thermal_exchange = (
        warming_speed
        * (ambient_thermal_level - parcel_thermal_level)
        * jnp.power(parcel_weight_amount, 1.0 / 3.0)
    )
    following_thermal_level = (
        parcel_thermal_level
        + (thermal_exchange - latent_boiling_energy * evaporated_weight) / parcel_weight_amount
    )
    following_weight = parcel_weight_amount - evaporated_weight
    momentum_terms = (
        parcel_weight_amount * (parcel_velocity - following_motion)
        + evaporated_weight * following_motion
    )
    energy_terms = vapour_heat * evaporated_weight - thermal_exchange
    source_terms = jnp.concatenate([momentum_terms, energy_terms[None], species_rates], axis=0)
    source_terms = source_terms * (alive_mask * volume_inverse)
    updated_parcel_record = jnp.concatenate(
        [following_motion, following_thermal_level[None], following_weight[None]], axis=0
    )
    parcel_next = jnp.where(alive_mask[None] > 0.5, updated_parcel_record, parcel_record)
    return (source_terms, parcel_next, evaporated_weight * alive_mask)


def neighbours(values_grid):
    edge = values_grid.shape[0]
    padded_x = jnp.pad(values_grid, ((1, 1), (0, 0)))
    summed = padded_x[2:] + padded_x[:-2]
    padded_y = jnp.pad(values_grid, ((0, 0), (edge, edge)))
    summed = summed + padded_y[:, 2 * edge :] + padded_y[:, : -2 * edge]
    padded_z = jnp.pad(values_grid, ((0, 0), (1, 1)))
    depth = jnp.arange(values_grid.shape[1], dtype=jnp.int32) % edge
    upper_mask = (depth < edge - 1).astype(values_grid.dtype)
    lower_mask = (depth > 0).astype(values_grid.dtype)
    return summed + padded_z[:, 2:] * upper_mask + padded_z[:, :-2] * lower_mask


def relax(coarse_source):
    solution = jnp.zeros_like(coarse_source)
    for sweep in range(SWEEPS):
        solution = (neighbours(solution) + coarse_source) / 6.0
    return solution


def body(gas_state, parcel_record, condensed_shares, surface_steam_factor, fine_cell, block_counts):
    fields = gas_state.shape[0]
    planes = gas_state.shape[1]
    cross_cells = gas_state.shape[2]
    slab_count = lax.axis_size("slab")
    cross_count = lax.axis_size("cross")
    padded_gas = with_halo(gas_state, (("slab", 1),), 1)
    gas_flat = padded_gas.reshape(fields, (planes + 2) * cross_cells)
    ambient_layer_fields = jnp.take(gas_flat, fine_cell, axis=1)
    slot_in_block = jnp.arange(BLOCK, dtype=jnp.int32)
    alive_mask = (slot_in_block[None, :] < block_counts[:, None]).reshape(-1).astype(jnp.float32)
    source_terms, parcel_next, evaporated_weight = advance(
        ambient_layer_fields, parcel_record, condensed_shares, surface_steam_factor, alive_mask
    )
    extended = (
        jnp.zeros((fields, (planes + 2) * cross_cells), jnp.float32)
        .at[:, fine_cell]
        .add(source_terms)
    )
    extended = extended.reshape(fields, planes + 2, cross_cells)
    from_above = shifted(extended[:, 0], "slab", -1)
    from_below = shifted(extended[:, planes + 1], "slab", 1)
    fine_source = extended[:, 1 : planes + 1]
    fine_source = fine_source.at[:, planes - 1].add(from_above)
    fine_source = fine_source.at[:, 0].add(from_below)
    fold = cross_cells * cross_count // (COARSE * COARSE)
    mass = 0.25 * fine_source[4:].sum(axis=(0, 1))
    piece = mass.reshape(cross_cells // fold, fold).sum(axis=1)
    pieces = lax.all_gather(piece, ("slab", "cross"))
    coarse_source = pieces.reshape(COARSE, slab_count // COARSE, COARSE * COARSE).sum(axis=1)
    correction = relax(coarse_source)
    return (parcel_next, fine_source, correction)


def solution(mesh):
    in_specs = (
        P(None, "slab", "cross"),
        P(None, ("slab", "cross")),
        P(None, ("slab", "cross")),
        P(),
        P(("slab", "cross")),
        P(("slab", "cross")),
    )
    out_specs = (P(None, ("slab", "cross")), P(None, "slab", "cross"), P())
    return jax.shard_map(body, mesh=mesh, in_specs=in_specs, out_specs=out_specs, check_vma=False)
```

```python
import jax
import jax.numpy as jnp
from jax import lax
from jax.experimental import pallas as pl
from jax.experimental.pallas import tpu as pltpu
from jax.sharding import PartitionSpec as P

BLOCK = 128
COARSE = 64


drag_rate = 0.5
evap_rate = 0.08
warming_speed = 0.3
latent_boiling_energy = 0.5
vapour_heat = 1.5
volume_inverse = 4.0


def with_halo(shard, sides, width):
    for axis, dim in sides:
        devices, length = (lax.axis_size(axis), shard.shape[dim])
        up = [(i, (i + 1) % devices) for i in range(devices - 1)]
        down = [(j, i) for i, j in up]
        last = lax.slice_in_dim(shard, length - width, length, axis=dim)
        leading = lax.slice_in_dim(shard, 0, width, axis=dim)
        before = lax.ppermute(last, axis, up)
        after = lax.ppermute(leading, axis, down)
        shard = jnp.concatenate([before, shard, after], axis=dim)
    return shard


def advance(
    ambient_layer_fields, parcel_record, condensed_shares, surface_steam_factor, alive_mask
):
    gas_velocity = ambient_layer_fields[0:3]
    ambient_thermal_level = ambient_layer_fields[3]
    gas_vapour = ambient_layer_fields[4:]
    parcel_velocity = parcel_record[0:3]
    parcel_thermal_level = parcel_record[3]
    parcel_weight_amount = parcel_record[4]
    slip_velocity = gas_velocity - parcel_velocity
    slip_squared = jnp.sum(slip_velocity * slip_velocity, axis=0)
    drag_factor = (
        drag_rate
        * jnp.power(parcel_weight_amount, -2.0 / 3.0)
        * (1.0 + 0.15 * jnp.power(slip_squared + 1.0, 0.3435))
    )
    following_motion = (parcel_velocity + drag_factor * gas_velocity) / (1.0 + drag_factor)
    surface_steam_share = (
        condensed_shares
        * surface_steam_factor[:, None]
        * jnp.exp(2.0 * (parcel_thermal_level - 0.75))
    )
    species_rates = evap_rate * parcel_weight_amount * (surface_steam_share - gas_vapour)
    evaporated_weight = jnp.sum(species_rates, axis=0)
    thermal_exchange = (
        warming_speed
        * (ambient_thermal_level - parcel_thermal_level)
        * jnp.power(parcel_weight_amount, 1.0 / 3.0)
    )
    following_thermal_level = (
        parcel_thermal_level
        + (thermal_exchange - latent_boiling_energy * evaporated_weight) / parcel_weight_amount
    )
    following_weight = parcel_weight_amount - evaporated_weight
    momentum_terms = (
        parcel_weight_amount * (parcel_velocity - following_motion)
        + evaporated_weight * following_motion
    )
    energy_terms = vapour_heat * evaporated_weight - thermal_exchange
    source_terms = jnp.concatenate([momentum_terms, energy_terms[None], species_rates], axis=0)
    source_terms = source_terms * (alive_mask * volume_inverse)
    updated_parcel_record = jnp.concatenate(
        [following_motion, following_thermal_level[None], following_weight[None]], axis=0
    )
    parcel_next = jnp.where(alive_mask[None] > 0.5, updated_parcel_record, parcel_record)
    return (source_terms, parcel_next, evaporated_weight * alive_mask)


LINE = 16
RING = 4
LANES = 128
ROWS = 8


def spread_kernel(
    own_ref, outer_ref, edge_ref, halo_ref, grid_ref, got,
    pair_send, pair_recv, edge_send, edge_recv, line_send, line_recv,
    minor_send, minor_recv, major_send, major_recv, core_send, core_recv,
):
    slabs = 2 * RING * LINE
    slab = lax.axis_index("slab")
    cross = lax.axis_index("cross")
    core = lax.rem(cross, 2)
    z = lax.rem(slab, LINE)
    x = lax.rem(lax.div(slab, LINE), RING)
    y = lax.div(cross, 2) * 2 + lax.div(slab, RING * LINE)
    odd = lax.rem(slab, 2)
    sign = 2 * odd - 1
    pair = lax.div(slab, 2)
    line_pair = lax.div(z, 2)
    major = core * x + (1 - core) * y
    minor = core * y + (1 - core) * x

    def near(by):
        return (lax.rem(slab + by + slabs, slabs), cross)

    def place(at_x, at_y, at_z):
        return (lax.rem(at_y, 2) * (RING * LINE) + at_x * LINE + at_z, lax.div(at_y, 2) * 2 + core)

    def in_line(by):
        return lax.rem(z + by + LINE, LINE)

    def minor_peer(other):
        return place(core * x + (1 - core) * other, core * other + (1 - core) * y, z)

    def major_peer(other):
        return place(core * other + (1 - core) * x, core * y + (1 - core) * other, z)

    def turn(own, by):
        return lax.rem(own + by, RING)

    def copy(src, dst, send, recv, device):
        return pltpu.make_async_remote_copy(
            src_ref=src, dst_ref=dst, send_sem=send, recv_sem=recv,
            device_id=device, device_id_type=pl.DeviceIdType.MESH,
        )

    other_core = (slab, cross + 1 - 2 * core)
    line_from = [sign * k for k in (1, 3, 5, 7)] + [-sign * k for k in (2, 4, 6)]
    low = lax.rem(2 * pair - 1 + slabs, slabs)
    high = lax.rem(2 * pair + 2, slabs)

    barrier = pltpu.get_barrier_semaphore()
    sources = [near(-sign), (low, cross), (high, cross), near(-1), near(1)]
    sources += [place(x, y, in_line(by)) for by in line_from]
    sources += [minor_peer(turn(minor, by)) for by in (1, 2, 3)]
    sources += [major_peer(turn(major, by)) for by in (1, 2, 3)]
    sources += [other_core]
    for device in sources:
        pl.semaphore_signal(barrier, inc=1, device_id=device, device_id_type=pl.DeviceIdType.MESH)
    pl.semaphore_wait(barrier, len(sources))

    copies = [
        copy(own_ref, got.at[0], pair_send.at[0], pair_recv.at[0], near(-sign)),
        copy(outer_ref, got.at[2 - odd], pair_send.at[1], pair_recv.at[2 - odd], near(sign)),
        copy(outer_ref, got.at[2 - odd], pair_send.at[2], pair_recv.at[2 - odd], near(2 * sign)),
    ]
    for each in copies:
        each.start()
    for slot in range(3):
        copy(own_ref, got.at[slot], pair_send.at[slot], pair_recv.at[slot], near(1)).wait_recv()
    grid_ref[core, major, minor, line_pair] = (own_ref[...] + got[0]) + (got[1] + got[2])
    edges = [
        copy(edge_ref.at[0], halo_ref.at[1], edge_send.at[0], edge_recv.at[1], near(-1)),
        copy(edge_ref.at[1], halo_ref.at[0], edge_send.at[1], edge_recv.at[0], near(1)),
    ]
    tile = grid_ref.at[core, major, minor, line_pair]
    line = [
        copy(tile, tile, line_send.at[k - 1], line_recv.at[line_pair], place(x, y, in_line(sign * k)))
        for k in range(1, 8)
    ]
    for each in line:
        each.start()
    for each in edges:
        each.start()
    for by in line_from:
        other = lax.div(in_line(by), 2)
        copy(
            tile, grid_ref.at[core, major, minor, other], line_send.at[0], line_recv.at[other], near(1)
        ).wait_recv()

    block = grid_ref.at[core, major, minor]
    minors = [
        copy(block, block, minor_send.at[by - 1], minor_recv.at[minor], minor_peer(turn(minor, by)))
        for by in (1, 2, 3)
    ]
    for each in minors:
        each.start()
    for by in (1, 2, 3):
        other = turn(minor, by)
        copy(
            block, grid_ref.at[core, major, other], minor_send.at[0], minor_recv.at[other], near(1)
        ).wait_recv()

    row = grid_ref.at[core, major]
    majors = [
        copy(row, row, major_send.at[by - 1], major_recv.at[major], major_peer(turn(major, by)))
        for by in (1, 2, 3)
    ]
    for each in majors:
        each.start()
    cores = []
    for by in range(RING):
        other = turn(major, by)
        arrived = grid_ref.at[core, other]
        if by:
            copy(row, arrived, major_send.at[0], major_recv.at[other], near(1)).wait_recv()
        each = copy(arrived, arrived, core_send.at[by], core_recv.at[other], other_core)
        each.start()
        cores.append(each)
    for by in range(RING):
        far = grid_ref.at[1 - core, by]
        copy(far, far, core_send.at[0], core_recv.at[by], other_core).wait_recv()
    for slot in range(2):
        copy(edge_ref.at[0], halo_ref.at[slot], edge_send.at[0], edge_recv.at[slot], near(1)).wait_recv()
    for each in copies + edges + line + minors + majors + cores:
        each.wait_send()


def spread(own, outer, edges):
    dma = pltpu.SemaphoreType.DMA
    vmem = pl.BlockSpec(memory_space=pltpu.VMEM)
    hbm = pl.BlockSpec(memory_space=pl.ANY)
    return pl.pallas_call(
        spread_kernel,
        out_shape=(
            jax.ShapeDtypeStruct(edges.shape, jnp.float32),
            jax.ShapeDtypeStruct((2, RING, RING, LINE // 2, ROWS, LANES), jnp.float32),
        ),
        in_specs=[vmem, vmem, hbm],
        out_specs=(hbm, vmem),
        scratch_shapes=[
            pltpu.VMEM((3, ROWS, LANES), jnp.float32),
            dma((3,)), dma((3,)), dma((2,)), dma((2,)), dma((7,)), dma((LINE // 2,)),
            dma((3,)), dma((RING,)), dma((3,)), dma((RING,)), dma((RING,)), dma((RING,)),
        ],
        compiler_params=pltpu.CompilerParams(
            collective_id=0, has_side_effects=True, vmem_limit_bytes=8 << 20
        ),
        name="spread",
    )(own, outer, edges)


def finish_kernel(base_ref, halo_ref, grid_ref, fine_ref, out_ref, source, even, uneven):
    fields, planes, cells = base_ref.shape
    row = lax.broadcasted_iota(jnp.int32, (planes, cells), 0)
    first = row == 0
    last = row == planes - 1
    for f in range(fields):
        low = jnp.broadcast_to(halo_ref[0, f : f + 1, :], (planes, cells))
        high = jnp.broadcast_to(halo_ref[1, f : f + 1, :], (planes, cells))
        fine_ref[f] = base_ref[f] + jnp.where(first, low, jnp.where(last, high, 0.0))

    half = RING * RING * (LINE // 2) * ROWS
    tiles = COARSE * COARSE // LANES
    blank = jnp.zeros((ROWS, tiles * LANES), jnp.float32)
    for held in (even, uneven):
        held[0:ROWS, :] = blank
        held[COARSE + ROWS : COARSE + 2 * ROWS, :] = blank
    for k in range(tiles):
        y_hi, core, i = k // 16, (k // 8) % 2, k % 8
        cols = slice(k * LANES, (k + 1) * LANES)
        for t in range(COARSE // ROWS):
            y_lo, x = t // RING, t % RING
            if core == 0:
                at = ((y_hi * 2 + y_lo) * RING + x) * (LINE // 2) * ROWS + i
            else:
                at = half + (x * RING + y_hi * 2 + y_lo) * (LINE // 2) * ROWS + i
            value = grid_ref[pl.ds(at, ROWS, stride=ROWS), :] * (1.0 / 6.0)
            source[t * ROWS : (t + 1) * ROWS, cols] = value
            even[(t + 1) * ROWS : (t + 2) * ROWS, cols] = value

    lane = lax.broadcasted_iota(jnp.int32, (ROWS, LANES), 1)
    edge = LANES // 2
    depth = lax.rem(lane, edge)
    upper = depth < edge - 1
    lower = depth > 0
    left = lane < edge

    def sweep(src, dst, top):
        def one(t, carry):
            at = pl.multiple_of(t * ROWS, ROWS)
            rolled = []
            mid = []
            for k in range(tiles):
                cols = slice(k * LANES, (k + 1) * LANES)
                value = src[pl.ds(at + ROWS, ROWS), cols]
                mid.append(value)
                rolled.append(pltpu.roll(value, edge, 1))
            none = jnp.zeros((ROWS, LANES), jnp.float32)
            for k in range(tiles):
                cols = slice(k * LANES, (k + 1) * LANES)
                before = rolled[k - 1] if k else none
                after = rolled[k + 1] if k + 1 < tiles else none
                total = rolled[k] + jnp.where(left, before, after)
                total += jnp.where(upper, pltpu.roll(mid[k], LANES - 1, 1), 0.0)
                total += jnp.where(lower, pltpu.roll(mid[k], 1, 1), 0.0)
                sub = lax.broadcasted_iota(jnp.int32, (ROWS, LANES), 0)
                up = src[pl.ds(at, ROWS), cols]
                down = src[pl.ds(at + 2 * ROWS, ROWS), cols]
                total += jnp.where(sub == 0, pltpu.roll(up, 1, 0), pltpu.roll(mid[k], 1, 0))
                total += jnp.where(
                    sub == ROWS - 1, pltpu.roll(down, ROWS - 1, 0), pltpu.roll(mid[k], ROWS - 1, 0)
                )
                dst[pl.ds(at + top, ROWS), cols] = total * (1.0 / 6.0) + source[pl.ds(at, ROWS), cols]
            return carry

        lax.fori_loop(0, COARSE // ROWS, one, 0)

    sweep(even, uneven, ROWS)
    sweep(uneven, even, ROWS)
    sweep(even, out_ref, 0)


def finish(base, halo, grid):
    side = (COARSE, COARSE * COARSE)
    padded = (COARSE + 2 * ROWS, COARSE * COARSE)
    vmem = pl.BlockSpec(memory_space=pltpu.VMEM)
    return pl.pallas_call(
        finish_kernel,
        out_shape=(
            jax.ShapeDtypeStruct(base.shape, jnp.float32),
            jax.ShapeDtypeStruct(side, jnp.float32),
        ),
        in_specs=[vmem, vmem, vmem],
        out_specs=(vmem, vmem),
        scratch_shapes=[
            pltpu.VMEM(side, jnp.float32),
            pltpu.VMEM(padded, jnp.float32),
            pltpu.VMEM(padded, jnp.float32),
        ],
        compiler_params=pltpu.CompilerParams(vmem_limit_bytes=32 << 20),
        name="finish",
    )(base, halo, grid.reshape(-1, LANES))


def body(gas_state, parcel_record, condensed_shares, surface_steam_factor, fine_cell, block_counts):
    fields = gas_state.shape[0]
    planes = gas_state.shape[1]
    cross_cells = gas_state.shape[2]
    padded_gas = with_halo(gas_state, (("slab", 1),), 1)
    gas_flat = padded_gas.reshape(fields, (planes + 2) * cross_cells)
    ambient_layer_fields = jnp.take(gas_flat, fine_cell, axis=1)
    slot_in_block = jnp.arange(BLOCK, dtype=jnp.int32)
    alive_mask = (slot_in_block[None, :] < block_counts[:, None]).reshape(-1).astype(jnp.float32)
    source_terms, parcel_next, evaporated_weight = advance(
        ambient_layer_fields, parcel_record, condensed_shares, surface_steam_factor, alive_mask
    )
    extended = (
        jnp.zeros((fields, (planes + 2) * cross_cells), jnp.float32)
        .at[:, fine_cell]
        .add(source_terms)
    )
    extended = extended.reshape(fields, planes + 2, cross_cells)
    mass = 0.25 * extended[4:].sum(axis=0).reshape(planes + 2, ROWS, LANES, 2).sum(axis=3)
    even = lax.axis_index("slab") % 2 == 0
    own = mass[1 : planes + 1].sum(axis=0) + jnp.where(even, mass[planes + 1], mass[0])
    outer = jnp.where(even, mass[0], mass[planes + 1])
    edges = jnp.stack([extended[:, 0], extended[:, planes + 1]])
    halo, grid = spread(own, outer, edges)
    fine_source, correction = finish(extended[:, 1 : planes + 1], halo, grid)
    return (parcel_next, fine_source, correction)


def solution(mesh):
    in_specs = (
        P(None, "slab", "cross"),
        P(None, ("slab", "cross")),
        P(None, ("slab", "cross")),
        P(),
        P(("slab", "cross")),
        P(("slab", "cross")),
    )
    out_specs = (P(None, ("slab", "cross")), P(None, "slab", "cross"), P())
    return jax.shard_map(body, mesh=mesh, in_specs=in_specs, out_specs=out_specs, check_vma=False)
```

```python
import jax
import jax.numpy as jnp
from jax import lax
from jax.experimental import pallas as pl
from jax.experimental.pallas import tpu as pltpu
from jax.sharding import PartitionSpec as P

BLOCK = 128
COARSE = 64


drag_rate = 0.5
evap_rate = 0.08
warming_speed = 0.3
latent_boiling_energy = 0.5
vapour_heat = 1.5
volume_inverse = 4.0


LINE = 16
RING = 4
LANES = 128
ROWS = 8


def spread_kernel(
    own_ref, outer_ref, edge_ref, halo_ref, grid_ref, got,
    pair_send, pair_recv, edge_send, edge_recv, line_send, line_recv,
    minor_send, minor_recv, major_send, major_recv, core_send, core_recv,
):
    slabs = 2 * RING * LINE
    slab = lax.axis_index("slab")
    cross = lax.axis_index("cross")
    core = lax.rem(cross, 2)
    z = lax.rem(slab, LINE)
    x = lax.rem(lax.div(slab, LINE), RING)
    y = lax.div(cross, 2) * 2 + lax.div(slab, RING * LINE)
    odd = lax.rem(slab, 2)
    sign = 2 * odd - 1
    pair = lax.div(slab, 2)
    line_pair = lax.div(z, 2)
    major = core * x + (1 - core) * y
    minor = core * y + (1 - core) * x

    def near(by):
        return (lax.rem(slab + by + slabs, slabs), cross)

    def place(at_x, at_y, at_z):
        return (lax.rem(at_y, 2) * (RING * LINE) + at_x * LINE + at_z, lax.div(at_y, 2) * 2 + core)

    def in_line(by):
        return lax.rem(z + by + LINE, LINE)

    def minor_peer(other):
        return place(core * x + (1 - core) * other, core * other + (1 - core) * y, z)

    def major_peer(other):
        return place(core * other + (1 - core) * x, core * y + (1 - core) * other, z)

    def turn(own, by):
        return lax.rem(own + by, RING)

    def copy(src, dst, send, recv, device):
        return pltpu.make_async_remote_copy(
            src_ref=src, dst_ref=dst, send_sem=send, recv_sem=recv,
            device_id=device, device_id_type=pl.DeviceIdType.MESH,
        )

    other_core = (slab, cross + 1 - 2 * core)
    line_from = [sign * k for k in (1, 3, 5, 7)] + [-sign * k for k in (2, 4, 6)]
    low = lax.rem(2 * pair - 1 + slabs, slabs)
    high = lax.rem(2 * pair + 2, slabs)

    barrier = pltpu.get_barrier_semaphore()
    sources = [near(-sign), (low, cross), (high, cross), near(-1), near(1)]
    sources += [place(x, y, in_line(by)) for by in line_from]
    sources += [minor_peer(turn(minor, by)) for by in (1, 2, 3)]
    sources += [major_peer(turn(major, by)) for by in (1, 2, 3)]
    sources += [other_core]
    for device in sources:
        pl.semaphore_signal(barrier, inc=1, device_id=device, device_id_type=pl.DeviceIdType.MESH)
    pl.semaphore_wait(barrier, len(sources))

    copies = [
        copy(own_ref, got.at[0], pair_send.at[0], pair_recv.at[0], near(-sign)),
        copy(outer_ref, got.at[2 - odd], pair_send.at[1], pair_recv.at[2 - odd], near(sign)),
        copy(outer_ref, got.at[2 - odd], pair_send.at[2], pair_recv.at[2 - odd], near(2 * sign)),
    ]
    for each in copies:
        each.start()
    for slot in range(3):
        copy(own_ref, got.at[slot], pair_send.at[slot], pair_recv.at[slot], near(1)).wait_recv()
    grid_ref[core, major, minor, line_pair] = (own_ref[...] + got[0]) + (got[1] + got[2])
    edges = [
        copy(edge_ref.at[0], halo_ref.at[1], edge_send.at[0], edge_recv.at[1], near(-1)),
        copy(edge_ref.at[1], halo_ref.at[0], edge_send.at[1], edge_recv.at[0], near(1)),
    ]
    tile = grid_ref.at[core, major, minor, line_pair]
    line = [
        copy(tile, tile, line_send.at[k - 1], line_recv.at[line_pair], place(x, y, in_line(sign * k)))
        for k in range(1, 8)
    ]
    for each in line:
        each.start()
    for each in edges:
        each.start()
    for by in line_from:
        other = lax.div(in_line(by), 2)
        copy(
            tile, grid_ref.at[core, major, minor, other], line_send.at[0], line_recv.at[other], near(1)
        ).wait_recv()

    block = grid_ref.at[core, major, minor]
    minors = [
        copy(block, block, minor_send.at[by - 1], minor_recv.at[minor], minor_peer(turn(minor, by)))
        for by in (1, 2, 3)
    ]
    for each in minors:
        each.start()
    for by in (1, 2, 3):
        other = turn(minor, by)
        copy(
            block, grid_ref.at[core, major, other], minor_send.at[0], minor_recv.at[other], near(1)
        ).wait_recv()

    row = grid_ref.at[core, major]
    majors = [
        copy(row, row, major_send.at[by - 1], major_recv.at[major], major_peer(turn(major, by)))
        for by in (1, 2, 3)
    ]
    for each in majors:
        each.start()
    cores = []
    for by in range(RING):
        other = turn(major, by)
        arrived = grid_ref.at[core, other]
        if by:
            copy(row, arrived, major_send.at[0], major_recv.at[other], near(1)).wait_recv()
        each = copy(arrived, arrived, core_send.at[by], core_recv.at[other], other_core)
        each.start()
        cores.append(each)
    for by in range(RING):
        far = grid_ref.at[1 - core, by]
        copy(far, far, core_send.at[0], core_recv.at[by], other_core).wait_recv()
    for slot in range(2):
        copy(edge_ref.at[0], halo_ref.at[slot], edge_send.at[0], edge_recv.at[slot], near(1)).wait_recv()
    for each in copies + edges + line + minors + majors + cores:
        each.wait_send()


def spread(own, outer, edges):
    dma = pltpu.SemaphoreType.DMA
    vmem = pl.BlockSpec(memory_space=pltpu.VMEM)
    hbm = pl.BlockSpec(memory_space=pl.ANY)
    return pl.pallas_call(
        spread_kernel,
        out_shape=(
            jax.ShapeDtypeStruct(edges.shape, jnp.float32),
            jax.ShapeDtypeStruct((2, RING, RING, LINE // 2, ROWS, LANES), jnp.float32),
        ),
        in_specs=[vmem, vmem, hbm],
        out_specs=(hbm, vmem),
        scratch_shapes=[
            pltpu.VMEM((3, ROWS, LANES), jnp.float32),
            dma((3,)), dma((3,)), dma((2,)), dma((2,)), dma((7,)), dma((LINE // 2,)),
            dma((3,)), dma((RING,)), dma((3,)), dma((RING,)), dma((RING,)), dma((RING,)),
        ],
        compiler_params=pltpu.CompilerParams(
            collective_id=0, has_side_effects=True, vmem_limit_bytes=8 << 20
        ),
        name="spread",
    )(own, outer, edges)


def finish_kernel(base_ref, halo_ref, grid_ref, fine_ref, out_ref, source, even, uneven):
    fields, planes, cells = base_ref.shape
    row = lax.broadcasted_iota(jnp.int32, (planes, cells), 0)
    first = row == 0
    last = row == planes - 1
    for f in range(fields):
        low = jnp.broadcast_to(halo_ref[0, f : f + 1, :], (planes, cells))
        high = jnp.broadcast_to(halo_ref[1, f : f + 1, :], (planes, cells))
        fine_ref[f] = base_ref[f] + jnp.where(first, low, jnp.where(last, high, 0.0))

    half = RING * RING * (LINE // 2) * ROWS
    tiles = COARSE * COARSE // LANES
    blank = jnp.zeros((ROWS, tiles * LANES), jnp.float32)
    for held in (even, uneven):
        held[0:ROWS, :] = blank
        held[COARSE + ROWS : COARSE + 2 * ROWS, :] = blank
    for k in range(tiles):
        y_hi, core, i = k // 16, (k // 8) % 2, k % 8
        cols = slice(k * LANES, (k + 1) * LANES)
        for t in range(COARSE // ROWS):
            y_lo, x = t // RING, t % RING
            if core == 0:
                at = ((y_hi * 2 + y_lo) * RING + x) * (LINE // 2) * ROWS + i
            else:
                at = half + (x * RING + y_hi * 2 + y_lo) * (LINE // 2) * ROWS + i
            value = grid_ref[pl.ds(at, ROWS, stride=ROWS), :] * (1.0 / 6.0)
            source[t * ROWS : (t + 1) * ROWS, cols] = value
            even[(t + 1) * ROWS : (t + 2) * ROWS, cols] = value

    lane = lax.broadcasted_iota(jnp.int32, (ROWS, LANES), 1)
    edge = LANES // 2
    depth = lax.rem(lane, edge)
    upper = depth < edge - 1
    lower = depth > 0
    left = lane < edge

    def sweep(src, dst, top):
        def one(t, carry):
            at = pl.multiple_of(t * ROWS, ROWS)
            rolled = []
            mid = []
            for k in range(tiles):
                cols = slice(k * LANES, (k + 1) * LANES)
                value = src[pl.ds(at + ROWS, ROWS), cols]
                mid.append(value)
                rolled.append(pltpu.roll(value, edge, 1))
            none = jnp.zeros((ROWS, LANES), jnp.float32)
            for k in range(tiles):
                cols = slice(k * LANES, (k + 1) * LANES)
                before = rolled[k - 1] if k else none
                after = rolled[k + 1] if k + 1 < tiles else none
                total = rolled[k] + jnp.where(left, before, after)
                total += jnp.where(upper, pltpu.roll(mid[k], LANES - 1, 1), 0.0)
                total += jnp.where(lower, pltpu.roll(mid[k], 1, 1), 0.0)
                sub = lax.broadcasted_iota(jnp.int32, (ROWS, LANES), 0)
                up = src[pl.ds(at, ROWS), cols]
                down = src[pl.ds(at + 2 * ROWS, ROWS), cols]
                total += jnp.where(sub == 0, pltpu.roll(up, 1, 0), pltpu.roll(mid[k], 1, 0))
                total += jnp.where(
                    sub == ROWS - 1, pltpu.roll(down, ROWS - 1, 0), pltpu.roll(mid[k], ROWS - 1, 0)
                )
                dst[pl.ds(at + top, ROWS), cols] = total * (1.0 / 6.0) + source[pl.ds(at, ROWS), cols]
            return carry

        lax.fori_loop(0, COARSE // ROWS, one, 0)

    sweep(even, uneven, ROWS)
    sweep(uneven, even, ROWS)
    sweep(even, out_ref, 0)


def finish(base, halo, grid):
    side = (COARSE, COARSE * COARSE)
    padded = (COARSE + 2 * ROWS, COARSE * COARSE)
    vmem = pl.BlockSpec(memory_space=pltpu.VMEM)
    return pl.pallas_call(
        finish_kernel,
        out_shape=(
            jax.ShapeDtypeStruct(base.shape, jnp.float32),
            jax.ShapeDtypeStruct(side, jnp.float32),
        ),
        in_specs=[vmem, vmem, vmem],
        out_specs=(vmem, vmem),
        scratch_shapes=[
            pltpu.VMEM(side, jnp.float32),
            pltpu.VMEM(padded, jnp.float32),
            pltpu.VMEM(padded, jnp.float32),
        ],
        compiler_params=pltpu.CompilerParams(vmem_limit_bytes=32 << 20),
        name="finish",
    )(base, halo, grid.reshape(-1, LANES))


CHUNK = 512
PER_PLANE = 4
UNROLL = 4


def parts_of(value):
    high = value.astype(jnp.bfloat16)
    rest = value - high.astype(jnp.float32)
    middle = rest.astype(jnp.bfloat16)
    low = (rest - middle.astype(jnp.float32)).astype(jnp.bfloat16)
    return jnp.concatenate([high, middle, low], axis=0)


def joined(value):
    third = value.shape[0] // 3
    return value[:third] + (value[third : 2 * third] + value[2 * third :])


def spray_kernel(
    cell_at, count_at, gas_ref, low_ref, high_ref, record_ref, shares_ref, steam_ref, cell_ref,
    next_ref, base_ref, edge_ref, own_ref, outer_ref,
    gas_parts, gathered, terms, total, block_of, chunk_of, base_of,
):
    fields, planes, cells = gas_ref.shape
    blocks = cell_ref.shape[0]
    chunks = (planes + 2) * PER_PLANE

    def listed(b, i):
        first = lax.shift_right_logical(cell_at[b * BLOCK], 9)
        last = lax.shift_right_logical(cell_at[b * BLOCK + BLOCK - 1], 9)

        def one(j, i):
            block_of[i] = b
            chunk_of[i] = j
            base_of[i] = j * CHUNK
            return i + 1

        return lax.fori_loop(first, last + 1, one, i)

    pairs = lax.fori_loop(0, blocks, listed, 0)
    for k in range(UNROLL):
        block_of[pairs + k] = 0
        chunk_of[pairs + k] = 0
        base_of[pairs + k] = chunks * CHUNK
    rounds = lax.div(pairs + UNROLL - 1, UNROLL)

    for p in range(planes + 2):
        for q in range(PER_PLANE):
            cols = slice(q * CHUNK, (q + 1) * CHUNK)
            if p == 0:
                value = low_ref[:, cols]
            elif p == planes + 1:
                value = high_ref[:, cols]
            else:
                value = gas_ref[:, p - 1, cols]
            gas_parts[p * PER_PLANE + q] = parts_of(value)
    gathered[...] = jnp.zeros(gathered.shape, jnp.float32)
    total[...] = jnp.zeros(total.shape, jnp.float32)
    row = lax.broadcasted_iota(jnp.int32, (CHUNK, BLOCK), 0)

    def picked(i):
        place = cell_ref[pl.ds(block_of[i], 1), :] - base_of[i]
        return jnp.where(row == place, 1.0, 0.0).astype(jnp.bfloat16)

    def gather(n, carry):
        for k in range(UNROLL):
            i = n * UNROLL + k
            part = jnp.dot(gas_parts[chunk_of[i]], picked(i), preferred_element_type=jnp.float32)
            gathered[block_of[i]] += joined(part)
        return carry

    lax.fori_loop(0, rounds, gather, 0)

    lane = lax.broadcasted_iota(jnp.int32, (1, BLOCK), 1)
    steam = steam_ref[...]

    def step(n, carry):
        for k in range(UNROLL):
            b = n * UNROLL + k
            cols = pl.ds(pl.multiple_of(b * BLOCK, BLOCK), BLOCK)
            gas = gathered[b]
            record = record_ref[:, cols]
            alive = lane < count_at[b]
            gas_velocity, gas_heat, vapour = gas[0:3], gas[3:4], gas[4:]
            velocity, heat, weight = record[0:3], record[3:4], record[4:5]
            slip = gas_velocity - velocity
            slip = slip * slip
            slip = slip[0:1] + slip[1:2] + slip[2:3]
            log_weight = jnp.log(weight)
            factor = drag_rate * jnp.exp(log_weight * (-2.0 / 3.0))
            factor = factor * (1.0 + 0.15 * jnp.exp(0.3435 * jnp.log(slip + 1.0)))
            moved = (velocity + factor * gas_velocity) / (1.0 + factor)
            surface = shares_ref[:, cols] * steam * jnp.exp(2.0 * (heat - 0.75))
            rates = evap_rate * weight * (surface - vapour)
            lost = jnp.sum(rates, axis=0, keepdims=True)
            exchange = warming_speed * (gas_heat - heat) * jnp.exp(log_weight * (1.0 / 3.0))
            warmed = heat + (exchange - latent_boiling_energy * lost) / weight
            scale = jnp.where(alive, volume_inverse, 0.0)
            terms[b, 0:3] = (weight * (velocity - moved) + lost * moved) * scale
            terms[b, 3:4] = (vapour_heat * lost - exchange) * scale
            terms[b, 4:16] = rates * scale
            next_ref[0:3, cols] = jnp.where(alive, moved, velocity)
            next_ref[3:4, cols] = jnp.where(alive, warmed, heat)
            next_ref[4:5, cols] = jnp.where(alive, weight - lost, weight)
        return carry

    lax.fori_loop(0, blocks // UNROLL, step, 0)

    def scatter(n, carry):
        for k in range(UNROLL):
            i = n * UNROLL + k
            part = lax.dot_general(
                parts_of(terms[block_of[i]]), picked(i), (((1,), (1,)), ((), ())),
                preferred_element_type=jnp.float32,
            )
            total[chunk_of[i]] += joined(part)
        return carry

    lax.fori_loop(0, rounds, scatter, 0)

    half = CHUNK // 2
    fold_row = lax.broadcasted_iota(jnp.int32, (half, LANES), 0)
    fold_lane = lax.broadcasted_iota(jnp.int32, (half, LANES), 1)
    fold = jnp.where(lax.shift_right_logical(fold_row, 1) == fold_lane, 1.0, 0.0).astype(jnp.bfloat16)

    def mass(value):
        kept = jnp.sum(value[4:], axis=0, keepdims=True)
        rows = [
            joined(jnp.dot(parts_of(kept[:, h * half : (h + 1) * half]), fold, preferred_element_type=jnp.float32))
            for h in range(2)
        ]
        return rows

    own, low, high = [], [], []
    for q in range(PER_PLANE):
        cols = slice(q * CHUNK, (q + 1) * CHUNK)
        below = total[q]
        above = total[(planes + 1) * PER_PLANE + q]
        edge_ref[0, :, cols] = below
        edge_ref[1, :, cols] = above
        inside = None
        for p in range(planes):
            value = total[(p + 1) * PER_PLANE + q]
            base_ref[:, p, cols] = value
            inside = value if inside is None else inside + value
        own += mass(inside)
        low += mass(below)
        high += mass(above)
    own, low, high = (0.25 * jnp.concatenate(rows, axis=0) for rows in (own, low, high))
    odd = lax.rem(lax.axis_index("slab"), 2) == 1
    own_ref[...] = own + jnp.where(odd, low, high)
    outer_ref[...] = jnp.where(odd, high, low)


def spray(gas_state, low, high, parcel_record, condensed_shares, surface_steam_factor, fine_cell, block_counts):
    fields, planes, cells = gas_state.shape
    blocks = block_counts.shape[0]
    chunks = (planes + 2) * PER_PLANE
    room = chunks + blocks + UNROLL
    vmem = pl.BlockSpec(memory_space=pltpu.VMEM)
    smem = pl.BlockSpec(memory_space=pltpu.SMEM)
    array = lambda *shape: jax.ShapeDtypeStruct(shape, jnp.float32)
    return pl.pallas_call(
        spray_kernel,
        out_shape=(
            array(*parcel_record.shape), array(*gas_state.shape), array(2, fields, cells),
            array(ROWS, LANES), array(ROWS, LANES),
        ),
        in_specs=[smem, smem] + [vmem] * 7,
        out_specs=(vmem,) * 5,
        scratch_shapes=[
            pltpu.VMEM((chunks, 3 * fields, CHUNK), jnp.bfloat16),
            pltpu.VMEM((blocks, fields, BLOCK), jnp.float32),
            pltpu.VMEM((blocks, fields, BLOCK), jnp.float32),
            pltpu.VMEM((chunks, fields, CHUNK), jnp.float32),
            pltpu.SMEM((room,), jnp.int32),
            pltpu.SMEM((room,), jnp.int32),
            pltpu.SMEM((room,), jnp.int32),
        ],
        compiler_params=pltpu.CompilerParams(vmem_limit_bytes=32 << 20),
        name="spray",
    )(
        fine_cell, block_counts, gas_state, low, high, parcel_record, condensed_shares,
        surface_steam_factor.reshape(-1, 1), fine_cell.reshape(blocks, BLOCK),
    )


def exchanged(shard):
    devices = lax.axis_size("slab")
    up = [(i, (i + 1) % devices) for i in range(devices)]
    down = [(j, i) for i, j in up]
    before = lax.ppermute(shard[:, -1], "slab", up)
    after = lax.ppermute(shard[:, 0], "slab", down)
    return before, after


def body(gas_state, parcel_record, condensed_shares, surface_steam_factor, fine_cell, block_counts):
    low, high = exchanged(gas_state)
    parcel_next, base, edges, own, outer = spray(
        gas_state, low, high, parcel_record, condensed_shares, surface_steam_factor, fine_cell, block_counts
    )
    halo, grid = spread(own, outer, edges)
    fine_source, correction = finish(base, halo, grid)
    return (parcel_next, fine_source, correction)


def solution(mesh):
    in_specs = (
        P(None, "slab", "cross"),
        P(None, ("slab", "cross")),
        P(None, ("slab", "cross")),
        P(),
        P(("slab", "cross")),
        P(("slab", "cross")),
    )
    out_specs = (P(None, ("slab", "cross")), P(None, "slab", "cross"), P())
    return jax.shard_map(body, mesh=mesh, in_specs=in_specs, out_specs=out_specs, check_vma=False)
```

```python
import jax
import jax.numpy as jnp
from jax import lax
from jax.experimental import pallas as pl
from jax.experimental.pallas import tpu as pltpu
from jax.sharding import PartitionSpec as P

BLOCK = 128
COARSE = 64


drag_rate = 0.5
evap_rate = 0.08
warming_speed = 0.3
latent_boiling_energy = 0.5
vapour_heat = 1.5
volume_inverse = 4.0


LINE = 16
RING = 4
LANES = 128
ROWS = 8
FIELDS = 16
PLANES = 8
TILES = 16
CHUNK = 512
PER_PLANE = 4
SHIFT = 9
UNROLL = 4
PAIRS = 72
ROOM = 80


def parts_of(value):
    high = value.astype(jnp.bfloat16)
    rest = value - high.astype(jnp.float32)
    middle = rest.astype(jnp.bfloat16)
    low = (rest - middle.astype(jnp.float32)).astype(jnp.bfloat16)
    return jnp.concatenate([high, middle, low], axis=0)


def joined(value):
    third = value.shape[0] // 3
    return value[:third] + (value[third : 2 * third] + value[2 * third :])


def plane_rows(tile, plane):
    return pl.ds(tile * PLANES + plane, FIELDS, stride=TILES * PLANES)


def send(src, dst, send_sem, recv_sem, device):
    return pltpu.make_async_remote_copy(
        src_ref=src, dst_ref=dst, send_sem=send_sem, recv_sem=recv_sem,
        device_id=device, device_id_type=pl.DeviceIdType.MESH,
    )


def halo_kernel(gas_ref, parts_ref, sent, got, send_sem, recv_sem):
    slabs = 2 * RING * LINE
    slab = lax.axis_index("slab")
    cross = lax.axis_index("cross")
    below = (lax.rem(slab - 1 + slabs, slabs), cross)
    above = (lax.rem(slab + 1, slabs), cross)
    barrier = pltpu.get_barrier_semaphore()
    for device in (below, above):
        pl.semaphore_signal(barrier, inc=1, device_id=device, device_id_type=pl.DeviceIdType.MESH)
    for side, plane in ((0, 0), (1, PLANES - 1)):
        for t in range(TILES):
            sent[side, :, t * LANES : (t + 1) * LANES] = gas_ref[plane_rows(t, plane), :]
    pl.semaphore_wait(barrier, 2)
    copies = [
        send(sent.at[0], got.at[1], send_sem.at[0], recv_sem.at[1], below),
        send(sent.at[1], got.at[0], send_sem.at[1], recv_sem.at[0], above),
    ]
    for each in copies:
        each.start()
    group = CHUNK // LANES
    for p in range(PLANES):
        for q in range(PER_PLANE):
            value = [gas_ref[plane_rows(q * group + t, p), :] for t in range(group)]
            parts_ref[(p + 1) * PER_PLANE + q] = parts_of(jnp.concatenate(value, axis=1))
    for side, plane in ((0, 0), (1, PLANES + 1)):
        send(sent.at[0], got.at[side], send_sem.at[0], recv_sem.at[side], above).wait_recv()
        for q in range(PER_PLANE):
            parts_ref[plane * PER_PLANE + q] = parts_of(got[side, :, q * CHUNK : (q + 1) * CHUNK])
    for each in copies:
        each.wait_send()


def halo(gas_rows):
    vmem = pl.BlockSpec(memory_space=pltpu.VMEM)
    dma = pltpu.SemaphoreType.DMA
    chunks = (PLANES + 2) * PER_PLANE
    return pl.pallas_call(
        halo_kernel,
        out_shape=jax.ShapeDtypeStruct((chunks, 3 * FIELDS, CHUNK), jnp.bfloat16),
        in_specs=[vmem],
        out_specs=vmem,
        scratch_shapes=[
            pltpu.VMEM((2, FIELDS, TILES * LANES), jnp.float32),
            pltpu.VMEM((2, FIELDS, TILES * LANES), jnp.float32),
            dma((2,)), dma((2,)),
        ],
        compiler_params=pltpu.CompilerParams(
            collective_id=1, has_side_effects=True, vmem_limit_bytes=16 << 20
        ),
        name="halo",
    )(gas_rows)


def spray_kernel(
    cell_at, count_at, gas_parts, record_ref, shares_ref, steam_ref, cell_ref, next_ref, terms,
    table, gathered,
):
    blocks = cell_ref.shape[0]
    chunks = (PLANES + 2) * PER_PLANE

    def listed(b, i):
        first = lax.shift_right_logical(cell_at[b * BLOCK], SHIFT)
        last = lax.shift_right_logical(cell_at[b * BLOCK + BLOCK - 1], SHIFT)

        def one(j, i):
            table[i] = b
            table[ROOM + i] = j
            table[2 * ROOM + j] = i
            return i + 1

        return lax.fori_loop(first, last + 1, one, i)

    for c in range(chunks):
        table[2 * ROOM + c] = PAIRS
    pairs = lax.fori_loop(0, blocks, listed, 0)

    def blank(i, carry):
        table[i] = 0
        table[ROOM + i] = -1
        return carry

    lax.fori_loop(pairs, PAIRS, blank, 0)
    rounds = lax.div(pairs + UNROLL - 1, UNROLL)

    gathered[...] = jnp.zeros(gathered.shape, jnp.float32)
    row = lax.broadcasted_iota(jnp.int32, (CHUNK, BLOCK), 0)

    def picked(i):
        c = table[ROOM + i]
        place = cell_ref[pl.ds(table[i], 1), :] - jnp.where(c < 0, chunks, c) * CHUNK
        return jnp.where(row == place, 1.0, 0.0).astype(jnp.bfloat16)

    def gather(n, carry):
        for k in range(UNROLL):
            i = n * UNROLL + k
            held = gas_parts[jnp.maximum(table[ROOM + i], 0)]
            part = jnp.dot(held, picked(i), preferred_element_type=jnp.float32)
            gathered[table[i]] += joined(part)
        return carry

    lax.fori_loop(0, rounds, gather, 0)

    lane = lax.broadcasted_iota(jnp.int32, (1, BLOCK), 1)
    steam = steam_ref[...]

    def step(n, carry):
        for k in range(UNROLL):
            b = n * UNROLL + k
            cols = pl.ds(pl.multiple_of(b * BLOCK, BLOCK), BLOCK)
            gas = gathered[b]
            record = record_ref[:, cols]
            alive = lane < count_at[b]
            gas_velocity, gas_heat, vapour = gas[0:3], gas[3:4], gas[4:]
            velocity, heat, weight = record[0:3], record[3:4], record[4:5]
            slip = gas_velocity - velocity
            slip = slip * slip
            slip = slip[0:1] + slip[1:2] + slip[2:3]
            log_weight = jnp.log(weight)
            factor = drag_rate * jnp.exp(log_weight * (-2.0 / 3.0))
            factor = factor * (1.0 + 0.15 * jnp.exp(0.3435 * jnp.log(slip + 1.0)))
            moved = (velocity + factor * gas_velocity) / (1.0 + factor)
            surface = shares_ref[:, cols] * steam * jnp.exp(2.0 * (heat - 0.75))
            rates = evap_rate * weight * (surface - vapour)
            lost = jnp.sum(rates, axis=0, keepdims=True)
            exchange = warming_speed * (gas_heat - heat) * jnp.exp(log_weight * (1.0 / 3.0))
            warmed = heat + (exchange - latent_boiling_energy * lost) / weight
            scale = jnp.where(alive, volume_inverse, 0.0)
            terms[b, 0:3] = (weight * (velocity - moved) + lost * moved) * scale
            terms[b, 3:4] = (vapour_heat * lost - exchange) * scale
            terms[b, 4:16] = rates * scale
            next_ref[0:3, cols] = jnp.where(alive, moved, velocity)
            next_ref[3:4, cols] = jnp.where(alive, warmed, heat)
            next_ref[4:5, cols] = jnp.where(alive, weight - lost, weight)
        return carry

    lax.fori_loop(0, blocks // UNROLL, step, 0)


def spray(gas_parts, parcel_record, condensed_shares, surface_steam_factor, fine_cell, block_counts):
    blocks = block_counts.shape[0]
    vmem = pl.BlockSpec(memory_space=pltpu.VMEM)
    smem = pl.BlockSpec(memory_space=pltpu.SMEM)
    return pl.pallas_call(
        spray_kernel,
        out_shape=(
            jax.ShapeDtypeStruct(parcel_record.shape, jnp.float32),
            jax.ShapeDtypeStruct((blocks, FIELDS, BLOCK), jnp.float32),
            jax.ShapeDtypeStruct((3 * ROOM,), jnp.int32),
        ),
        in_specs=[smem, smem] + [vmem] * 5,
        out_specs=(vmem, vmem, smem),
        scratch_shapes=[
            pltpu.VMEM((blocks, FIELDS, BLOCK), jnp.float32),
        ],
        compiler_params=pltpu.CompilerParams(vmem_limit_bytes=16 << 20),
        name="spray",
    )(
        fine_cell, block_counts, gas_parts, parcel_record, condensed_shares,
        surface_steam_factor.reshape(-1, 1), fine_cell.reshape(blocks, BLOCK),
    )


def scatter(table, cell_ref, terms_ref, base_ref, edge, slots):
    chunks = (PLANES + 2) * PER_PLANE
    row = lax.broadcasted_iota(jnp.int32, (CHUNK, BLOCK), 0)

    def step(n, carry):
        total, before = carry
        for k in range(UNROLL):
            i = n * UNROLL + k
            b = table[i]
            c = table[ROOM + i]
            place = cell_ref[pl.ds(b, 1), :] - jnp.where(c < 0, chunks, c) * CHUNK
            picked = jnp.where(row == place, 1.0, 0.0).astype(jnp.bfloat16)
            part = lax.dot_general(
                parts_of(terms_ref[b]), picked, (((1,), (1,)), ((), ())),
                preferred_element_type=jnp.float32,
            )
            total = joined(part) + total * jnp.where(c == before, 1.0, 0.0)
            slots[i] = total
            before = c
        return total, before

    none = jnp.zeros((FIELDS, CHUNK), jnp.float32)
    lax.fori_loop(0, PAIRS // UNROLL, step, (none, -2))
    slots[PAIRS] = none

    half = CHUNK // 2
    fold_row = lax.broadcasted_iota(jnp.int32, (half, LANES), 0)
    fold_lane = lax.broadcasted_iota(jnp.int32, (half, LANES), 1)
    fold = jnp.where(lax.shift_right_logical(fold_row, 1) == fold_lane, 1.0, 0.0).astype(jnp.bfloat16)

    def mass(value):
        kept = jnp.sum(value[4:], axis=0, keepdims=True)
        return [
            joined(jnp.dot(parts_of(kept[:, h * half : (h + 1) * half]), fold, preferred_element_type=jnp.float32))
            for h in range(2)
        ]

    own, low, high = [], [], []
    group = CHUNK // LANES
    for q in range(PER_PLANE):
        cols = slice(q * CHUNK, (q + 1) * CHUNK)
        below = slots[table[2 * ROOM + q]]
        above = slots[table[2 * ROOM + (PLANES + 1) * PER_PLANE + q]]
        edge[0, :, cols] = below
        edge[1, :, cols] = above
        inside = None
        for p in range(PLANES):
            value = slots[table[2 * ROOM + (p + 1) * PER_PLANE + q]]
            for t in range(group):
                base_ref[plane_rows(q * group + t, p), :] = value[:, t * LANES : (t + 1) * LANES]
            inside = value if inside is None else inside + value
        own += mass(inside)
        low += mass(below)
        high += mass(above)
    return tuple(0.25 * jnp.concatenate(rows, axis=0) for rows in (own, low, high))


def spread_kernel(
    table, cell_ref, terms_ref, base_ref, halo_ref, grid_ref, own_ref, outer_ref, edge_ref, slots, got,
    pair_send, pair_recv, edge_send, edge_recv, line_send, line_recv,
    minor_send, minor_recv, major_send, major_recv, core_send, core_recv,
):
    slabs = 2 * RING * LINE
    slab = lax.axis_index("slab")
    cross = lax.axis_index("cross")
    core = lax.rem(cross, 2)
    z = lax.rem(slab, LINE)
    x = lax.rem(lax.div(slab, LINE), RING)
    y = lax.div(cross, 2) * 2 + lax.div(slab, RING * LINE)
    odd = lax.rem(slab, 2)
    sign = 2 * odd - 1
    pair = lax.div(slab, 2)
    line_pair = lax.div(z, 2)
    major = core * x + (1 - core) * y
    minor = core * y + (1 - core) * x

    def near(by):
        return (lax.rem(slab + by + slabs, slabs), cross)

    def place(at_x, at_y, at_z):
        return (lax.rem(at_y, 2) * (RING * LINE) + at_x * LINE + at_z, lax.div(at_y, 2) * 2 + core)

    def in_line(by):
        return lax.rem(z + by + LINE, LINE)

    def minor_peer(other):
        return place(core * x + (1 - core) * other, core * other + (1 - core) * y, z)

    def major_peer(other):
        return place(core * other + (1 - core) * x, core * y + (1 - core) * other, z)

    def turn(own, by):
        return lax.rem(own + by, RING)

    copy = send

    other_core = (slab, cross + 1 - 2 * core)
    line_from = [sign * k for k in (1, 3, 5, 7)] + [-sign * k for k in (2, 4, 6)]
    low = lax.rem(2 * pair - 1 + slabs, slabs)
    high = lax.rem(2 * pair + 2, slabs)

    barrier = pltpu.get_barrier_semaphore()
    sources = [near(-sign), (low, cross), (high, cross), near(-1), near(1)]
    sources += [place(x, y, in_line(by)) for by in line_from]
    sources += [minor_peer(turn(minor, by)) for by in (1, 2, 3)]
    sources += [major_peer(turn(major, by)) for by in (1, 2, 3)]
    sources += [other_core]
    for device in sources:
        pl.semaphore_signal(barrier, inc=1, device_id=device, device_id_type=pl.DeviceIdType.MESH)
    own, low_tile, high_tile = scatter(table, cell_ref, terms_ref, base_ref, edge_ref, slots)
    own_ref[...] = own + jnp.where(odd == 1, low_tile, high_tile)
    outer_ref[...] = jnp.where(odd == 1, high_tile, low_tile)
    pl.semaphore_wait(barrier, len(sources))

    copies = [
        copy(own_ref, got.at[0], pair_send.at[0], pair_recv.at[0], near(-sign)),
        copy(outer_ref, got.at[2 - odd], pair_send.at[1], pair_recv.at[2 - odd], near(sign)),
        copy(outer_ref, got.at[2 - odd], pair_send.at[2], pair_recv.at[2 - odd], near(2 * sign)),
    ]
    for each in copies:
        each.start()
    for slot in range(3):
        copy(own_ref, got.at[slot], pair_send.at[slot], pair_recv.at[slot], near(1)).wait_recv()
    grid_ref[core, major, minor, line_pair] = (own_ref[...] + got[0]) + (got[1] + got[2])
    edges = [
        copy(edge_ref.at[0], halo_ref.at[1], edge_send.at[0], edge_recv.at[1], near(-1)),
        copy(edge_ref.at[1], halo_ref.at[0], edge_send.at[1], edge_recv.at[0], near(1)),
    ]
    tile = grid_ref.at[core, major, minor, line_pair]
    line = [
        copy(tile, tile, line_send.at[k - 1], line_recv.at[line_pair], place(x, y, in_line(sign * k)))
        for k in range(1, 8)
    ]
    for each in line:
        each.start()
    for each in edges:
        each.start()
    for by in line_from:
        other = lax.div(in_line(by), 2)
        copy(
            tile, grid_ref.at[core, major, minor, other], line_send.at[0], line_recv.at[other], near(1)
        ).wait_recv()

    block = grid_ref.at[core, major, minor]
    minors = [
        copy(block, block, minor_send.at[by - 1], minor_recv.at[minor], minor_peer(turn(minor, by)))
        for by in (1, 2, 3)
    ]
    for each in minors:
        each.start()
    for by in (1, 2, 3):
        other = turn(minor, by)
        copy(
            block, grid_ref.at[core, major, other], minor_send.at[0], minor_recv.at[other], near(1)
        ).wait_recv()

    row = grid_ref.at[core, major]
    majors = [
        copy(row, row, major_send.at[by - 1], major_recv.at[major], major_peer(turn(major, by)))
        for by in (1, 2, 3)
    ]
    for each in majors:
        each.start()
    cores = []
    for by in range(RING):
        other = turn(major, by)
        arrived = grid_ref.at[core, other]
        if by:
            copy(row, arrived, major_send.at[0], major_recv.at[other], near(1)).wait_recv()
        each = copy(arrived, arrived, core_send.at[by], core_recv.at[other], other_core)
        each.start()
        cores.append(each)
    for by in range(RING):
        far = grid_ref.at[1 - core, by]
        copy(far, far, core_send.at[0], core_recv.at[by], other_core).wait_recv()
    for slot in range(2):
        copy(edge_ref.at[0], halo_ref.at[slot], edge_send.at[0], edge_recv.at[slot], near(1)).wait_recv()
    for each in copies + edges + line + minors + majors + cores:
        each.wait_send()


def spread(table, cells, terms):
    dma = pltpu.SemaphoreType.DMA
    vmem = pl.BlockSpec(memory_space=pltpu.VMEM)
    smem = pl.BlockSpec(memory_space=pltpu.SMEM)
    side = (2, FIELDS, TILES * LANES)
    return pl.pallas_call(
        spread_kernel,
        out_shape=(
            jax.ShapeDtypeStruct((FIELDS * TILES * PLANES, LANES), jnp.float32),
            jax.ShapeDtypeStruct(side, jnp.float32),
            jax.ShapeDtypeStruct((2, RING, RING, LINE // 2, ROWS, LANES), jnp.float32),
        ),
        in_specs=[smem, vmem, vmem],
        out_specs=(vmem, vmem, vmem),
        scratch_shapes=[
            pltpu.VMEM((ROWS, LANES), jnp.float32),
            pltpu.VMEM((ROWS, LANES), jnp.float32),
            pltpu.VMEM(side, jnp.float32),
            pltpu.VMEM((PAIRS + 1, FIELDS, CHUNK), jnp.float32),
            pltpu.VMEM((3, ROWS, LANES), jnp.float32),
            dma((3,)), dma((3,)), dma((2,)), dma((2,)), dma((7,)), dma((LINE // 2,)),
            dma((3,)), dma((RING,)), dma((3,)), dma((RING,)), dma((RING,)), dma((RING,)),
        ],
        compiler_params=pltpu.CompilerParams(
            collective_id=0, has_side_effects=True, vmem_limit_bytes=16 << 20
        ),
        name="spread",
    )(table, cells, terms)


def finish_kernel(base_ref, halo_ref, grid_ref, fine_ref, out_ref, fine, source, even, uneven, flat, result, fine_sem, out_sem):
    sub = lax.broadcasted_iota(jnp.int32, (ROWS, LANES), 0)
    lane = lax.broadcasted_iota(jnp.int32, (ROWS, LANES), 1)
    first = sub == 0
    last = sub == ROWS - 1
    for f in range(FIELDS):
        for t in range(TILES):
            cols = slice(t * LANES, (t + 1) * LANES)
            rows = slice((f * TILES + t) * PLANES, (f * TILES + t + 1) * PLANES)
            low = jnp.broadcast_to(halo_ref[0, f : f + 1, cols], (PLANES, LANES))
            high = jnp.broadcast_to(halo_ref[1, f : f + 1, cols], (PLANES, LANES))
            fine[rows, :] = base_ref[rows, :] + jnp.where(first, low, jnp.where(last, high, 0.0))
    fine_copy = pltpu.make_async_copy(fine, fine_ref, fine_sem)
    fine_copy.start()

    wide = COARSE // 2
    none = jnp.zeros((wide, LANES), jnp.float32)
    for held in (even, uneven):
        held[0] = none
        held[COARSE + 1] = none
    for plane in range(COARSE):
        y_lo, x, j = plane // 32, (plane // 8) % RING, plane % 8
        for c in range(RING):
            y = (c // 2) * 2 + y_lo
            at = grid_ref[0, y, x, j] if c % 2 == 0 else grid_ref[1, x, y, j]
            value = at * (1.0 / 6.0)
            source[plane, c * ROWS : (c + 1) * ROWS, :] = value
            even[plane + 1, c * ROWS : (c + 1) * ROWS, :] = value

    half = LANES // 2
    depth = lax.rem(lane, half)
    upper = jnp.where(depth < half - 1, 1.0, 0.0)
    lower = jnp.where(depth > 0, 1.0, 0.0)
    left = lane < half
    blank = jnp.zeros((ROWS, LANES), jnp.float32)

    def relaxed(src, plane):
        mid = [src[plane + 1, c * ROWS : (c + 1) * ROWS, :] for c in range(RING)]
        turned = [pltpu.roll(value, half, 1) for value in mid]
        down = [blank] + [pltpu.roll(value, 1, 0) for value in turned]
        up = [pltpu.roll(value, ROWS - 1, 0) for value in turned] + [blank]
        for c in range(RING):
            tile = slice(c * ROWS, (c + 1) * ROWS)
            before = jnp.where(first, down[c], down[c + 1])
            after = jnp.where(last, up[c + 1], up[c])
            total = turned[c] + jnp.where(left, before, after)
            total += pltpu.roll(mid[c], LANES - 1, 1) * upper
            total += pltpu.roll(mid[c], 1, 1) * lower
            total += src[plane, tile, :] + src[plane + 2, tile, :]
            yield tile, total * (1.0 / 6.0) + source[plane, tile, :]

    def sweep(src, dst):
        def some(n, carry):
            for k in range(UNROLL):
                plane = n * UNROLL + k
                for tile, value in relaxed(src, plane):
                    dst[plane + 1, tile, :] = value
            return carry

        lax.fori_loop(0, COARSE // UNROLL, some, 0)

    sweep(even, uneven)
    sweep(uneven, even)
    copies = []
    for group in range(COARSE // ROWS):
        for k in range(ROWS):
            plane = group * ROWS + k
            for tile, value in relaxed(even, plane):
                flat[plane * wide + tile.start : plane * wide + tile.stop, :] = value
        rows = slice(group * ROWS, (group + 1) * ROWS)
        for r in range(wide):
            value = flat[pl.ds(group * ROWS * wide + r, ROWS, stride=wide), :]
            result[rows, r * LANES : (r + 1) * LANES] = value
        each = pltpu.make_async_copy(result.at[rows], out_ref.at[rows], out_sem.at[group])
        each.start()
        copies.append(each)
    for each in copies:
        each.wait()
    fine_copy.wait()


def finish(base, halo_sum, grid):
    wide = COARSE // 2
    vmem = pl.BlockSpec(memory_space=pltpu.VMEM)
    hbm = pl.BlockSpec(memory_space=pl.ANY)
    dma = pltpu.SemaphoreType.DMA
    return pl.pallas_call(
        finish_kernel,
        out_shape=(
            jax.ShapeDtypeStruct(base.shape, jnp.float32),
            jax.ShapeDtypeStruct((COARSE, COARSE * COARSE), jnp.float32),
        ),
        in_specs=[vmem, vmem, vmem],
        out_specs=(hbm, hbm),
        scratch_shapes=[
            pltpu.VMEM(base.shape, jnp.float32),
            pltpu.VMEM((COARSE, wide, LANES), jnp.float32),
            pltpu.VMEM((COARSE + 2, wide, LANES), jnp.float32),
            pltpu.VMEM((COARSE + 2, wide, LANES), jnp.float32),
            pltpu.VMEM((COARSE * wide, LANES), jnp.float32),
            pltpu.VMEM((COARSE, COARSE * COARSE), jnp.float32),
            dma, dma((COARSE // ROWS,)),
        ],
        compiler_params=pltpu.CompilerParams(vmem_limit_bytes=16 << 20),
        name="finish",
    )(base, halo_sum, grid)


def body(gas_state, parcel_record, condensed_shares, surface_steam_factor, fine_cell, block_counts):
    rows = gas_state.reshape(FIELDS, PLANES, TILES, LANES).transpose(0, 2, 1, 3).reshape(-1, LANES)
    parts = halo(rows)
    parcel_next, terms, table = spray(
        parts, parcel_record, condensed_shares, surface_steam_factor, fine_cell, block_counts
    )
    base, halo_sum, grid = spread(table, fine_cell.reshape(-1, BLOCK), terms)
    fine_rows, correction = finish(base, halo_sum, grid)
    fine_source = fine_rows.reshape(FIELDS, TILES, PLANES, LANES).transpose(0, 2, 1, 3).reshape(gas_state.shape)
    return (parcel_next, fine_source, correction)


def solution(mesh):
    in_specs = (
        P(None, "slab", "cross"),
        P(None, ("slab", "cross")),
        P(None, ("slab", "cross")),
        P(),
        P(("slab", "cross")),
        P(("slab", "cross")),
    )
    out_specs = (P(None, ("slab", "cross")), P(None, "slab", "cross"), P())
    return jax.shard_map(body, mesh=mesh, in_specs=in_specs, out_specs=out_specs, check_vma=False)
```

```python
import jax
import jax.numpy as jnp
from jax import lax
from jax.experimental import pallas as pl
from jax.experimental.pallas import tpu as pltpu
from jax.sharding import PartitionSpec as P

BLOCK = 128
COARSE = 64


drag_rate = 0.5
evap_rate = 0.08
warming_speed = 0.3
latent_boiling_energy = 0.5
vapour_heat = 1.5
volume_inverse = 4.0


LINE = 16
RING = 4
LANES = 128
ROWS = 8
FIELDS = 16
PLANES = 8
TILES = 16
CHUNK = 512
PER_PLANE = 4
SHIFT = 9
UNROLL = 4
PAIRS = 72
ROOM = 80
LAG_MINOR = 5
LAG_MAJOR = 5
STRIDE = 40


def parts_of(value):
    high = value.astype(jnp.bfloat16)
    rest = value - high.astype(jnp.float32)
    middle = rest.astype(jnp.bfloat16)
    low = (rest - middle.astype(jnp.float32)).astype(jnp.bfloat16)
    return jnp.concatenate([high, middle, low], axis=0)


def joined(value):
    third = value.shape[0] // 3
    return value[:third] + (value[third : 2 * third] + value[2 * third :])


def plane_rows(tile, plane):
    return pl.ds(tile * PLANES + plane, FIELDS, stride=TILES * PLANES)


def send(src, dst, send_sem, recv_sem, device):
    return pltpu.make_async_remote_copy(
        src_ref=src, dst_ref=dst, send_sem=send_sem, recv_sem=recv_sem,
        device_id=device, device_id_type=pl.DeviceIdType.MESH,
    )


def halo_kernel(gas_ref, parts_ref, sent, got, send_sem, recv_sem):
    slabs = 2 * RING * LINE
    slab = lax.axis_index("slab")
    cross = lax.axis_index("cross")
    below = (lax.rem(slab - 1 + slabs, slabs), cross)
    above = (lax.rem(slab + 1, slabs), cross)
    barrier = pltpu.get_barrier_semaphore()
    for device in (below, above):
        pl.semaphore_signal(barrier, inc=1, device_id=device, device_id_type=pl.DeviceIdType.MESH)
    for side, plane in ((0, 0), (1, PLANES - 1)):
        for t in range(TILES):
            sent[side, :, t * LANES : (t + 1) * LANES] = gas_ref[plane_rows(t, plane), :]
    pl.semaphore_wait(barrier, 2)
    copies = [
        send(sent.at[0], got.at[1], send_sem.at[0], recv_sem.at[1], below),
        send(sent.at[1], got.at[0], send_sem.at[1], recv_sem.at[0], above),
    ]
    for each in copies:
        each.start()
    group = CHUNK // LANES
    for p in range(PLANES):
        for q in range(PER_PLANE):
            value = [gas_ref[plane_rows(q * group + t, p), :] for t in range(group)]
            parts_ref[(p + 1) * PER_PLANE + q] = parts_of(jnp.concatenate(value, axis=1))
    for side, plane in ((0, 0), (1, PLANES + 1)):
        send(sent.at[0], got.at[side], send_sem.at[0], recv_sem.at[side], above).wait_recv()
        for q in range(PER_PLANE):
            parts_ref[plane * PER_PLANE + q] = parts_of(got[side, :, q * CHUNK : (q + 1) * CHUNK])
    for each in copies:
        each.wait_send()


def halo(gas_rows):
    vmem = pl.BlockSpec(memory_space=pltpu.VMEM)
    dma = pltpu.SemaphoreType.DMA
    chunks = (PLANES + 2) * PER_PLANE
    return pl.pallas_call(
        halo_kernel,
        out_shape=jax.ShapeDtypeStruct((chunks, 3 * FIELDS, CHUNK), jnp.bfloat16),
        in_specs=[vmem],
        out_specs=vmem,
        scratch_shapes=[
            pltpu.VMEM((2, FIELDS, TILES * LANES), jnp.float32),
            pltpu.VMEM((2, FIELDS, TILES * LANES), jnp.float32),
            dma((2,)), dma((2,)),
        ],
        compiler_params=pltpu.CompilerParams(
            collective_id=1, has_side_effects=True, vmem_limit_bytes=16 << 20
        ),
        name="halo",
    )(gas_rows)


def spray_kernel(
    cell_at, count_at, gas_parts, record_ref, shares_ref, steam_ref, cell_ref, next_ref, terms,
    table, gathered,
):
    blocks = cell_ref.shape[0]
    chunks = (PLANES + 2) * PER_PLANE

    def listed(b, i):
        first = lax.shift_right_logical(cell_at[b * BLOCK], SHIFT)
        last = lax.shift_right_logical(cell_at[b * BLOCK + BLOCK - 1], SHIFT)

        def one(j, i):
            table[i] = b
            table[ROOM + i] = j
            table[2 * ROOM + j] = i
            return i + 1

        return lax.fori_loop(first, last + 1, one, i)

    for c in range(chunks):
        table[2 * ROOM + c] = PAIRS
    pairs = lax.fori_loop(0, blocks, listed, 0)

    def blank(i, carry):
        table[i] = 0
        table[ROOM + i] = -1
        return carry

    lax.fori_loop(pairs, PAIRS, blank, 0)
    rounds = lax.div(pairs + UNROLL - 1, UNROLL)

    gathered[...] = jnp.zeros(gathered.shape, jnp.float32)
    row = lax.broadcasted_iota(jnp.int32, (CHUNK, BLOCK), 0)

    def picked(i):
        c = table[ROOM + i]
        place = cell_ref[pl.ds(table[i], 1), :] - jnp.where(c < 0, chunks, c) * CHUNK
        return jnp.where(row == place, 1.0, 0.0).astype(jnp.bfloat16)

    def gather(n, carry):
        for k in range(UNROLL):
            i = n * UNROLL + k
            held = gas_parts[jnp.maximum(table[ROOM + i], 0)]
            part = jnp.dot(held, picked(i), preferred_element_type=jnp.float32)
            gathered[table[i]] += joined(part)
        return carry

    lax.fori_loop(0, rounds, gather, 0)

    lane = lax.broadcasted_iota(jnp.int32, (1, BLOCK), 1)
    species = lax.broadcasted_iota(jnp.int32, (steam_ref.shape[0], BLOCK), 0)
    steam = jnp.zeros(species.shape, jnp.float32)
    for k in range(steam_ref.shape[0]):
        steam = jnp.where(species == k, steam_ref[k], steam)

    def step(n, carry):
        for k in range(UNROLL):
            b = n * UNROLL + k
            cols = pl.ds(pl.multiple_of(b * BLOCK, BLOCK), BLOCK)
            gas = gathered[b]
            record = record_ref[:, cols]
            alive = lane < count_at[b]
            gas_velocity, gas_heat, vapour = gas[0:3], gas[3:4], gas[4:]
            velocity, heat, weight = record[0:3], record[3:4], record[4:5]
            slip = gas_velocity - velocity
            slip = slip * slip
            slip = slip[0:1] + slip[1:2] + slip[2:3]
            log_weight = jnp.log(weight)
            factor = drag_rate * jnp.exp(log_weight * (-2.0 / 3.0))
            factor = factor * (1.0 + 0.15 * jnp.exp(0.3435 * jnp.log(slip + 1.0)))
            moved = (velocity + factor * gas_velocity) / (1.0 + factor)
            surface = shares_ref[:, cols] * steam * jnp.exp(2.0 * (heat - 0.75))
            rates = evap_rate * weight * (surface - vapour)
            lost = jnp.sum(rates, axis=0, keepdims=True)
            exchange = warming_speed * (gas_heat - heat) * jnp.exp(log_weight * (1.0 / 3.0))
            warmed = heat + (exchange - latent_boiling_energy * lost) / weight
            scale = jnp.where(alive, volume_inverse, 0.0)
            terms[b, 0:3] = (weight * (velocity - moved) + lost * moved) * scale
            terms[b, 3:4] = (vapour_heat * lost - exchange) * scale
            terms[b, 4:16] = rates * scale
            next_ref[0:3, cols] = jnp.where(alive, moved, velocity)
            next_ref[3:4, cols] = jnp.where(alive, warmed, heat)
            next_ref[4:5, cols] = jnp.where(alive, weight - lost, weight)
        return carry

    lax.fori_loop(0, blocks // UNROLL, step, 0)


def spray(gas_parts, parcel_record, condensed_shares, surface_steam_factor, fine_cell, block_counts):
    blocks = block_counts.shape[0]
    vmem = pl.BlockSpec(memory_space=pltpu.VMEM)
    smem = pl.BlockSpec(memory_space=pltpu.SMEM)
    return pl.pallas_call(
        spray_kernel,
        out_shape=(
            jax.ShapeDtypeStruct(parcel_record.shape, jnp.float32),
            jax.ShapeDtypeStruct((blocks, FIELDS, BLOCK), jnp.float32),
            jax.ShapeDtypeStruct((3 * ROOM,), jnp.int32),
        ),
        in_specs=[smem, smem] + [vmem] * 3 + [smem, vmem],
        out_specs=(vmem, vmem, smem),
        scratch_shapes=[
            pltpu.VMEM((blocks, FIELDS, BLOCK), jnp.float32),
        ],
        compiler_params=pltpu.CompilerParams(vmem_limit_bytes=16 << 20),
        name="spray",
    )(
        fine_cell, block_counts, gas_parts, parcel_record, condensed_shares,
        surface_steam_factor, fine_cell.reshape(blocks, BLOCK),
    )


def scatter(table, cell_ref, terms_ref, base_ref, edge, slots):
    chunks = (PLANES + 2) * PER_PLANE
    row = lax.broadcasted_iota(jnp.int32, (CHUNK, BLOCK), 0)

    def step(n, carry):
        total, before = carry
        for k in range(UNROLL):
            i = n * UNROLL + k
            b = table[i]
            c = table[ROOM + i]
            place = cell_ref[pl.ds(b, 1), :] - jnp.where(c < 0, chunks, c) * CHUNK
            picked = jnp.where(row == place, 1.0, 0.0).astype(jnp.bfloat16)
            part = lax.dot_general(
                parts_of(terms_ref[b]), picked, (((1,), (1,)), ((), ())),
                preferred_element_type=jnp.float32,
            )
            total = joined(part) + total * jnp.where(c == before, 1.0, 0.0)
            slots[i] = total
            before = c
        return total, before

    none = jnp.zeros((FIELDS, CHUNK), jnp.float32)
    lax.fori_loop(0, PAIRS // UNROLL, step, (none, -2))
    slots[PAIRS] = none

    half = CHUNK // 2
    fold_row = lax.broadcasted_iota(jnp.int32, (half, LANES), 0)
    fold_lane = lax.broadcasted_iota(jnp.int32, (half, LANES), 1)
    fold = jnp.where(lax.shift_right_logical(fold_row, 1) == fold_lane, 1.0, 0.0).astype(jnp.bfloat16)

    def mass(value):
        kept = jnp.sum(value[4:], axis=0, keepdims=True)
        return [
            joined(jnp.dot(parts_of(kept[:, h * half : (h + 1) * half]), fold, preferred_element_type=jnp.float32))
            for h in range(2)
        ]

    own, low, high = [], [], []
    group = CHUNK // LANES
    for q in range(PER_PLANE):
        cols = slice(q * CHUNK, (q + 1) * CHUNK)
        below = slots[table[2 * ROOM + q]]
        above = slots[table[2 * ROOM + (PLANES + 1) * PER_PLANE + q]]
        edge[0, :, cols] = below
        edge[1, :, cols] = above
        inside = None
        for p in range(PLANES):
            value = slots[table[2 * ROOM + (p + 1) * PER_PLANE + q]]
            for t in range(group):
                base_ref[plane_rows(q * group + t, p), :] = value[:, t * LANES : (t + 1) * LANES]
            inside = value if inside is None else inside + value
        own += mass(inside)
        low += mass(below)
        high += mass(above)
    return tuple(0.25 * jnp.concatenate(rows, axis=0) for rows in (own, low, high))


def spread_kernel(
    table, cell_ref, terms_ref, base_ref, halo_ref, grid_ref, own_ref, outer_ref, edge_ref, slots, got,
    pair_send, pair_recv, edge_send, edge_recv, line_send, line_recv,
    minor_send, minor_recv, major_send, major_recv, core_send, core_recv,
):
    slabs = 2 * RING * LINE
    slab = lax.axis_index("slab")
    cross = lax.axis_index("cross")
    core = lax.rem(cross, 2)
    z = lax.rem(slab, LINE)
    x = lax.rem(lax.div(slab, LINE), RING)
    y = lax.div(cross, 2) * 2 + lax.div(slab, RING * LINE)
    odd = lax.rem(slab, 2)
    sign = 2 * odd - 1
    pair = lax.div(slab, 2)
    line_pair = lax.div(z, 2)
    major = core * x + (1 - core) * y
    minor = core * y + (1 - core) * x

    def near(by):
        return (lax.rem(slab + by + slabs, slabs), cross)

    def place(at_x, at_y, at_z):
        return (lax.rem(at_y, 2) * (RING * LINE) + at_x * LINE + at_z, lax.div(at_y, 2) * 2 + core)

    def in_line(by):
        return lax.rem(z + by + LINE, LINE)

    def minor_peer(other):
        return place(core * x + (1 - core) * other, core * other + (1 - core) * y, z)

    def major_peer(other):
        return place(core * other + (1 - core) * x, core * y + (1 - core) * other, z)

    def turn(own, by):
        return lax.rem(own + by, RING)

    copy = send

    other_core = (slab, cross + 1 - 2 * core)
    line_from = [sign * k for k in (1, 3, 5, 7)] + [-sign * k for k in (2, 4, 6)]
    low = lax.rem(2 * pair - 1 + slabs, slabs)
    high = lax.rem(2 * pair + 2, slabs)

    barrier = pltpu.get_barrier_semaphore()
    sources = [near(-sign), (low, cross), (high, cross), near(-1), near(1)]
    sources += [place(x, y, in_line(by)) for by in line_from]
    sources += [minor_peer(turn(minor, by)) for by in (1, 2, 3)]
    sources += [major_peer(turn(major, by)) for by in (1, 2, 3)]
    sources += [other_core]
    for device in sources:
        pl.semaphore_signal(barrier, inc=1, device_id=device, device_id_type=pl.DeviceIdType.MESH)
    own, low_tile, high_tile = scatter(table, cell_ref, terms_ref, base_ref, edge_ref, slots)
    own_ref[...] = own + jnp.where(odd == 1, low_tile, high_tile)
    outer_ref[...] = jnp.where(odd == 1, high_tile, low_tile)
    pl.semaphore_wait(barrier, len(sources))

    copies = [
        copy(own_ref, got.at[0], pair_send.at[0], pair_recv.at[0], near(-sign)),
        copy(outer_ref, got.at[2 - odd], pair_send.at[1], pair_recv.at[2 - odd], near(sign)),
        copy(outer_ref, got.at[2 - odd], pair_send.at[2], pair_recv.at[2 - odd], near(2 * sign)),
    ]
    for each in copies:
        each.start()
    for slot in range(3):
        copy(own_ref, got.at[slot], pair_send.at[slot], pair_recv.at[slot], near(1)).wait_recv()
    grid_ref[core, major, minor, line_pair] = (own_ref[...] + got[0]) + (got[1] + got[2])
    edges = [
        copy(edge_ref.at[0], halo_ref.at[1], edge_send.at[0], edge_recv.at[1], near(-1)),
        copy(edge_ref.at[1], halo_ref.at[0], edge_send.at[1], edge_recv.at[0], near(1)),
    ]
    tile = grid_ref.at[core, major, minor, line_pair]
    for k in range(1, 8):
        each = copy(tile, tile, line_send.at[k - 1], line_recv.at[line_pair], place(x, y, in_line(sign * k)))
        each.start()
        copies.append(each)
    tiles = [line_pair] + [lax.div(in_line(sign * k if k % 2 else -sign * k), 2) for k in range(1, 8)]

    def go(src, dst, send_sem, recv_sem, device):
        each = copy(src, dst, send_sem, recv_sem, device)
        each.start()
        copies.append(each)

    def to_minors(k):
        t = tiles[k]
        src = grid_ref.at[core, major, minor, t]
        if k:
            copy(src, src, line_send.at[0], line_recv.at[t], near(1)).wait_recv()
        for by in (1, 2, 3):
            go(src, src, minor_send.at[by - 1, k], minor_recv.at[minor, t], minor_peer(turn(minor, by)))

    def to_majors(k):
        t = tiles[k]
        for by in (1, 2, 3):
            src = grid_ref.at[core, major, turn(minor, by), t]
            copy(src, src, minor_send.at[0, k], minor_recv.at[turn(minor, by), t], near(1)).wait_recv()
        src = grid_ref.at[core, major, :, t]
        for by in (1, 2, 3):
            go(src, src, major_send.at[by - 1, k], major_recv.at[major, t], major_peer(turn(major, by)))
        go(src, src, core_send.at[0, k], core_recv.at[major, t], other_core)

    def to_core(k):
        t = tiles[k]
        for by in (1, 2, 3):
            src = grid_ref.at[core, turn(major, by), :, t]
            copy(src, src, major_send.at[0, k], major_recv.at[turn(major, by), t], near(1)).wait_recv()
            go(src, src, core_send.at[by, k], core_recv.at[turn(major, by), t], other_core)

    for step in range(8 + LAG_MINOR + LAG_MAJOR):
        if step < 8:
            to_minors(step)
        if step == 0:
            for each in edges:
                each.start()
        if 0 <= step - LAG_MINOR < 8:
            to_majors(step - LAG_MINOR)
        if 0 <= step - LAG_MINOR - LAG_MAJOR < 8:
            to_core(step - LAG_MINOR - LAG_MAJOR)
    for by in range(RING):
        for k in range(8):
            src = grid_ref.at[1 - core, by, :, k]
            copy(src, src, core_send.at[0, k], core_recv.at[by, k], other_core).wait_recv()
    for slot in range(2):
        copy(edge_ref.at[0], halo_ref.at[slot], edge_send.at[0], edge_recv.at[slot], near(1)).wait_recv()
    for each in copies + edges:
        each.wait_send()


def spread(table, cells, terms):
    dma = pltpu.SemaphoreType.DMA
    vmem = pl.BlockSpec(memory_space=pltpu.VMEM)
    smem = pl.BlockSpec(memory_space=pltpu.SMEM)
    side = (2, FIELDS, TILES * LANES)
    return pl.pallas_call(
        spread_kernel,
        out_shape=(
            jax.ShapeDtypeStruct((FIELDS * TILES * PLANES, LANES), jnp.float32),
            jax.ShapeDtypeStruct(side, jnp.float32),
            jax.ShapeDtypeStruct((2, RING, RING, LINE // 2, ROWS, LANES), jnp.float32),
        ),
        in_specs=[smem, vmem, vmem],
        out_specs=(vmem, vmem, vmem),
        scratch_shapes=[
            pltpu.VMEM((ROWS, LANES), jnp.float32),
            pltpu.VMEM((ROWS, LANES), jnp.float32),
            pltpu.VMEM(side, jnp.float32),
            pltpu.VMEM((PAIRS + 1, FIELDS, CHUNK), jnp.float32),
            pltpu.VMEM((3, ROWS, LANES), jnp.float32),
            dma((3,)), dma((3,)), dma((2,)), dma((2,)), dma((7,)), dma((LINE // 2,)),
            dma((3, 8)), dma((RING, 8)), dma((3, 8)), dma((RING, 8)), dma((RING, 8)), dma((RING, 8)),
        ],
        compiler_params=pltpu.CompilerParams(
            collective_id=0, has_side_effects=True, vmem_limit_bytes=16 << 20
        ),
        name="spread",
    )(table, cells, terms)


def finish_kernel(base_ref, halo_ref, grid_ref, fine_ref, out_ref, fine, source, even, uneven, even_turned, uneven_turned, flat, result, fine_sem, out_sem):
    sub = lax.broadcasted_iota(jnp.int32, (ROWS, LANES), 0)
    lane = lax.broadcasted_iota(jnp.int32, (ROWS, LANES), 1)
    first = sub == 0
    last = sub == ROWS - 1
    for f in range(FIELDS):
        for t in range(TILES):
            cols = slice(t * LANES, (t + 1) * LANES)
            rows = slice((f * TILES + t) * PLANES, (f * TILES + t + 1) * PLANES)
            low = jnp.broadcast_to(halo_ref[0, f : f + 1, cols], (PLANES, LANES))
            high = jnp.broadcast_to(halo_ref[1, f : f + 1, cols], (PLANES, LANES))
            fine[rows, :] = base_ref[rows, :] + jnp.where(first, low, jnp.where(last, high, 0.0))
    fine_copy = pltpu.make_async_copy(fine, fine_ref, fine_sem)
    fine_copy.start()

    wide = COARSE // 2
    none = jnp.zeros((wide, LANES), jnp.float32)
    blank = jnp.zeros((ROWS, LANES), jnp.float32)
    half = LANES // 2
    for held, turned in ((even, even_turned), (uneven, uneven_turned)):
        held[0] = none
        held[COARSE + 1] = none
        for plane in range(COARSE + 1):
            turned[plane * STRIDE : plane * STRIDE + ROWS, :] = blank

    def keep(held, turned, plane, c, value):
        held[plane + 1, c * ROWS : (c + 1) * ROWS, :] = value
        at = pl.multiple_of(plane * STRIDE + (c + 1) * ROWS, ROWS)
        turned[pl.ds(at, ROWS), :] = pltpu.roll(value, half, 1)

    for plane in range(COARSE):
        y_lo, x, j = plane // 32, (plane // 8) % RING, plane % 8
        for c in range(RING):
            y = (c // 2) * 2 + y_lo
            at = grid_ref[0, y, x, j] if c % 2 == 0 else grid_ref[1, x, y, j]
            value = at * (1.0 / 6.0)
            source[plane, c * ROWS : (c + 1) * ROWS, :] = value
            keep(even, even_turned, plane, c, value)

    depth = lax.rem(lane, half)
    upper = depth < half - 1
    lower = depth > 0
    left = lane < half

    def relaxed(held, turned, plane, c):
        tile = slice(c * ROWS, (c + 1) * ROWS)
        at = plane * STRIDE + (c + 1) * ROWS
        mid = held[plane + 1, tile, :]
        across = jnp.where(left, turned[pl.ds(at - 1, ROWS), :], turned[pl.ds(at + 1, ROWS), :])
        total = turned[pl.ds(at, ROWS), :] + across
        along = jnp.where(upper, pltpu.roll(mid, LANES - 1, 1), 0.0)
        along += jnp.where(lower, pltpu.roll(mid, 1, 1), 0.0)
        total += along + (held[plane, tile, :] + held[plane + 2, tile, :])
        return total * (1.0 / 6.0) + source[plane, tile, :]

    def sweep(held, turned, to, to_turned):
        def some(n, carry):
            for k in range(UNROLL):
                for c in range(RING):
                    keep(to, to_turned, n * UNROLL + k, c, relaxed(held, turned, n * UNROLL + k, c))
            return carry

        lax.fori_loop(0, COARSE // UNROLL, some, 0)

    sweep(even, even_turned, uneven, uneven_turned)
    sweep(uneven, uneven_turned, even, even_turned)
    copies = []
    for group in range(COARSE // ROWS):
        for k in range(ROWS):
            plane = group * ROWS + k
            for c in range(RING):
                at = plane * wide + c * ROWS
                flat[at : at + ROWS, :] = relaxed(even, even_turned, plane, c)
        rows = slice(group * ROWS, (group + 1) * ROWS)
        for r in range(wide):
            value = flat[pl.ds(group * ROWS * wide + r, ROWS, stride=wide), :]
            result[rows, r * LANES : (r + 1) * LANES] = value
        each = pltpu.make_async_copy(result.at[rows], out_ref.at[rows], out_sem.at[group])
        each.start()
        copies.append(each)
    for each in copies:
        each.wait()
    fine_copy.wait()


def finish(base, halo_sum, grid):
    wide = COARSE // 2
    vmem = pl.BlockSpec(memory_space=pltpu.VMEM)
    hbm = pl.BlockSpec(memory_space=pl.ANY)
    dma = pltpu.SemaphoreType.DMA
    return pl.pallas_call(
        finish_kernel,
        out_shape=(
            jax.ShapeDtypeStruct(base.shape, jnp.float32),
            jax.ShapeDtypeStruct((COARSE, COARSE * COARSE), jnp.float32),
        ),
        in_specs=[vmem, vmem, vmem],
        out_specs=(hbm, hbm),
        scratch_shapes=[
            pltpu.VMEM(base.shape, jnp.float32),
            pltpu.VMEM((COARSE, wide, LANES), jnp.float32),
            pltpu.VMEM((COARSE + 2, wide, LANES), jnp.float32),
            pltpu.VMEM((COARSE + 2, wide, LANES), jnp.float32),
            pltpu.VMEM((COARSE * STRIDE + ROWS, LANES), jnp.float32),
            pltpu.VMEM((COARSE * STRIDE + ROWS, LANES), jnp.float32),
            pltpu.VMEM((COARSE * wide, LANES), jnp.float32),
            pltpu.VMEM((COARSE, COARSE * COARSE), jnp.float32),
            dma, dma((COARSE // ROWS,)),
        ],
        compiler_params=pltpu.CompilerParams(vmem_limit_bytes=16 << 20),
        name="finish",
    )(base, halo_sum, grid)


def body(gas_state, parcel_record, condensed_shares, surface_steam_factor, fine_cell, block_counts):
    rows = gas_state.reshape(FIELDS, PLANES, TILES, LANES).transpose(0, 2, 1, 3).reshape(-1, LANES)
    parts = halo(rows)
    parcel_next, terms, table = spray(
        parts, parcel_record, condensed_shares, surface_steam_factor, fine_cell, block_counts
    )
    base, halo_sum, grid = spread(table, fine_cell.reshape(-1, BLOCK), terms)
    fine_rows, correction = finish(base, halo_sum, grid)
    fine_source = fine_rows.reshape(FIELDS, TILES, PLANES, LANES).transpose(0, 2, 1, 3).reshape(gas_state.shape)
    return (parcel_next, fine_source, correction)


def solution(mesh):
    in_specs = (
        P(None, "slab", "cross"),
        P(None, ("slab", "cross")),
        P(None, ("slab", "cross")),
        P(),
        P(("slab", "cross")),
        P(("slab", "cross")),
    )
    out_specs = (P(None, ("slab", "cross")), P(None, "slab", "cross"), P())
    return jax.shard_map(body, mesh=mesh, in_specs=in_specs, out_specs=out_specs, check_vma=False)
```

```python
import jax
import jax.numpy as jnp
from jax import lax
from jax.experimental import pallas as pl
from jax.experimental.pallas import tpu as pltpu
from jax.sharding import PartitionSpec as P

BLOCK = 128
COARSE = 64


drag_rate = 0.5
evap_rate = 0.08
warming_speed = 0.3
latent_boiling_energy = 0.5
vapour_heat = 1.5
volume_inverse = 4.0


LINE = 16
RING = 4
LANES = 128
ROWS = 8
FIELDS = 16
PLANES = 8
TILES = 16
CHUNK = 256
PER_PLANE = 8
SHIFT = 8
UNROLL = 16
STEP = 8
PAIRS = 112
ROOM = 120
LAG_MINOR = 5
LAG_MAJOR = 5
SPAN = 16


def parts_of(value):
    high = value.astype(jnp.bfloat16)
    rest = value - high.astype(jnp.float32)
    middle = rest.astype(jnp.bfloat16)
    low = (rest - middle.astype(jnp.float32)).astype(jnp.bfloat16)
    return jnp.concatenate([high, middle, low], axis=0)


def joined(value):
    third = value.shape[0] // 3
    return value[:third] + (value[third : 2 * third] + value[2 * third :])


def chosen(row, cells, chunk):
    place = cells - jnp.where(chunk < 0, (PLANES + 2) * PER_PLANE, chunk) * CHUNK
    place = jnp.where((place < 0) | (place >= CHUNK), -1, place)
    place = place.astype(jnp.float32).astype(jnp.bfloat16)
    return jnp.where(row == place, jnp.bfloat16(1), jnp.bfloat16(0))


def chunk_rows():
    row = lax.broadcasted_iota(jnp.int32, (CHUNK, BLOCK), 0)
    return row.astype(jnp.float32).astype(jnp.bfloat16)


def plane_rows(tile, plane):
    return pl.ds(tile * PLANES + plane, FIELDS, stride=TILES * PLANES)


def send(src, dst, send_sem, recv_sem, device):
    return pltpu.make_async_remote_copy(
        src_ref=src, dst_ref=dst, send_sem=send_sem, recv_sem=recv_sem,
        device_id=device, device_id_type=pl.DeviceIdType.MESH,
    )


def halo_kernel(gas_ref, parts_ref, sent, got, send_sem, recv_sem):
    slabs = 2 * RING * LINE
    slab = lax.axis_index("slab")
    cross = lax.axis_index("cross")
    below = (lax.rem(slab - 1 + slabs, slabs), cross)
    above = (lax.rem(slab + 1, slabs), cross)
    barrier = pltpu.get_barrier_semaphore()
    for device in (below, above):
        pl.semaphore_signal(barrier, inc=1, device_id=device, device_id_type=pl.DeviceIdType.MESH)
    for side, plane in ((0, 0), (1, PLANES - 1)):
        for t in range(TILES):
            sent[side, :, t * LANES : (t + 1) * LANES] = gas_ref[plane_rows(t, plane), :]
    pl.semaphore_wait(barrier, 2)
    copies = [
        send(sent.at[0], got.at[1], send_sem.at[0], recv_sem.at[1], below),
        send(sent.at[1], got.at[0], send_sem.at[1], recv_sem.at[0], above),
    ]
    for each in copies:
        each.start()
    group = CHUNK // LANES
    for p in range(PLANES):
        for q in range(PER_PLANE):
            value = [gas_ref[plane_rows(q * group + t, p), :] for t in range(group)]
            parts_ref[(p + 1) * PER_PLANE + q] = parts_of(jnp.concatenate(value, axis=1))
    for side, plane in ((0, 0), (1, PLANES + 1)):
        send(sent.at[0], got.at[side], send_sem.at[0], recv_sem.at[side], above).wait_recv()
        for q in range(PER_PLANE):
            parts_ref[plane * PER_PLANE + q] = parts_of(got[side, :, q * CHUNK : (q + 1) * CHUNK])
    for each in copies:
        each.wait_send()


def halo(gas_rows):
    vmem = pl.BlockSpec(memory_space=pltpu.VMEM)
    dma = pltpu.SemaphoreType.DMA
    chunks = (PLANES + 2) * PER_PLANE
    return pl.pallas_call(
        halo_kernel,
        out_shape=jax.ShapeDtypeStruct((chunks, 3 * FIELDS, CHUNK), jnp.bfloat16),
        in_specs=[vmem],
        out_specs=vmem,
        scratch_shapes=[
            pltpu.VMEM((2, FIELDS, TILES * LANES), jnp.float32),
            pltpu.VMEM((2, FIELDS, TILES * LANES), jnp.float32),
            dma((2,)), dma((2,)),
        ],
        compiler_params=pltpu.CompilerParams(
            collective_id=1, has_side_effects=True, vmem_limit_bytes=16 << 20
        ),
        name="halo",
    )(gas_rows)


def spray_kernel(
    cell_at, count_at, gas_parts, record_ref, shares_ref, steam_ref, cell_ref, next_ref, terms,
    table, gathered,
):
    blocks = cell_ref.shape[0]
    chunks = (PLANES + 2) * PER_PLANE

    def listed(b, i):
        first = lax.shift_right_logical(cell_at[b * BLOCK], SHIFT)
        last = lax.shift_right_logical(cell_at[b * BLOCK + BLOCK - 1], SHIFT)

        def one(j, i):
            table[i] = b
            table[ROOM + i] = j
            table[2 * ROOM + j] = i
            return i + 1

        return lax.fori_loop(first, last + 1, one, i)

    for c in range(chunks):
        table[2 * ROOM + c] = PAIRS
    pairs = lax.fori_loop(0, blocks, listed, 0)

    def blank(i, carry):
        table[i] = 0
        table[ROOM + i] = -1
        return carry

    lax.fori_loop(pairs, PAIRS, blank, 0)
    rounds = lax.div(pairs + UNROLL - 1, UNROLL)

    gathered[...] = jnp.zeros(gathered.shape, jnp.float32)
    row = chunk_rows()

    def picked(i):
        return chosen(row, cell_ref[pl.ds(table[i], 1), :], table[ROOM + i])

    def gather(n, carry):
        for k in range(UNROLL):
            i = n * UNROLL + k
            held = gas_parts[jnp.maximum(table[ROOM + i], 0)]
            part = jnp.dot(held, picked(i), preferred_element_type=jnp.float32)
            gathered[table[i]] += joined(part)
        return carry

    lax.fori_loop(0, rounds, gather, 0)

    lane = lax.broadcasted_iota(jnp.int32, (1, BLOCK), 1)
    species = lax.broadcasted_iota(jnp.int32, (steam_ref.shape[0], BLOCK), 0)
    steam = jnp.zeros(species.shape, jnp.float32)
    for k in range(steam_ref.shape[0]):
        steam = jnp.where(species == k, steam_ref[k], steam)

    def step(n, carry):
        for k in range(STEP):
            b = n * STEP + k
            cols = pl.ds(pl.multiple_of(b * BLOCK, BLOCK), BLOCK)
            gas = gathered[b]
            record = record_ref[:, cols]
            alive = lane < count_at[b]
            gas_velocity, gas_heat, vapour = gas[0:3], gas[3:4], gas[4:]
            velocity, heat, weight = record[0:3], record[3:4], record[4:5]
            slip = gas_velocity - velocity
            slip = slip * slip
            slip = slip[0:1] + slip[1:2] + slip[2:3]
            log_weight = jnp.log(weight)
            factor = drag_rate * jnp.exp(log_weight * (-2.0 / 3.0))
            factor = factor * (1.0 + 0.15 * jnp.exp(0.3435 * jnp.log(slip + 1.0)))
            moved = (velocity + factor * gas_velocity) / (1.0 + factor)
            surface = shares_ref[:, cols] * steam * jnp.exp(2.0 * (heat - 0.75))
            rates = evap_rate * weight * (surface - vapour)
            lost = jnp.sum(rates, axis=0, keepdims=True)
            exchange = warming_speed * (gas_heat - heat) * jnp.exp(log_weight * (1.0 / 3.0))
            warmed = heat + (exchange - latent_boiling_energy * lost) / weight
            scale = jnp.where(alive, volume_inverse, 0.0)
            terms[b, 0:3] = (weight * (velocity - moved) + lost * moved) * scale
            terms[b, 3:4] = (vapour_heat * lost - exchange) * scale
            terms[b, 4:16] = rates * scale
            next_ref[0:3, cols] = jnp.where(alive, moved, velocity)
            next_ref[3:4, cols] = jnp.where(alive, warmed, heat)
            next_ref[4:5, cols] = jnp.where(alive, weight - lost, weight)
        return carry

    lax.fori_loop(0, blocks // STEP, step, 0)


def spray(gas_parts, parcel_record, condensed_shares, surface_steam_factor, fine_cell, block_counts):
    blocks = block_counts.shape[0]
    vmem = pl.BlockSpec(memory_space=pltpu.VMEM)
    smem = pl.BlockSpec(memory_space=pltpu.SMEM)
    return pl.pallas_call(
        spray_kernel,
        out_shape=(
            jax.ShapeDtypeStruct(parcel_record.shape, jnp.float32),
            jax.ShapeDtypeStruct((blocks, FIELDS, BLOCK), jnp.float32),
            jax.ShapeDtypeStruct((3 * ROOM,), jnp.int32),
        ),
        in_specs=[smem, smem] + [vmem] * 3 + [smem, vmem],
        out_specs=(vmem, vmem, smem),
        scratch_shapes=[
            pltpu.VMEM((blocks, FIELDS, BLOCK), jnp.float32),
        ],
        compiler_params=pltpu.CompilerParams(vmem_limit_bytes=16 << 20),
        name="spray",
    )(
        fine_cell, block_counts, gas_parts, parcel_record, condensed_shares,
        surface_steam_factor, fine_cell.reshape(blocks, BLOCK),
    )


def scatter(table, cell_ref, terms_ref, base_ref, edge, slots):
    row = chunk_rows()

    def step(n, carry):
        total, before = carry
        for k in range(UNROLL):
            i = n * UNROLL + k
            b = table[i]
            c = table[ROOM + i]
            picked = chosen(row, cell_ref[pl.ds(b, 1), :], c)
            part = lax.dot_general(
                parts_of(terms_ref[b]), picked, (((1,), (1,)), ((), ())),
                preferred_element_type=jnp.float32,
            )
            total = joined(part) + total * jnp.where(c == before, 1.0, 0.0)
            slots[i] = total
            before = c
        return total, before

    none = jnp.zeros((FIELDS, CHUNK), jnp.float32)
    lax.fori_loop(0, PAIRS // UNROLL, step, (none, -2))
    slots[PAIRS] = none

    fold_row = lax.broadcasted_iota(jnp.int32, (CHUNK, LANES), 0)
    fold_lane = lax.broadcasted_iota(jnp.int32, (CHUNK, LANES), 1)
    fold = jnp.where(lax.shift_right_logical(fold_row, 1) == fold_lane, 1.0, 0.0).astype(jnp.bfloat16)

    def mass(value):
        kept = jnp.sum(value[4:], axis=0, keepdims=True)
        return [joined(jnp.dot(parts_of(kept), fold, preferred_element_type=jnp.float32))]

    own, low, high = [], [], []
    group = CHUNK // LANES
    for q in range(PER_PLANE):
        cols = slice(q * CHUNK, (q + 1) * CHUNK)
        below = slots[table[2 * ROOM + q]]
        above = slots[table[2 * ROOM + (PLANES + 1) * PER_PLANE + q]]
        edge[0, :, cols] = below
        edge[1, :, cols] = above
        inside = None
        for p in range(PLANES):
            value = slots[table[2 * ROOM + (p + 1) * PER_PLANE + q]]
            for t in range(group):
                base_ref[plane_rows(q * group + t, p), :] = value[:, t * LANES : (t + 1) * LANES]
            inside = value if inside is None else inside + value
        own += mass(inside)
        low += mass(below)
        high += mass(above)
    return tuple(0.25 * jnp.concatenate(rows, axis=0) for rows in (own, low, high))


def spread_kernel(
    table, cell_ref, terms_ref, base_ref, halo_ref, grid_ref, own_ref, outer_ref, edge_ref, slots, got,
    pair_send, pair_recv, edge_send, edge_recv, line_send, line_recv,
    minor_send, minor_recv, major_send, major_recv, core_send, core_recv,
):
    slabs = 2 * RING * LINE
    slab = lax.axis_index("slab")
    cross = lax.axis_index("cross")
    core = lax.rem(cross, 2)
    z = lax.rem(slab, LINE)
    x = lax.rem(lax.div(slab, LINE), RING)
    y = lax.div(cross, 2) * 2 + lax.div(slab, RING * LINE)
    odd = lax.rem(slab, 2)
    sign = 2 * odd - 1
    pair = lax.div(slab, 2)
    line_pair = lax.div(z, 2)
    major = core * x + (1 - core) * y
    minor = core * y + (1 - core) * x

    def near(by):
        return (lax.rem(slab + by + slabs, slabs), cross)

    def place(at_x, at_y, at_z):
        return (lax.rem(at_y, 2) * (RING * LINE) + at_x * LINE + at_z, lax.div(at_y, 2) * 2 + core)

    def in_line(by):
        return lax.rem(z + by + LINE, LINE)

    def minor_peer(other):
        return place(core * x + (1 - core) * other, core * other + (1 - core) * y, z)

    def major_peer(other):
        return place(core * other + (1 - core) * x, core * y + (1 - core) * other, z)

    def turn(own, by):
        return lax.rem(own + by, RING)

    copy = send

    other_core = (slab, cross + 1 - 2 * core)
    line_from = [sign * k for k in (1, 3, 5, 7)] + [-sign * k for k in (2, 4, 6)]
    low = lax.rem(2 * pair - 1 + slabs, slabs)
    high = lax.rem(2 * pair + 2, slabs)

    barrier = pltpu.get_barrier_semaphore()
    sources = [near(-sign), (low, cross), (high, cross), near(-1), near(1)]
    sources += [place(x, y, in_line(by)) for by in line_from]
    sources += [minor_peer(turn(minor, by)) for by in (1, 2, 3)]
    sources += [major_peer(turn(major, by)) for by in (1, 2, 3)]
    sources += [other_core]
    for device in sources:
        pl.semaphore_signal(barrier, inc=1, device_id=device, device_id_type=pl.DeviceIdType.MESH)
    own, low_tile, high_tile = scatter(table, cell_ref, terms_ref, base_ref, edge_ref, slots)
    own_ref[...] = own + jnp.where(odd == 1, low_tile, high_tile)
    outer_ref[...] = jnp.where(odd == 1, high_tile, low_tile)
    pl.semaphore_wait(barrier, len(sources))

    copies = [
        copy(own_ref, got.at[0], pair_send.at[0], pair_recv.at[0], near(-sign)),
        copy(outer_ref, got.at[2 - odd], pair_send.at[1], pair_recv.at[2 - odd], near(sign)),
        copy(outer_ref, got.at[2 - odd], pair_send.at[2], pair_recv.at[2 - odd], near(2 * sign)),
    ]
    for each in copies:
        each.start()
    for slot in range(3):
        copy(own_ref, got.at[slot], pair_send.at[slot], pair_recv.at[slot], near(1)).wait_recv()
    grid_ref[core, major, minor, line_pair] = (own_ref[...] + got[0]) + (got[1] + got[2])
    edges = [
        copy(edge_ref.at[0], halo_ref.at[1], edge_send.at[0], edge_recv.at[1], near(-1)),
        copy(edge_ref.at[1], halo_ref.at[0], edge_send.at[1], edge_recv.at[0], near(1)),
    ]
    tile = grid_ref.at[core, major, minor, line_pair]
    for k in range(1, 8):
        each = copy(tile, tile, line_send.at[k - 1], line_recv.at[line_pair], place(x, y, in_line(sign * k)))
        each.start()
        copies.append(each)
    tiles = [line_pair] + [lax.div(in_line(sign * k if k % 2 else -sign * k), 2) for k in range(1, 8)]

    def go(src, dst, send_sem, recv_sem, device):
        each = copy(src, dst, send_sem, recv_sem, device)
        each.start()
        copies.append(each)

    def to_minors(k):
        t = tiles[k]
        src = grid_ref.at[core, major, minor, t]
        if k:
            copy(src, src, line_send.at[0], line_recv.at[t], near(1)).wait_recv()
        for by in (1, 2, 3):
            go(src, src, minor_send.at[by - 1, k], minor_recv.at[minor, t], minor_peer(turn(minor, by)))

    def to_majors(k):
        t = tiles[k]
        for by in (1, 2, 3):
            src = grid_ref.at[core, major, turn(minor, by), t]
            copy(src, src, minor_send.at[0, k], minor_recv.at[turn(minor, by), t], near(1)).wait_recv()
        src = grid_ref.at[core, major, :, t]
        for by in (1, 2, 3):
            go(src, src, major_send.at[by - 1, k], major_recv.at[major, t], major_peer(turn(major, by)))
        go(src, src, core_send.at[0, k], core_recv.at[major, t], other_core)

    def to_core(k):
        t = tiles[k]
        for by in (1, 2, 3):
            src = grid_ref.at[core, turn(major, by), :, t]
            copy(src, src, major_send.at[0, k], major_recv.at[turn(major, by), t], near(1)).wait_recv()
            go(src, src, core_send.at[by, k], core_recv.at[turn(major, by), t], other_core)

    for step in range(8 + LAG_MINOR + LAG_MAJOR):
        if step < 8:
            to_minors(step)
        if step == 0:
            for each in edges:
                each.start()
        if 0 <= step - LAG_MINOR < 8:
            to_majors(step - LAG_MINOR)
        if 0 <= step - LAG_MINOR - LAG_MAJOR < 8:
            to_core(step - LAG_MINOR - LAG_MAJOR)
    for by in range(RING):
        for k in range(8):
            src = grid_ref.at[1 - core, by, :, k]
            copy(src, src, core_send.at[0, k], core_recv.at[by, k], other_core).wait_recv()
    for slot in range(2):
        copy(edge_ref.at[0], halo_ref.at[slot], edge_send.at[0], edge_recv.at[slot], near(1)).wait_recv()
    for each in copies + edges:
        each.wait_send()


def spread(table, cells, terms):
    dma = pltpu.SemaphoreType.DMA
    vmem = pl.BlockSpec(memory_space=pltpu.VMEM)
    smem = pl.BlockSpec(memory_space=pltpu.SMEM)
    side = (2, FIELDS, TILES * LANES)
    return pl.pallas_call(
        spread_kernel,
        out_shape=(
            jax.ShapeDtypeStruct((FIELDS * TILES * PLANES, LANES), jnp.float32),
            jax.ShapeDtypeStruct(side, jnp.float32),
            jax.ShapeDtypeStruct((2, RING, RING, LINE // 2, ROWS, LANES), jnp.float32),
        ),
        in_specs=[smem, vmem, vmem],
        out_specs=(vmem, vmem, vmem),
        scratch_shapes=[
            pltpu.VMEM((ROWS, LANES), jnp.float32),
            pltpu.VMEM((ROWS, LANES), jnp.float32),
            pltpu.VMEM(side, jnp.float32),
            pltpu.VMEM((PAIRS + 1, FIELDS, CHUNK), jnp.float32),
            pltpu.VMEM((3, ROWS, LANES), jnp.float32),
            dma((3,)), dma((3,)), dma((2,)), dma((2,)), dma((7,)), dma((LINE // 2,)),
            dma((3, 8)), dma((RING, 8)), dma((3, 8)), dma((RING, 8)), dma((RING, 8)), dma((RING, 8)),
        ],
        compiler_params=pltpu.CompilerParams(
            collective_id=0, has_side_effects=True, vmem_limit_bytes=16 << 20
        ),
        name="spread",
    )(table, cells, terms)


def finish_kernel(base_ref, halo_ref, grid_ref, fine_ref, out_ref, fine, source, even, uneven, flat, result, fine_sem, out_sem):
    sub = lax.broadcasted_iota(jnp.int32, (ROWS, LANES), 0)
    lane = lax.broadcasted_iota(jnp.int32, (ROWS, LANES), 1)
    first = sub == 0
    last = sub == ROWS - 1
    for f in range(FIELDS):
        for t in range(TILES):
            cols = slice(t * LANES, (t + 1) * LANES)
            rows = slice((f * TILES + t) * PLANES, (f * TILES + t + 1) * PLANES)
            low = jnp.broadcast_to(halo_ref[0, f : f + 1, cols], (PLANES, LANES))
            high = jnp.broadcast_to(halo_ref[1, f : f + 1, cols], (PLANES, LANES))
            fine[rows, :] = base_ref[rows, :] + jnp.where(first, low, jnp.where(last, high, 0.0))
    fine_copy = pltpu.make_async_copy(fine, fine_ref, fine_sem)
    fine_copy.start()

    wide = COARSE // 2
    none = jnp.zeros((wide, LANES), jnp.float32)
    for held in (even, uneven):
        held[0] = none
        held[COARSE + 1] = none
    for plane in range(COARSE):
        y_lo, x, j = plane // 32, (plane // 8) % RING, plane % 8
        for c in range(RING):
            y = (c // 2) * 2 + y_lo
            at = grid_ref[0, y, x, j] if c % 2 == 0 else grid_ref[1, x, y, j]
            value = at * (1.0 / 6.0)
            source[plane, c * ROWS : (c + 1) * ROWS, :] = value
            even[plane + 1, c * ROWS : (c + 1) * ROWS, :] = value

    half = LANES // 2
    depth = lax.rem(lane, half)
    upper = jnp.where(depth < half - 1, 1.0, 0.0)
    lower = jnp.where(depth > 0, 1.0, 0.0)
    left = lane < half
    blank = jnp.zeros((ROWS, LANES), jnp.float32)

    def relaxed(src, plane):
        mid = [src[plane + 1, c * ROWS : (c + 1) * ROWS, :] for c in range(RING)]
        turned = [pltpu.roll(value, half, 1) for value in mid]
        down = [blank] + [pltpu.roll(value, 1, 0) for value in turned]
        up = [pltpu.roll(value, ROWS - 1, 0) for value in turned] + [blank]
        for c in range(RING):
            tile = slice(c * ROWS, (c + 1) * ROWS)
            before = jnp.where(first, down[c], down[c + 1])
            after = jnp.where(last, up[c + 1], up[c])
            total = turned[c] + jnp.where(left, before, after)
            total += pltpu.roll(mid[c], LANES - 1, 1) * upper
            total += pltpu.roll(mid[c], 1, 1) * lower
            total += src[plane, tile, :] + src[plane + 2, tile, :]
            yield tile, total * (1.0 / 6.0) + source[plane, tile, :]

    def sweep(src, dst):
        def some(n, carry):
            for k in range(SPAN):
                plane = n * SPAN + k
                for tile, value in relaxed(src, plane):
                    dst[plane + 1, tile, :] = value
            return carry

        lax.fori_loop(0, COARSE // SPAN, some, 0)

    sweep(even, uneven)
    sweep(uneven, even)
    copies = []
    for group in range(COARSE // ROWS):
        for k in range(ROWS):
            plane = group * ROWS + k
            for tile, value in relaxed(even, plane):
                flat[plane * wide + tile.start : plane * wide + tile.stop, :] = value
        rows = slice(group * ROWS, (group + 1) * ROWS)
        for r in range(wide):
            value = flat[pl.ds(group * ROWS * wide + r, ROWS, stride=wide), :]
            result[rows, r * LANES : (r + 1) * LANES] = value
        each = pltpu.make_async_copy(result.at[rows], out_ref.at[rows], out_sem.at[group])
        each.start()
        copies.append(each)
    for each in copies:
        each.wait()
    fine_copy.wait()


def finish(base, halo_sum, grid):
    wide = COARSE // 2
    vmem = pl.BlockSpec(memory_space=pltpu.VMEM)
    hbm = pl.BlockSpec(memory_space=pl.ANY)
    dma = pltpu.SemaphoreType.DMA
    return pl.pallas_call(
        finish_kernel,
        out_shape=(
            jax.ShapeDtypeStruct(base.shape, jnp.float32),
            jax.ShapeDtypeStruct((COARSE, COARSE * COARSE), jnp.float32),
        ),
        in_specs=[vmem, vmem, vmem],
        out_specs=(hbm, hbm),
        scratch_shapes=[
            pltpu.VMEM(base.shape, jnp.float32),
            pltpu.VMEM((COARSE, wide, LANES), jnp.float32),
            pltpu.VMEM((COARSE + 2, wide, LANES), jnp.float32),
            pltpu.VMEM((COARSE + 2, wide, LANES), jnp.float32),
            pltpu.VMEM((COARSE * wide, LANES), jnp.float32),
            pltpu.VMEM((COARSE, COARSE * COARSE), jnp.float32),
            dma, dma((COARSE // ROWS,)),
        ],
        compiler_params=pltpu.CompilerParams(vmem_limit_bytes=16 << 20),
        name="finish",
    )(base, halo_sum, grid)


def body(gas_state, parcel_record, condensed_shares, surface_steam_factor, fine_cell, block_counts):
    rows = gas_state.reshape(FIELDS, PLANES, TILES, LANES).transpose(0, 2, 1, 3).reshape(-1, LANES)
    parts = halo(rows)
    parcel_next, terms, table = spray(
        parts, parcel_record, condensed_shares, surface_steam_factor, fine_cell, block_counts
    )
    base, halo_sum, grid = spread(table, fine_cell.reshape(-1, BLOCK), terms)
    fine_rows, correction = finish(base, halo_sum, grid)
    fine_source = fine_rows.reshape(FIELDS, TILES, PLANES, LANES).transpose(0, 2, 1, 3).reshape(gas_state.shape)
    return (parcel_next, fine_source, correction)


def solution(mesh):
    in_specs = (
        P(None, "slab", "cross"),
        P(None, ("slab", "cross")),
        P(None, ("slab", "cross")),
        P(),
        P(("slab", "cross")),
        P(("slab", "cross")),
    )
    out_specs = (P(None, ("slab", "cross")), P(None, "slab", "cross"), P())
    return jax.shard_map(body, mesh=mesh, in_specs=in_specs, out_specs=out_specs, check_vma=False)
```

```python
import jax
import jax.numpy as jnp
from jax import lax
from jax.experimental import pallas as pl
from jax.experimental.pallas import tpu as pltpu
from jax.sharding import PartitionSpec as P

BLOCK = 128
COARSE = 64


drag_rate = 0.5
evap_rate = 0.08
warming_speed = 0.3
latent_boiling_energy = 0.5
vapour_heat = 1.5
volume_inverse = 4.0


LINE = 16
RING = 4
LANES = 128
ROWS = 8
FIELDS = 16
PLANES = 8
TILES = 16
CHUNK = 256
PER_PLANE = 8
SHIFT = 8
UNROLL = 16
STEP = 8
PAIRS = 112
ROOM = 120
EDGES = 48
LAST = 2 * ROOM
ENDS = 3 * ROOM
EDGE_BLOCK = 4 * ROOM
EDGE_CHUNK = 5 * ROOM
EDGE_ENDS = 6 * ROOM
LAG_MINOR = 5
LAG_MAJOR = 5
SPAN = 16


def parts_of(value):
    high = value.astype(jnp.bfloat16)
    rest = value - high.astype(jnp.float32)
    middle = rest.astype(jnp.bfloat16)
    low = (rest - middle.astype(jnp.float32)).astype(jnp.bfloat16)
    return jnp.concatenate([high, middle, low], axis=0)


def joined(value):
    third = value.shape[0] // 3
    return value[:third] + (value[third : 2 * third] + value[2 * third :])


def chosen(row, cells, chunk):
    place = cells - jnp.where(chunk < 0, (PLANES + 2) * PER_PLANE, chunk) * CHUNK
    place = jnp.where((place < 0) | (place >= CHUNK), -1, place)
    place = place.astype(jnp.float32).astype(jnp.bfloat16)
    return jnp.where(row == place, jnp.bfloat16(1), jnp.bfloat16(0))


def chunk_rows():
    row = lax.broadcasted_iota(jnp.int32, (CHUNK, BLOCK), 0)
    return row.astype(jnp.float32).astype(jnp.bfloat16)


def plane_rows(tile, plane):
    return pl.ds(tile * PLANES + plane, FIELDS, stride=TILES * PLANES)


def send(src, dst, send_sem, recv_sem, device):
    return pltpu.make_async_remote_copy(
        src_ref=src, dst_ref=dst, send_sem=send_sem, recv_sem=recv_sem,
        device_id=device, device_id_type=pl.DeviceIdType.MESH,
    )


def table_kernel(cell_at, table):
    blocks = cell_at.shape[0] // BLOCK
    chunks = (PLANES + 2) * PER_PLANE
    inner = (PER_PLANE, (PLANES + 1) * PER_PLANE)
    for c in range(chunks):
        table[LAST + c] = PAIRS

    def listed(b, state):
        i, edge = state
        first = lax.shift_right_logical(cell_at[b * BLOCK], SHIFT)
        last = lax.shift_right_logical(cell_at[b * BLOCK + BLOCK - 1], SHIFT)

        def one(c, state):
            i, at = state
            table[i] = b
            table[ROOM + i] = c
            table[LAST + c] = i
            table[EDGE_BLOCK + at] = b
            table[EDGE_CHUNK + at] = c
            outer = (c < inner[0]) | (c >= inner[1])
            return i + 1, at + jnp.where(outer, 1, 0)

        i, after = lax.fori_loop(first, last + 1, one, (i, edge))
        table[ENDS + b] = i - 1
        table[EDGE_ENDS + b] = jnp.where(after > edge, after - 1, EDGES)
        return i, after

    pairs, edges = lax.fori_loop(0, blocks, listed, (0, 0))

    def blank(start):
        def one(i, carry):
            table[start + i] = 0
            table[start + ROOM + i] = -1
            return carry

        return one

    lax.fori_loop(pairs, PAIRS, blank(0), 0)
    lax.fori_loop(edges, EDGES, blank(EDGE_BLOCK), 0)


def tables(fine_cell):
    smem = pl.BlockSpec(memory_space=pltpu.SMEM)
    return pl.pallas_call(
        table_kernel,
        out_shape=jax.ShapeDtypeStruct((7 * ROOM,), jnp.int32),
        in_specs=[smem],
        out_specs=smem,
        name="tables",
    )(fine_cell)


def gather(table, start, steps, unroll, cell_ref, held, slots):
    row = chunk_rows()

    def step(n, carry):
        total, before = carry
        for k in range(unroll):
            i = n * unroll + k
            b = table[start + i]
            c = table[start + ROOM + i]
            part = jnp.dot(
                held(jnp.maximum(c, 0)), chosen(row, cell_ref[pl.ds(b, 1), :], c),
                preferred_element_type=jnp.float32,
            )
            total = joined(part) + total * jnp.where(b == before, 1.0, 0.0)
            slots[i] = total
            before = b
        return total, before

    none = jnp.zeros((FIELDS, BLOCK), jnp.float32)
    lax.fori_loop(0, steps // unroll, step, (none, -1))
    slots[steps] = none


def halo_kernel(table, cell_ref, gas_ref, inner_ref, outer_ref, parts_ref, sent, got, send_sem, recv_sem):
    slabs = 2 * RING * LINE
    slab = lax.axis_index("slab")
    cross = lax.axis_index("cross")
    below = (lax.rem(slab - 1 + slabs, slabs), cross)
    above = (lax.rem(slab + 1, slabs), cross)
    barrier = pltpu.get_barrier_semaphore()
    for device in (below, above):
        pl.semaphore_signal(barrier, inc=1, device_id=device, device_id_type=pl.DeviceIdType.MESH)
    for side, plane in ((0, 0), (1, PLANES - 1)):
        for t in range(TILES):
            sent[side, :, t * LANES : (t + 1) * LANES] = gas_ref[plane_rows(t, plane), :]
    pl.semaphore_wait(barrier, 2)
    copies = [
        send(sent.at[0], got.at[1], send_sem.at[0], recv_sem.at[1], below),
        send(sent.at[1], got.at[0], send_sem.at[1], recv_sem.at[0], above),
    ]
    for each in copies:
        each.start()
    group = CHUNK // LANES
    for p in range(PLANES):
        for q in range(PER_PLANE):
            value = [gas_ref[plane_rows(q * group + t, p), :] for t in range(group)]
            parts_ref[(p + 1) * PER_PLANE + q] = parts_of(jnp.concatenate(value, axis=1))
    none = jnp.zeros(parts_ref.shape[1:], jnp.bfloat16)
    for q in range(PER_PLANE):
        parts_ref[q] = none
        parts_ref[(PLANES + 1) * PER_PLANE + q] = none
    gather(table, 0, PAIRS, UNROLL, cell_ref, lambda c: parts_ref[c], inner_ref)
    for side in (0, 1):
        send(sent.at[0], got.at[side], send_sem.at[0], recv_sem.at[side], above).wait_recv()
        for q in range(PER_PLANE):
            outer_ref[side * PER_PLANE + q] = parts_of(got[side, :, q * CHUNK : (q + 1) * CHUNK])
    for each in copies:
        each.wait_send()


def halo(table, cells, gas_rows):
    vmem = pl.BlockSpec(memory_space=pltpu.VMEM)
    smem = pl.BlockSpec(memory_space=pltpu.SMEM)
    dma = pltpu.SemaphoreType.DMA
    chunks = (PLANES + 2) * PER_PLANE
    parts = (3 * FIELDS, CHUNK)
    return pl.pallas_call(
        halo_kernel,
        out_shape=(
            jax.ShapeDtypeStruct((PAIRS + 1, FIELDS, BLOCK), jnp.float32),
            jax.ShapeDtypeStruct((2 * PER_PLANE,) + parts, jnp.bfloat16),
        ),
        in_specs=[smem, vmem, vmem],
        out_specs=(vmem, vmem),
        scratch_shapes=[
            pltpu.VMEM((chunks,) + parts, jnp.bfloat16),
            pltpu.VMEM((2, FIELDS, TILES * LANES), jnp.float32),
            pltpu.VMEM((2, FIELDS, TILES * LANES), jnp.float32),
            dma((2,)), dma((2,)),
        ],
        compiler_params=pltpu.CompilerParams(
            collective_id=1, has_side_effects=True, vmem_limit_bytes=16 << 20
        ),
        name="halo",
    )(table, cells, gas_rows)


def advance(table, count_at, steam_ref, inner_ref, outer_ref, record_ref, shares_ref, cell_ref, next_ref, terms, slots):
    def held(c):
        return outer_ref[jnp.where(c < PER_PLANE, c, jnp.maximum(c - PLANES * PER_PLANE, 0))]

    blocks = cell_ref.shape[0]
    gather(table, EDGE_BLOCK, EDGES, UNROLL, cell_ref, held, slots)
    lane = lax.broadcasted_iota(jnp.int32, (1, BLOCK), 1)
    species = lax.broadcasted_iota(jnp.int32, (steam_ref.shape[0], BLOCK), 0)
    steam = jnp.zeros(species.shape, jnp.float32)
    for k in range(steam_ref.shape[0]):
        steam = jnp.where(species == k, steam_ref[k], steam)

    def step(n, carry):
        for k in range(STEP):
            b = n * STEP + k
            cols = pl.ds(pl.multiple_of(b * BLOCK, BLOCK), BLOCK)
            gas = inner_ref[table[ENDS + b]] + slots[table[EDGE_ENDS + b]]
            record = record_ref[:, cols]
            alive = lane < count_at[b]
            gas_velocity, gas_heat, vapour = gas[0:3], gas[3:4], gas[4:]
            velocity, heat, weight = record[0:3], record[3:4], record[4:5]
            slip = gas_velocity - velocity
            slip = slip * slip
            slip = slip[0:1] + slip[1:2] + slip[2:3]
            log_weight = jnp.log(weight)
            factor = drag_rate * jnp.exp(log_weight * (-2.0 / 3.0))
            factor = factor * (1.0 + 0.15 * jnp.exp(0.3435 * jnp.log(slip + 1.0)))
            moved = (velocity + factor * gas_velocity) / (1.0 + factor)
            surface = shares_ref[:, cols] * steam * jnp.exp(2.0 * (heat - 0.75))
            rates = evap_rate * weight * (surface - vapour)
            lost = jnp.sum(rates, axis=0, keepdims=True)
            exchange = warming_speed * (gas_heat - heat) * jnp.exp(log_weight * (1.0 / 3.0))
            warmed = heat + (exchange - latent_boiling_energy * lost) / weight
            scale = jnp.where(alive, volume_inverse, 0.0)
            terms[b, 0:3] = (weight * (velocity - moved) + lost * moved) * scale
            terms[b, 3:4] = (vapour_heat * lost - exchange) * scale
            terms[b, 4:16] = rates * scale
            next_ref[0:3, cols] = jnp.where(alive, moved, velocity)
            next_ref[3:4, cols] = jnp.where(alive, warmed, heat)
            next_ref[4:5, cols] = jnp.where(alive, weight - lost, weight)
        return carry

    lax.fori_loop(0, blocks // STEP, step, 0)


def scatter(table, cell_ref, terms_ref, base_ref, edge, slots):
    row = chunk_rows()

    def step(n, carry):
        total, before = carry
        for k in range(UNROLL):
            i = n * UNROLL + k
            b = table[i]
            c = table[ROOM + i]
            picked = chosen(row, cell_ref[pl.ds(b, 1), :], c)
            part = lax.dot_general(
                parts_of(terms_ref[b]), picked, (((1,), (1,)), ((), ())),
                preferred_element_type=jnp.float32,
            )
            total = joined(part) + total * jnp.where(c == before, 1.0, 0.0)
            slots[i] = total
            before = c
        return total, before

    none = jnp.zeros((FIELDS, CHUNK), jnp.float32)
    lax.fori_loop(0, PAIRS // UNROLL, step, (none, -2))
    slots[PAIRS] = none

    fold_row = lax.broadcasted_iota(jnp.int32, (CHUNK, LANES), 0)
    fold_lane = lax.broadcasted_iota(jnp.int32, (CHUNK, LANES), 1)
    fold = jnp.where(lax.shift_right_logical(fold_row, 1) == fold_lane, 1.0, 0.0).astype(jnp.bfloat16)

    def mass(value):
        kept = jnp.sum(value[4:], axis=0, keepdims=True)
        return [joined(jnp.dot(parts_of(kept), fold, preferred_element_type=jnp.float32))]

    own, low, high = [], [], []
    group = CHUNK // LANES
    for q in range(PER_PLANE):
        cols = slice(q * CHUNK, (q + 1) * CHUNK)
        below = slots[table[2 * ROOM + q]]
        above = slots[table[2 * ROOM + (PLANES + 1) * PER_PLANE + q]]
        edge[0, :, cols] = below
        edge[1, :, cols] = above
        inside = None
        for p in range(PLANES):
            value = slots[table[2 * ROOM + (p + 1) * PER_PLANE + q]]
            for t in range(group):
                base_ref[plane_rows(q * group + t, p), :] = value[:, t * LANES : (t + 1) * LANES]
            inside = value if inside is None else inside + value
        own += mass(inside)
        low += mass(below)
        high += mass(above)
    return tuple(0.25 * jnp.concatenate(rows, axis=0) for rows in (own, low, high))


def spread_kernel(
    table, count_at, steam_ref, inner_ref, parts_ref, record_ref, shares_ref, cell_ref,
    next_ref, base_ref, halo_ref, grid_ref, own_ref, outer_ref, edge_ref, terms, edge_slots, slots, got,
    pair_send, pair_recv, edge_send, edge_recv, line_send, line_recv,
    minor_send, minor_recv, major_send, major_recv, core_send, core_recv,
):
    slabs = 2 * RING * LINE
    slab = lax.axis_index("slab")
    cross = lax.axis_index("cross")
    core = lax.rem(cross, 2)
    z = lax.rem(slab, LINE)
    x = lax.rem(lax.div(slab, LINE), RING)
    y = lax.div(cross, 2) * 2 + lax.div(slab, RING * LINE)
    odd = lax.rem(slab, 2)
    sign = 2 * odd - 1
    pair = lax.div(slab, 2)
    line_pair = lax.div(z, 2)
    major = core * x + (1 - core) * y
    minor = core * y + (1 - core) * x

    def near(by):
        return (lax.rem(slab + by + slabs, slabs), cross)

    def place(at_x, at_y, at_z):
        return (lax.rem(at_y, 2) * (RING * LINE) + at_x * LINE + at_z, lax.div(at_y, 2) * 2 + core)

    def in_line(by):
        return lax.rem(z + by + LINE, LINE)

    def minor_peer(other):
        return place(core * x + (1 - core) * other, core * other + (1 - core) * y, z)

    def major_peer(other):
        return place(core * other + (1 - core) * x, core * y + (1 - core) * other, z)

    def turn(own, by):
        return lax.rem(own + by, RING)

    copy = send

    other_core = (slab, cross + 1 - 2 * core)
    line_from = [sign * k for k in (1, 3, 5, 7)] + [-sign * k for k in (2, 4, 6)]
    low = lax.rem(2 * pair - 1 + slabs, slabs)
    high = lax.rem(2 * pair + 2, slabs)

    barrier = pltpu.get_barrier_semaphore()
    sources = [near(-sign), (low, cross), (high, cross), near(-1), near(1)]
    sources += [place(x, y, in_line(by)) for by in line_from]
    sources += [minor_peer(turn(minor, by)) for by in (1, 2, 3)]
    sources += [major_peer(turn(major, by)) for by in (1, 2, 3)]
    sources += [other_core]
    for device in sources:
        pl.semaphore_signal(barrier, inc=1, device_id=device, device_id_type=pl.DeviceIdType.MESH)
    advance(
        table, count_at, steam_ref, inner_ref, parts_ref, record_ref, shares_ref, cell_ref,
        next_ref, terms, edge_slots,
    )
    own, low_tile, high_tile = scatter(table, cell_ref, terms, base_ref, edge_ref, slots)
    own_ref[...] = own + jnp.where(odd == 1, low_tile, high_tile)
    outer_ref[...] = jnp.where(odd == 1, high_tile, low_tile)
    pl.semaphore_wait(barrier, len(sources))

    copies = [
        copy(own_ref, got.at[0], pair_send.at[0], pair_recv.at[0], near(-sign)),
        copy(outer_ref, got.at[2 - odd], pair_send.at[1], pair_recv.at[2 - odd], near(sign)),
        copy(outer_ref, got.at[2 - odd], pair_send.at[2], pair_recv.at[2 - odd], near(2 * sign)),
    ]
    for each in copies:
        each.start()
    for slot in range(3):
        copy(own_ref, got.at[slot], pair_send.at[slot], pair_recv.at[slot], near(1)).wait_recv()
    grid_ref[core, major, minor, line_pair] = (own_ref[...] + got[0]) + (got[1] + got[2])
    edges = [
        copy(edge_ref.at[0], halo_ref.at[1], edge_send.at[0], edge_recv.at[1], near(-1)),
        copy(edge_ref.at[1], halo_ref.at[0], edge_send.at[1], edge_recv.at[0], near(1)),
    ]
    tile = grid_ref.at[core, major, minor, line_pair]
    for k in range(1, 8):
        each = copy(tile, tile, line_send.at[k - 1], line_recv.at[line_pair], place(x, y, in_line(sign * k)))
        each.start()
        copies.append(each)
    tiles = [line_pair] + [lax.div(in_line(sign * k if k % 2 else -sign * k), 2) for k in range(1, 8)]

    def go(src, dst, send_sem, recv_sem, device):
        each = copy(src, dst, send_sem, recv_sem, device)
        each.start()
        copies.append(each)

    def to_minors(k):
        t = tiles[k]
        src = grid_ref.at[core, major, minor, t]
        if k:
            copy(src, src, line_send.at[0], line_recv.at[t], near(1)).wait_recv()
        for by in (1, 2, 3):
            go(src, src, minor_send.at[by - 1, k], minor_recv.at[minor, t], minor_peer(turn(minor, by)))

    def to_majors(k):
        t = tiles[k]
        for by in (1, 2, 3):
            src = grid_ref.at[core, major, turn(minor, by), t]
            copy(src, src, minor_send.at[0, k], minor_recv.at[turn(minor, by), t], near(1)).wait_recv()
        src = grid_ref.at[core, major, :, t]
        for by in (1, 2, 3):
            go(src, src, major_send.at[by - 1, k], major_recv.at[major, t], major_peer(turn(major, by)))
        go(src, src, core_send.at[0, k], core_recv.at[major, t], other_core)

    def to_core(k):
        t = tiles[k]
        for by in (1, 2, 3):
            src = grid_ref.at[core, turn(major, by), :, t]
            copy(src, src, major_send.at[0, k], major_recv.at[turn(major, by), t], near(1)).wait_recv()
            go(src, src, core_send.at[by, k], core_recv.at[turn(major, by), t], other_core)

    for step in range(8 + LAG_MINOR + LAG_MAJOR):
        if step < 8:
            to_minors(step)
        if step == 0:
            for each in edges:
                each.start()
        if 0 <= step - LAG_MINOR < 8:
            to_majors(step - LAG_MINOR)
        if 0 <= step - LAG_MINOR - LAG_MAJOR < 8:
            to_core(step - LAG_MINOR - LAG_MAJOR)
    for by in range(RING):
        for k in range(8):
            src = grid_ref.at[1 - core, by, :, k]
            copy(src, src, core_send.at[0, k], core_recv.at[by, k], other_core).wait_recv()
    for slot in range(2):
        copy(edge_ref.at[0], halo_ref.at[slot], edge_send.at[0], edge_recv.at[slot], near(1)).wait_recv()
    for each in copies + edges:
        each.wait_send()


def spread(table, block_counts, steam, inner, parts, record, shares, cells):
    dma = pltpu.SemaphoreType.DMA
    vmem = pl.BlockSpec(memory_space=pltpu.VMEM)
    smem = pl.BlockSpec(memory_space=pltpu.SMEM)
    side = (2, FIELDS, TILES * LANES)
    return pl.pallas_call(
        spread_kernel,
        out_shape=(
            jax.ShapeDtypeStruct(record.shape, jnp.float32),
            jax.ShapeDtypeStruct((FIELDS * TILES * PLANES, LANES), jnp.float32),
            jax.ShapeDtypeStruct(side, jnp.float32),
            jax.ShapeDtypeStruct((2, RING, RING, LINE // 2, ROWS, LANES), jnp.float32),
        ),
        in_specs=[smem] * 3 + [vmem] * 5,
        out_specs=(vmem,) * 4,
        scratch_shapes=[
            pltpu.VMEM((ROWS, LANES), jnp.float32),
            pltpu.VMEM((ROWS, LANES), jnp.float32),
            pltpu.VMEM(side, jnp.float32),
            pltpu.VMEM((cells.shape[0], FIELDS, BLOCK), jnp.float32),
            pltpu.VMEM((EDGES + 1, FIELDS, BLOCK), jnp.float32),
            pltpu.VMEM((PAIRS + 1, FIELDS, CHUNK), jnp.float32),
            pltpu.VMEM((3, ROWS, LANES), jnp.float32),
            dma((3,)), dma((3,)), dma((2,)), dma((2,)), dma((7,)), dma((LINE // 2,)),
            dma((3, 8)), dma((RING, 8)), dma((3, 8)), dma((RING, 8)), dma((RING, 8)), dma((RING, 8)),
        ],
        compiler_params=pltpu.CompilerParams(
            collective_id=0, has_side_effects=True, vmem_limit_bytes=16 << 20
        ),
        name="spread",
    )(table, block_counts, steam, inner, parts, record, shares, cells)


def finish_kernel(moved_ref, base_ref, halo_ref, grid_ref, next_ref, fine_ref, out_ref, fine, source, even, uneven, flat, result, fine_sem, out_sem):
    next_ref[...] = moved_ref[...]
    sub = lax.broadcasted_iota(jnp.int32, (ROWS, LANES), 0)
    lane = lax.broadcasted_iota(jnp.int32, (ROWS, LANES), 1)
    first = sub == 0
    last = sub == ROWS - 1
    for f in range(FIELDS):
        for t in range(TILES):
            cols = slice(t * LANES, (t + 1) * LANES)
            rows = slice((f * TILES + t) * PLANES, (f * TILES + t + 1) * PLANES)
            low = jnp.broadcast_to(halo_ref[0, f : f + 1, cols], (PLANES, LANES))
            high = jnp.broadcast_to(halo_ref[1, f : f + 1, cols], (PLANES, LANES))
            fine[rows, :] = base_ref[rows, :] + jnp.where(first, low, jnp.where(last, high, 0.0))
    fine_copy = pltpu.make_async_copy(fine, fine_ref, fine_sem)
    fine_copy.start()

    wide = COARSE // 2
    none = jnp.zeros((wide, LANES), jnp.float32)
    for held in (even, uneven):
        held[0] = none
        held[COARSE + 1] = none
    for plane in range(COARSE):
        y_lo, x, j = plane // 32, (plane // 8) % RING, plane % 8
        for c in range(RING):
            y = (c // 2) * 2 + y_lo
            at = grid_ref[0, y, x, j] if c % 2 == 0 else grid_ref[1, x, y, j]
            value = at * (1.0 / 6.0)
            source[plane, c * ROWS : (c + 1) * ROWS, :] = value
            even[plane + 1, c * ROWS : (c + 1) * ROWS, :] = value

    half = LANES // 2
    depth = lax.rem(lane, half)
    upper = jnp.where(depth < half - 1, 1.0, 0.0)
    lower = jnp.where(depth > 0, 1.0, 0.0)
    left = lane < half
    blank = jnp.zeros((ROWS, LANES), jnp.float32)

    def relaxed(src, plane):
        mid = [src[plane + 1, c * ROWS : (c + 1) * ROWS, :] for c in range(RING)]
        turned = [pltpu.roll(value, half, 1) for value in mid]
        down = [blank] + [pltpu.roll(value, 1, 0) for value in turned]
        up = [pltpu.roll(value, ROWS - 1, 0) for value in turned] + [blank]
        for c in range(RING):
            tile = slice(c * ROWS, (c + 1) * ROWS)
            before = jnp.where(first, down[c], down[c + 1])
            after = jnp.where(last, up[c + 1], up[c])
            total = turned[c] + jnp.where(left, before, after)
            total += pltpu.roll(mid[c], LANES - 1, 1) * upper
            total += pltpu.roll(mid[c], 1, 1) * lower
            total += src[plane, tile, :] + src[plane + 2, tile, :]
            yield tile, total * (1.0 / 6.0) + source[plane, tile, :]

    def sweep(src, dst):
        def some(n, carry):
            for k in range(SPAN):
                plane = n * SPAN + k
                for tile, value in relaxed(src, plane):
                    dst[plane + 1, tile, :] = value
            return carry

        lax.fori_loop(0, COARSE // SPAN, some, 0)

    sweep(even, uneven)
    sweep(uneven, even)
    copies = []
    for group in range(COARSE // ROWS):
        for k in range(ROWS):
            plane = group * ROWS + k
            for tile, value in relaxed(even, plane):
                flat[plane * wide + tile.start : plane * wide + tile.stop, :] = value
        rows = slice(group * ROWS, (group + 1) * ROWS)
        for r in range(wide):
            value = flat[pl.ds(group * ROWS * wide + r, ROWS, stride=wide), :]
            result[rows, r * LANES : (r + 1) * LANES] = value
        each = pltpu.make_async_copy(result.at[rows], out_ref.at[rows], out_sem.at[group])
        each.start()
        copies.append(each)
    for each in copies:
        each.wait()
    fine_copy.wait()


def finish(moved, base, halo_sum, grid):
    wide = COARSE // 2
    vmem = pl.BlockSpec(memory_space=pltpu.VMEM)
    hbm = pl.BlockSpec(memory_space=pl.ANY)
    dma = pltpu.SemaphoreType.DMA
    return pl.pallas_call(
        finish_kernel,
        out_shape=(
            jax.ShapeDtypeStruct(moved.shape, jnp.float32),
            jax.ShapeDtypeStruct(base.shape, jnp.float32),
            jax.ShapeDtypeStruct((COARSE, COARSE * COARSE), jnp.float32),
        ),
        in_specs=[vmem] * 4,
        out_specs=(vmem, hbm, hbm),
        scratch_shapes=[
            pltpu.VMEM(base.shape, jnp.float32),
            pltpu.VMEM((COARSE, wide, LANES), jnp.float32),
            pltpu.VMEM((COARSE + 2, wide, LANES), jnp.float32),
            pltpu.VMEM((COARSE + 2, wide, LANES), jnp.float32),
            pltpu.VMEM((COARSE * wide, LANES), jnp.float32),
            pltpu.VMEM((COARSE, COARSE * COARSE), jnp.float32),
            dma, dma((COARSE // ROWS,)),
        ],
        compiler_params=pltpu.CompilerParams(vmem_limit_bytes=16 << 20),
        name="finish",
    )(moved, base, halo_sum, grid)


def body(gas_state, parcel_record, condensed_shares, surface_steam_factor, fine_cell, block_counts):
    rows = gas_state.reshape(FIELDS, PLANES, TILES, LANES).transpose(0, 2, 1, 3).reshape(-1, LANES)
    cells = fine_cell.reshape(-1, BLOCK)
    table = tables(fine_cell)
    inner, outer = halo(table, cells, rows)
    moved, base, halo_sum, grid = spread(
        table, block_counts, surface_steam_factor, inner, outer, parcel_record, condensed_shares, cells
    )
    parcel_next, fine_rows, correction = finish(moved, base, halo_sum, grid)
    fine_source = fine_rows.reshape(FIELDS, TILES, PLANES, LANES).transpose(0, 2, 1, 3).reshape(gas_state.shape)
    return (parcel_next, fine_source, correction)


def solution(mesh):
    in_specs = (
        P(None, "slab", "cross"),
        P(None, ("slab", "cross")),
        P(None, ("slab", "cross")),
        P(),
        P(("slab", "cross")),
        P(("slab", "cross")),
    )
    out_specs = (P(None, ("slab", "cross")), P(None, "slab", "cross"), P())
    return jax.shard_map(body, mesh=mesh, in_specs=in_specs, out_specs=out_specs, check_vma=False)
```

```python
import jax
import jax.numpy as jnp
from jax import lax
from jax.experimental import pallas as pl
from jax.experimental.pallas import tpu as pltpu
from jax.sharding import PartitionSpec as P

BLOCK = 128
COARSE = 64


drag_rate = 0.5
evap_rate = 0.08
warming_speed = 0.3
latent_boiling_energy = 0.5
vapour_heat = 1.5
volume_inverse = 4.0


LINE = 16
RING = 4
LANES = 128
ROWS = 8
FIELDS = 16
PLANES = 8
TILES = 16
CHUNK = 256
PER_PLANE = 8
SHIFT = 8
UNROLL = 16
STEP = 8
PAIRS = 112
EDGES = 48
LAST = 2
ENDS = 3
EDGE_BLOCK = 4
EDGE_ENDS = 6
LAG_MINOR = 5
LAG_MAJOR = 5
SPAN = 16


def parts_of(value):
    high = value.astype(jnp.bfloat16)
    rest = value - high.astype(jnp.float32)
    middle = rest.astype(jnp.bfloat16)
    low = (rest - middle.astype(jnp.float32)).astype(jnp.bfloat16)
    return jnp.concatenate([high, middle, low], axis=0)


def joined(value):
    third = value.shape[0] // 3
    return value[:third] + (value[third : 2 * third] + value[2 * third :])


def chosen(row, cells, chunk):
    place = cells - jnp.where(chunk < 0, (PLANES + 2) * PER_PLANE, chunk) * CHUNK
    place = jnp.where((place < 0) | (place >= CHUNK), -1, place)
    place = place.astype(jnp.float32).astype(jnp.bfloat16)
    return jnp.where(row == place, jnp.bfloat16(1), jnp.bfloat16(0))


def chunk_rows():
    row = lax.broadcasted_iota(jnp.int32, (CHUNK, BLOCK), 0)
    return row.astype(jnp.float32).astype(jnp.bfloat16)


def within(value, top):
    return jnp.minimum(jnp.maximum(value, 0), top)


def plane_rows(tile, plane):
    return pl.ds(tile * PLANES + plane, FIELDS, stride=TILES * PLANES)


def send(src, dst, send_sem, recv_sem, device):
    return pltpu.make_async_remote_copy(
        src_ref=src, dst_ref=dst, send_sem=send_sem, recv_sem=recv_sem,
        device_id=device, device_id_type=pl.DeviceIdType.MESH,
    )


def list_pairs(cell_ref, table):
    blocks = cell_ref.shape[0]
    chunks = (PLANES + 2) * PER_PLANE
    first = lax.shift_right_logical(cell_ref[:, 0:1], SHIFT).astype(jnp.float32)
    last = lax.shift_right_logical(cell_ref[:, BLOCK - 1 : BLOCK], SHIFT).astype(jnp.float32)
    lane = lax.broadcasted_iota(jnp.int32, (blocks, LANES), 1).astype(jnp.float32)
    sub = lax.broadcasted_iota(jnp.int32, (blocks, LANES), 0).astype(jnp.float32)
    spot = lane[0:1]

    def over_blocks(value):
        return jnp.sum(value, axis=0, keepdims=True)

    def as_row(column):
        return over_blocks(jnp.where(sub == lane, column, 0.0))

    def starts(column):
        return jnp.sum(jnp.where(lane < sub, as_row(column), 0.0), axis=1, keepdims=True)

    def owner(start):
        return over_blocks(jnp.where(start <= lane, 1.0, 0.0)) - 1.0

    def at(block, column):
        return over_blocks(jnp.where(sub == block, column, 0.0))

    def put(row, value, low, high):
        table[row : row + 1, :] = jnp.clip(value.astype(jnp.int32), low, high)

    count = last - first + 1.0
    start = starts(count)
    block = owner(start)
    real = spot < over_blocks(count)
    put(0, jnp.where(real, block, 0.0), 0, blocks - 1)
    put(1, jnp.where(real, spot + at(block, first - start), -1.0), -1, chunks - 1)
    deep = owner(first)
    held = (deep >= 0.0) & (at(deep, last) >= spot)
    put(LAST, jnp.where(held, spot + at(deep, start - first), float(PAIRS)), 0, PAIRS)
    put(ENDS, as_row(start + count - 1.0), 0, PAIRS)

    top = float((PLANES + 1) * PER_PLANE)
    low = jnp.maximum(jnp.minimum(last, PER_PLANE - 1.0) - first + 1.0, 0.0)
    from_high = jnp.maximum(first, top)
    edges = low + jnp.maximum(last - from_high + 1.0, 0.0)
    start = starts(edges)
    block = owner(start)
    real = spot < over_blocks(edges)
    inside = spot - at(block, start)
    kept = at(block, low)
    chunk = jnp.where(inside < kept, at(block, first) + inside, at(block, from_high) + inside - kept)
    put(EDGE_BLOCK, jnp.where(real, block, 0.0), 0, blocks - 1)
    put(EDGE_BLOCK + 1, jnp.where(real, chunk, -1.0), -1, chunks - 1)
    put(EDGE_ENDS, as_row(jnp.where(edges > 0.0, start + edges - 1.0, float(EDGES))), 0, EDGES)


def gather(table, start, steps, unroll, cell_ref, held, slots):
    row = chunk_rows()

    def step(n, carry):
        total, before = carry
        for k in range(unroll):
            i = n * unroll + k
            b = within(table[start, i], cell_ref.shape[0] - 1)
            c = table[start + 1, i]
            part = jnp.dot(
                held(within(c, (PLANES + 2) * PER_PLANE - 1)), chosen(row, cell_ref[pl.ds(b, 1), :], c),
                preferred_element_type=jnp.float32,
            )
            total = joined(part) + total * jnp.where(b == before, 1.0, 0.0)
            slots[i] = total
            before = b
        return total, before

    none = jnp.zeros((FIELDS, BLOCK), jnp.float32)
    lax.fori_loop(0, steps // unroll, step, (none, -1))
    slots[steps] = none


def halo_kernel(
    cell_ref, gas_ref, inner_ref, outer_ref, table_ref, parts_ref, sent, got, table, table_sem, send_sem, recv_sem
):
    slabs = 2 * RING * LINE
    slab = lax.axis_index("slab")
    cross = lax.axis_index("cross")
    below = (lax.rem(slab - 1 + slabs, slabs), cross)
    above = (lax.rem(slab + 1, slabs), cross)
    barrier = pltpu.get_barrier_semaphore()
    for device in (below, above):
        pl.semaphore_signal(barrier, inc=1, device_id=device, device_id_type=pl.DeviceIdType.MESH)
    list_pairs(cell_ref, table_ref)
    table_ref[ROWS - 1 :, :] = jnp.zeros((1, LANES), jnp.int32)
    for side, plane in ((0, 0), (1, PLANES - 1)):
        for t in range(TILES):
            sent[side, :, t * LANES : (t + 1) * LANES] = gas_ref[plane_rows(t, plane), :]
    pl.semaphore_wait(barrier, 2)
    table_copy = pltpu.make_async_copy(table_ref, table, table_sem)
    copies = [
        send(sent.at[0], got.at[1], send_sem.at[0], recv_sem.at[1], below),
        send(sent.at[1], got.at[0], send_sem.at[1], recv_sem.at[0], above),
    ]
    for each in copies:
        each.start()
    table_copy.start()
    group = CHUNK // LANES
    for p in range(PLANES):
        for q in range(PER_PLANE):
            value = [gas_ref[plane_rows(q * group + t, p), :] for t in range(group)]
            parts_ref[(p + 1) * PER_PLANE + q] = parts_of(jnp.concatenate(value, axis=1))
    none = jnp.zeros(parts_ref.shape[1:], jnp.bfloat16)
    for q in range(PER_PLANE):
        parts_ref[q] = none
        parts_ref[(PLANES + 1) * PER_PLANE + q] = none
    table_copy.wait()
    gather(table, 0, PAIRS, UNROLL, cell_ref, lambda c: parts_ref[c], inner_ref)
    for side in (0, 1):
        send(sent.at[0], got.at[side], send_sem.at[0], recv_sem.at[side], above).wait_recv()
        for q in range(PER_PLANE):
            outer_ref[side * PER_PLANE + q] = parts_of(got[side, :, q * CHUNK : (q + 1) * CHUNK])
    for each in copies:
        each.wait_send()


def halo(cells, gas_rows):
    vmem = pl.BlockSpec(memory_space=pltpu.VMEM)
    dma = pltpu.SemaphoreType.DMA
    chunks = (PLANES + 2) * PER_PLANE
    parts = (3 * FIELDS, CHUNK)
    return pl.pallas_call(
        halo_kernel,
        out_shape=(
            jax.ShapeDtypeStruct((PAIRS + 1, FIELDS, BLOCK), jnp.float32),
            jax.ShapeDtypeStruct((2 * PER_PLANE,) + parts, jnp.bfloat16),
            jax.ShapeDtypeStruct((ROWS, LANES), jnp.int32),
        ),
        in_specs=[vmem, vmem],
        out_specs=(vmem, vmem, vmem),
        scratch_shapes=[
            pltpu.VMEM((chunks,) + parts, jnp.bfloat16),
            pltpu.VMEM((2, FIELDS, TILES * LANES), jnp.float32),
            pltpu.VMEM((2, FIELDS, TILES * LANES), jnp.float32),
            pltpu.SMEM((ROWS, LANES), jnp.int32),
            dma, dma((2,)), dma((2,)),
        ],
        compiler_params=pltpu.CompilerParams(
            collective_id=1, has_side_effects=True, vmem_limit_bytes=16 << 20
        ),
        name="halo",
    )(cells, gas_rows)


def advance(table, count_at, steam_ref, inner_ref, outer_ref, record_ref, shares_ref, cell_ref, next_ref, terms, slots):
    def held(c):
        return outer_ref[within(jnp.where(c < PER_PLANE, c, c - PLANES * PER_PLANE), 2 * PER_PLANE - 1)]

    blocks = cell_ref.shape[0]
    gather(table, EDGE_BLOCK, EDGES, UNROLL, cell_ref, held, slots)
    lane = lax.broadcasted_iota(jnp.int32, (1, BLOCK), 1)
    species = lax.broadcasted_iota(jnp.int32, (steam_ref.shape[0], BLOCK), 0)
    steam = jnp.zeros(species.shape, jnp.float32)
    for k in range(steam_ref.shape[0]):
        steam = jnp.where(species == k, steam_ref[k], steam)

    def step(n, carry):
        for k in range(STEP):
            b = n * STEP + k
            cols = pl.ds(pl.multiple_of(b * BLOCK, BLOCK), BLOCK)
            gas = inner_ref[within(table[ENDS, b], PAIRS)] + slots[within(table[EDGE_ENDS, b], EDGES)]
            record = record_ref[:, cols]
            alive = lane < count_at[b]
            gas_velocity, gas_heat, vapour = gas[0:3], gas[3:4], gas[4:]
            velocity, heat, weight = record[0:3], record[3:4], record[4:5]
            slip = gas_velocity - velocity
            slip = slip * slip
            slip = slip[0:1] + slip[1:2] + slip[2:3]
            log_weight = jnp.log(weight)
            factor = drag_rate * jnp.exp(log_weight * (-2.0 / 3.0))
            factor = factor * (1.0 + 0.15 * jnp.exp(0.3435 * jnp.log(slip + 1.0)))
            moved = (velocity + factor * gas_velocity) / (1.0 + factor)
            surface = shares_ref[:, cols] * steam * jnp.exp(2.0 * (heat - 0.75))
            rates = evap_rate * weight * (surface - vapour)
            lost = jnp.sum(rates, axis=0, keepdims=True)
            exchange = warming_speed * (gas_heat - heat) * jnp.exp(log_weight * (1.0 / 3.0))
            warmed = heat + (exchange - latent_boiling_energy * lost) / weight
            scale = jnp.where(alive, volume_inverse, 0.0)
            terms[b, 0:3] = (weight * (velocity - moved) + lost * moved) * scale
            terms[b, 3:4] = (vapour_heat * lost - exchange) * scale
            terms[b, 4:16] = rates * scale
            next_ref[0:3, cols] = jnp.where(alive, moved, velocity)
            next_ref[3:4, cols] = jnp.where(alive, warmed, heat)
            next_ref[4:5, cols] = jnp.where(alive, weight - lost, weight)
        return carry

    lax.fori_loop(0, blocks // STEP, step, 0)


def scatter(table, cell_ref, terms_ref, base_ref, edge, slots):
    row = chunk_rows()

    def step(n, carry):
        total, before = carry
        for k in range(UNROLL):
            i = n * UNROLL + k
            b = within(table[0, i], cell_ref.shape[0] - 1)
            c = table[1, i]
            picked = chosen(row, cell_ref[pl.ds(b, 1), :], c)
            part = lax.dot_general(
                parts_of(terms_ref[b]), picked, (((1,), (1,)), ((), ())),
                preferred_element_type=jnp.float32,
            )
            total = joined(part) + total * jnp.where(c == before, 1.0, 0.0)
            slots[i] = total
            before = c
        return total, before

    none = jnp.zeros((FIELDS, CHUNK), jnp.float32)
    lax.fori_loop(0, PAIRS // UNROLL, step, (none, -2))
    slots[PAIRS] = none

    fold_row = lax.broadcasted_iota(jnp.int32, (CHUNK, LANES), 0)
    fold_lane = lax.broadcasted_iota(jnp.int32, (CHUNK, LANES), 1)
    fold = jnp.where(lax.shift_right_logical(fold_row, 1) == fold_lane, 1.0, 0.0).astype(jnp.bfloat16)

    def mass(value):
        kept = jnp.sum(value[4:], axis=0, keepdims=True)
        return [joined(jnp.dot(parts_of(kept), fold, preferred_element_type=jnp.float32))]

    own, low, high = [], [], []
    group = CHUNK // LANES
    for q in range(PER_PLANE):
        cols = slice(q * CHUNK, (q + 1) * CHUNK)
        below = slots[within(table[LAST, q], PAIRS)]
        above = slots[within(table[LAST, (PLANES + 1) * PER_PLANE + q], PAIRS)]
        edge[0, :, cols] = below
        edge[1, :, cols] = above
        inside = None
        for p in range(PLANES):
            value = slots[within(table[LAST, (p + 1) * PER_PLANE + q], PAIRS)]
            for t in range(group):
                base_ref[plane_rows(q * group + t, p), :] = value[:, t * LANES : (t + 1) * LANES]
            inside = value if inside is None else inside + value
        own += mass(inside)
        low += mass(below)
        high += mass(above)
    return tuple(0.25 * jnp.concatenate(rows, axis=0) for rows in (own, low, high))


def spread_kernel(
    table, count_at, steam_ref, inner_ref, parts_ref, record_ref, shares_ref, cell_ref,
    next_ref, base_ref, halo_ref, grid_ref, own_ref, outer_ref, edge_ref, terms, edge_slots, slots, got,
    pair_send, pair_recv, edge_send, edge_recv, line_send, line_recv,
    minor_send, minor_recv, major_send, major_recv, core_send, core_recv,
):
    slabs = 2 * RING * LINE
    slab = lax.axis_index("slab")
    cross = lax.axis_index("cross")
    core = lax.rem(cross, 2)
    z = lax.rem(slab, LINE)
    x = lax.rem(lax.div(slab, LINE), RING)
    y = lax.div(cross, 2) * 2 + lax.div(slab, RING * LINE)
    odd = lax.rem(slab, 2)
    sign = 2 * odd - 1
    pair = lax.div(slab, 2)
    line_pair = lax.div(z, 2)
    major = core * x + (1 - core) * y
    minor = core * y + (1 - core) * x

    def near(by):
        return (lax.rem(slab + by + slabs, slabs), cross)

    def place(at_x, at_y, at_z):
        return (lax.rem(at_y, 2) * (RING * LINE) + at_x * LINE + at_z, lax.div(at_y, 2) * 2 + core)

    def in_line(by):
        return lax.rem(z + by + LINE, LINE)

    def minor_peer(other):
        return place(core * x + (1 - core) * other, core * other + (1 - core) * y, z)

    def major_peer(other):
        return place(core * other + (1 - core) * x, core * y + (1 - core) * other, z)

    def turn(own, by):
        return lax.rem(own + by, RING)

    copy = send

    other_core = (slab, cross + 1 - 2 * core)
    line_from = [sign * k for k in (1, 3, 5, 7)] + [-sign * k for k in (2, 4, 6)]
    low = lax.rem(2 * pair - 1 + slabs, slabs)
    high = lax.rem(2 * pair + 2, slabs)

    barrier = pltpu.get_barrier_semaphore()
    sources = [near(-sign), (low, cross), (high, cross), near(-1), near(1)]
    sources += [place(x, y, in_line(by)) for by in line_from]
    sources += [minor_peer(turn(minor, by)) for by in (1, 2, 3)]
    sources += [major_peer(turn(major, by)) for by in (1, 2, 3)]
    sources += [other_core]
    for device in sources:
        pl.semaphore_signal(barrier, inc=1, device_id=device, device_id_type=pl.DeviceIdType.MESH)
    advance(
        table, count_at, steam_ref, inner_ref, parts_ref, record_ref, shares_ref, cell_ref,
        next_ref, terms, edge_slots,
    )
    own, low_tile, high_tile = scatter(table, cell_ref, terms, base_ref, edge_ref, slots)
    own_ref[...] = own + jnp.where(odd == 1, low_tile, high_tile)
    outer_ref[...] = jnp.where(odd == 1, high_tile, low_tile)
    pl.semaphore_wait(barrier, len(sources))

    copies = [
        copy(own_ref, got.at[0], pair_send.at[0], pair_recv.at[0], near(-sign)),
        copy(outer_ref, got.at[2 - odd], pair_send.at[1], pair_recv.at[2 - odd], near(sign)),
        copy(outer_ref, got.at[2 - odd], pair_send.at[2], pair_recv.at[2 - odd], near(2 * sign)),
    ]
    for each in copies:
        each.start()
    for slot in range(3):
        copy(own_ref, got.at[slot], pair_send.at[slot], pair_recv.at[slot], near(1)).wait_recv()
    grid_ref[core, major, minor, line_pair] = (own_ref[...] + got[0]) + (got[1] + got[2])
    edges = [
        copy(edge_ref.at[0], halo_ref.at[1], edge_send.at[0], edge_recv.at[1], near(-1)),
        copy(edge_ref.at[1], halo_ref.at[0], edge_send.at[1], edge_recv.at[0], near(1)),
    ]
    tile = grid_ref.at[core, major, minor, line_pair]
    for k in range(1, 8):
        each = copy(tile, tile, line_send.at[k - 1], line_recv.at[line_pair], place(x, y, in_line(sign * k)))
        each.start()
        copies.append(each)
    tiles = [line_pair] + [lax.div(in_line(sign * k if k % 2 else -sign * k), 2) for k in range(1, 8)]

    def go(src, dst, send_sem, recv_sem, device):
        each = copy(src, dst, send_sem, recv_sem, device)
        each.start()
        copies.append(each)

    def to_minors(k):
        t = tiles[k]
        src = grid_ref.at[core, major, minor, t]
        if k:
            copy(src, src, line_send.at[0], line_recv.at[t], near(1)).wait_recv()
        for by in (1, 2, 3):
            go(src, src, minor_send.at[by - 1, k], minor_recv.at[minor, t], minor_peer(turn(minor, by)))

    def to_majors(k):
        t = tiles[k]
        for by in (1, 2, 3):
            src = grid_ref.at[core, major, turn(minor, by), t]
            copy(src, src, minor_send.at[0, k], minor_recv.at[turn(minor, by), t], near(1)).wait_recv()
        src = grid_ref.at[core, major, :, t]
        for by in (1, 2, 3):
            go(src, src, major_send.at[by - 1, k], major_recv.at[major, t], major_peer(turn(major, by)))
        go(src, src, core_send.at[0, k], core_recv.at[major, t], other_core)

    def to_core(k):
        t = tiles[k]
        for by in (1, 2, 3):
            src = grid_ref.at[core, turn(major, by), :, t]
            copy(src, src, major_send.at[0, k], major_recv.at[turn(major, by), t], near(1)).wait_recv()
            go(src, src, core_send.at[by, k], core_recv.at[turn(major, by), t], other_core)

    for step in range(8 + LAG_MINOR + LAG_MAJOR):
        if step < 8:
            to_minors(step)
        if step == 0:
            for each in edges:
                each.start()
        if 0 <= step - LAG_MINOR < 8:
            to_majors(step - LAG_MINOR)
        if 0 <= step - LAG_MINOR - LAG_MAJOR < 8:
            to_core(step - LAG_MINOR - LAG_MAJOR)
    for by in range(RING):
        for k in range(8):
            src = grid_ref.at[1 - core, by, :, k]
            copy(src, src, core_send.at[0, k], core_recv.at[by, k], other_core).wait_recv()
    for slot in range(2):
        copy(edge_ref.at[0], halo_ref.at[slot], edge_send.at[0], edge_recv.at[slot], near(1)).wait_recv()
    for each in copies + edges:
        each.wait_send()


def spread(table, block_counts, steam, inner, parts, record, shares, cells):
    dma = pltpu.SemaphoreType.DMA
    vmem = pl.BlockSpec(memory_space=pltpu.VMEM)
    smem = pl.BlockSpec(memory_space=pltpu.SMEM)
    side = (2, FIELDS, TILES * LANES)
    return pl.pallas_call(
        spread_kernel,
        out_shape=(
            jax.ShapeDtypeStruct(record.shape, jnp.float32),
            jax.ShapeDtypeStruct((FIELDS * TILES * PLANES, LANES), jnp.float32),
            jax.ShapeDtypeStruct(side, jnp.float32),
            jax.ShapeDtypeStruct((2, RING, RING, LINE // 2, ROWS, LANES), jnp.float32),
        ),
        in_specs=[smem] * 3 + [vmem] * 5,
        out_specs=(vmem,) * 4,
        scratch_shapes=[
            pltpu.VMEM((ROWS, LANES), jnp.float32),
            pltpu.VMEM((ROWS, LANES), jnp.float32),
            pltpu.VMEM(side, jnp.float32),
            pltpu.VMEM((cells.shape[0], FIELDS, BLOCK), jnp.float32),
            pltpu.VMEM((EDGES + 1, FIELDS, BLOCK), jnp.float32),
            pltpu.VMEM((PAIRS + 1, FIELDS, CHUNK), jnp.float32),
            pltpu.VMEM((3, ROWS, LANES), jnp.float32),
            dma((3,)), dma((3,)), dma((2,)), dma((2,)), dma((7,)), dma((LINE // 2,)),
            dma((3, 8)), dma((RING, 8)), dma((3, 8)), dma((RING, 8)), dma((RING, 8)), dma((RING, 8)),
        ],
        compiler_params=pltpu.CompilerParams(
            collective_id=0, has_side_effects=True, vmem_limit_bytes=16 << 20
        ),
        name="spread",
    )(table, block_counts, steam, inner, parts, record, shares, cells)


def finish_kernel(moved_ref, base_ref, halo_ref, grid_ref, next_ref, fine_ref, out_ref, fine, source, even, uneven, flat, result, fine_sem, out_sem):
    next_ref[...] = moved_ref[...]
    sub = lax.broadcasted_iota(jnp.int32, (ROWS, LANES), 0)
    lane = lax.broadcasted_iota(jnp.int32, (ROWS, LANES), 1)
    first = sub == 0
    last = sub == ROWS - 1
    for f in range(FIELDS):
        for t in range(TILES):
            cols = slice(t * LANES, (t + 1) * LANES)
            rows = slice((f * TILES + t) * PLANES, (f * TILES + t + 1) * PLANES)
            low = jnp.broadcast_to(halo_ref[0, f : f + 1, cols], (PLANES, LANES))
            high = jnp.broadcast_to(halo_ref[1, f : f + 1, cols], (PLANES, LANES))
            fine[rows, :] = base_ref[rows, :] + jnp.where(first, low, jnp.where(last, high, 0.0))
    fine_copy = pltpu.make_async_copy(fine, fine_ref, fine_sem)
    fine_copy.start()

    wide = COARSE // 2
    none = jnp.zeros((wide, LANES), jnp.float32)
    for held in (even, uneven):
        held[0] = none
        held[COARSE + 1] = none
    for plane in range(COARSE):
        y_lo, x, j = plane // 32, (plane // 8) % RING, plane % 8
        for c in range(RING):
            y = (c // 2) * 2 + y_lo
            at = grid_ref[0, y, x, j] if c % 2 == 0 else grid_ref[1, x, y, j]
            value = at * (1.0 / 6.0)
            source[plane, c * ROWS : (c + 1) * ROWS, :] = value
            even[plane + 1, c * ROWS : (c + 1) * ROWS, :] = value

    half = LANES // 2
    depth = lax.rem(lane, half)
    upper = jnp.where(depth < half - 1, 1.0, 0.0)
    lower = jnp.where(depth > 0, 1.0, 0.0)
    left = lane < half
    blank = jnp.zeros((ROWS, LANES), jnp.float32)

    def relaxed(src, plane):
        mid = [src[plane + 1, c * ROWS : (c + 1) * ROWS, :] for c in range(RING)]
        turned = [pltpu.roll(value, half, 1) for value in mid]
        down = [blank] + [pltpu.roll(value, 1, 0) for value in turned]
        up = [pltpu.roll(value, ROWS - 1, 0) for value in turned] + [blank]
        for c in range(RING):
            tile = slice(c * ROWS, (c + 1) * ROWS)
            before = jnp.where(first, down[c], down[c + 1])
            after = jnp.where(last, up[c + 1], up[c])
            total = turned[c] + jnp.where(left, before, after)
            total += pltpu.roll(mid[c], LANES - 1, 1) * upper
            total += pltpu.roll(mid[c], 1, 1) * lower
            total += src[plane, tile, :] + src[plane + 2, tile, :]
            yield tile, total * (1.0 / 6.0) + source[plane, tile, :]

    def sweep(src, dst):
        def some(n, carry):
            for k in range(SPAN):
                plane = n * SPAN + k
                for tile, value in relaxed(src, plane):
                    dst[plane + 1, tile, :] = value
            return carry

        lax.fori_loop(0, COARSE // SPAN, some, 0)

    sweep(even, uneven)
    sweep(uneven, even)
    copies = []
    for group in range(COARSE // ROWS):
        for k in range(ROWS):
            plane = group * ROWS + k
            for tile, value in relaxed(even, plane):
                flat[plane * wide + tile.start : plane * wide + tile.stop, :] = value
        rows = slice(group * ROWS, (group + 1) * ROWS)
        for r in range(wide):
            value = flat[pl.ds(group * ROWS * wide + r, ROWS, stride=wide), :]
            result[rows, r * LANES : (r + 1) * LANES] = value
        each = pltpu.make_async_copy(result.at[rows], out_ref.at[rows], out_sem.at[group])
        each.start()
        copies.append(each)
    for each in copies:
        each.wait()
    fine_copy.wait()


def finish(moved, base, halo_sum, grid):
    wide = COARSE // 2
    vmem = pl.BlockSpec(memory_space=pltpu.VMEM)
    hbm = pl.BlockSpec(memory_space=pl.ANY)
    dma = pltpu.SemaphoreType.DMA
    return pl.pallas_call(
        finish_kernel,
        out_shape=(
            jax.ShapeDtypeStruct(moved.shape, jnp.float32),
            jax.ShapeDtypeStruct(base.shape, jnp.float32),
            jax.ShapeDtypeStruct((COARSE, COARSE * COARSE), jnp.float32),
        ),
        in_specs=[vmem] * 4,
        out_specs=(vmem, hbm, hbm),
        scratch_shapes=[
            pltpu.VMEM(base.shape, jnp.float32),
            pltpu.VMEM((COARSE, wide, LANES), jnp.float32),
            pltpu.VMEM((COARSE + 2, wide, LANES), jnp.float32),
            pltpu.VMEM((COARSE + 2, wide, LANES), jnp.float32),
            pltpu.VMEM((COARSE * wide, LANES), jnp.float32),
            pltpu.VMEM((COARSE, COARSE * COARSE), jnp.float32),
            dma, dma((COARSE // ROWS,)),
        ],
        compiler_params=pltpu.CompilerParams(vmem_limit_bytes=16 << 20),
        name="finish",
    )(moved, base, halo_sum, grid)


def body(gas_state, parcel_record, condensed_shares, surface_steam_factor, fine_cell, block_counts):
    rows = gas_state.reshape(FIELDS, PLANES, TILES, LANES).transpose(0, 2, 1, 3).reshape(-1, LANES)
    cells = fine_cell.reshape(-1, BLOCK)
    inner, outer, table = halo(cells, rows)
    moved, base, halo_sum, grid = spread(
        table, block_counts, surface_steam_factor, inner, outer, parcel_record, condensed_shares, cells
    )
    parcel_next, fine_rows, correction = finish(moved, base, halo_sum, grid)
    fine_source = fine_rows.reshape(FIELDS, TILES, PLANES, LANES).transpose(0, 2, 1, 3).reshape(gas_state.shape)
    return (parcel_next, fine_source, correction)


def solution(mesh):
    in_specs = (
        P(None, "slab", "cross"),
        P(None, ("slab", "cross")),
        P(None, ("slab", "cross")),
        P(),
        P(("slab", "cross")),
        P(("slab", "cross")),
    )
    out_specs = (P(None, ("slab", "cross")), P(None, "slab", "cross"), P())
    return jax.shard_map(body, mesh=mesh, in_specs=in_specs, out_specs=out_specs, check_vma=False)
```

```python
import jax
import jax.numpy as jnp
from jax import lax
from jax.experimental import pallas as pl
from jax.experimental.pallas import tpu as pltpu
from jax.sharding import PartitionSpec as P

BLOCK = 128
COARSE = 64


drag_rate = 0.5
evap_rate = 0.08
warming_speed = 0.3
latent_boiling_energy = 0.5
vapour_heat = 1.5
volume_inverse = 4.0


LINE = 16
RING = 4
LANES = 128
ROWS = 8
FIELDS = 16
PLANES = 8
TILES = 16
CHUNK = 256
PER_PLANE = 8
SHIFT = 8
UNROLL = 16
STEP = 8
PAIRS = 112
EDGES = 48
LAST = 2
ENDS = 3
EDGE_BLOCK = 4
EDGE_ENDS = 6
LAG_MINOR = 5
LAG_MAJOR = 5
SPAN = 16


def parts_of(value):
    high = value.astype(jnp.bfloat16)
    rest = value - high.astype(jnp.float32)
    middle = rest.astype(jnp.bfloat16)
    low = (rest - middle.astype(jnp.float32)).astype(jnp.bfloat16)
    return jnp.concatenate([high, middle, low], axis=0)


def joined(value):
    third = value.shape[0] // 3
    return value[:third] + (value[third : 2 * third] + value[2 * third :])


def chosen(row, cells, chunk):
    place = cells - jnp.where(chunk < 0, (PLANES + 2) * PER_PLANE, chunk) * CHUNK
    place = jnp.where((place < 0) | (place >= CHUNK), -1, place)
    place = place.astype(jnp.float32).astype(jnp.bfloat16)
    return jnp.where(row == place, jnp.bfloat16(1), jnp.bfloat16(0))


def chunk_rows():
    row = lax.broadcasted_iota(jnp.int32, (CHUNK, BLOCK), 0)
    return row.astype(jnp.float32).astype(jnp.bfloat16)


def within(value, top):
    return jnp.minimum(jnp.maximum(value, 0), top)


def plane_rows(tile, plane):
    return pl.ds(tile * PLANES + plane, FIELDS, stride=TILES * PLANES)


def send(src, dst, send_sem, recv_sem, device):
    return pltpu.make_async_remote_copy(
        src_ref=src, dst_ref=dst, send_sem=send_sem, recv_sem=recv_sem,
        device_id=device, device_id_type=pl.DeviceIdType.MESH,
    )


def list_pairs(cell_ref, table):
    blocks = cell_ref.shape[0]
    chunks = (PLANES + 2) * PER_PLANE
    first = lax.shift_right_logical(cell_ref[:, 0:1], SHIFT).astype(jnp.float32)
    last = lax.shift_right_logical(cell_ref[:, BLOCK - 1 : BLOCK], SHIFT).astype(jnp.float32)
    lane = lax.broadcasted_iota(jnp.int32, (blocks, LANES), 1).astype(jnp.float32)
    sub = lax.broadcasted_iota(jnp.int32, (blocks, LANES), 0).astype(jnp.float32)
    spot = lane[0:1]

    def over_blocks(value):
        return jnp.sum(value, axis=0, keepdims=True)

    def as_row(column):
        return over_blocks(jnp.where(sub == lane, column, 0.0))

    def starts(column):
        return jnp.sum(jnp.where(lane < sub, as_row(column), 0.0), axis=1, keepdims=True)

    def owner(start):
        return over_blocks(jnp.where(start <= lane, 1.0, 0.0)) - 1.0

    def at(block, column):
        return over_blocks(jnp.where(sub == block, column, 0.0))

    def put(row, value, low, high):
        table[row : row + 1, :] = jnp.clip(value.astype(jnp.int32), low, high)

    count = last - first + 1.0
    start = starts(count)
    block = owner(start)
    real = spot < over_blocks(count)
    put(0, jnp.where(real, block, 0.0), 0, blocks - 1)
    put(1, jnp.where(real, spot + at(block, first - start), -1.0), -1, chunks - 1)
    deep = owner(first)
    held = (deep >= 0.0) & (at(deep, last) >= spot)
    put(LAST, jnp.where(held, spot + at(deep, start - first), float(PAIRS)), 0, PAIRS)
    put(ENDS, as_row(start + count - 1.0), 0, PAIRS)

    top = float((PLANES + 1) * PER_PLANE)
    low = jnp.maximum(jnp.minimum(last, PER_PLANE - 1.0) - first + 1.0, 0.0)
    from_high = jnp.maximum(first, top)
    edges = low + jnp.maximum(last - from_high + 1.0, 0.0)
    start = starts(edges)
    block = owner(start)
    real = spot < over_blocks(edges)
    inside = spot - at(block, start)
    kept = at(block, low)
    chunk = jnp.where(inside < kept, at(block, first) + inside, at(block, from_high) + inside - kept)
    put(EDGE_BLOCK, jnp.where(real, block, 0.0), 0, blocks - 1)
    put(EDGE_BLOCK + 1, jnp.where(real, chunk, -1.0), -1, chunks - 1)
    put(EDGE_ENDS, as_row(jnp.where(edges > 0.0, start + edges - 1.0, float(EDGES))), 0, EDGES)


def gather(table, start, steps, unroll, cell_ref, held, slots):
    row = chunk_rows()

    def step(n, carry):
        total, before = carry
        for k in range(unroll):
            i = n * unroll + k
            b = within(table[start, i], cell_ref.shape[0] - 1)
            c = table[start + 1, i]
            part = jnp.dot(
                held(within(c, (PLANES + 2) * PER_PLANE - 1)), chosen(row, cell_ref[pl.ds(b, 1), :], c),
                preferred_element_type=jnp.float32,
            )
            total = joined(part) + total * jnp.where(b == before, 1.0, 0.0)
            slots[i] = total
            before = b
        return total, before

    none = jnp.zeros((FIELDS, BLOCK), jnp.float32)
    lax.fori_loop(0, steps // unroll, step, (none, -1))
    slots[steps] = none


def halo_kernel(
    cell_ref, gas_ref, inner_ref, outer_ref, table_ref, parts_ref, sent, got, table, table_sem, send_sem, recv_sem
):
    slabs = 2 * RING * LINE
    slab = lax.axis_index("slab")
    cross = lax.axis_index("cross")
    below = (lax.rem(slab - 1 + slabs, slabs), cross)
    above = (lax.rem(slab + 1, slabs), cross)
    barrier = pltpu.get_barrier_semaphore()
    for device in (below, above):
        pl.semaphore_signal(barrier, inc=1, device_id=device, device_id_type=pl.DeviceIdType.MESH)
    list_pairs(cell_ref, table_ref)
    table_ref[ROWS - 1 :, :] = jnp.zeros((1, LANES), jnp.int32)
    for side, plane in ((0, 0), (1, PLANES - 1)):
        for t in range(TILES):
            sent[side, :, t * LANES : (t + 1) * LANES] = gas_ref[plane_rows(t, plane), :]
    pl.semaphore_wait(barrier, 2)
    table_copy = pltpu.make_async_copy(table_ref, table, table_sem)
    copies = [
        send(sent.at[0], got.at[1], send_sem.at[0], recv_sem.at[1], below),
        send(sent.at[1], got.at[0], send_sem.at[1], recv_sem.at[0], above),
    ]
    for each in copies:
        each.start()
    table_copy.start()
    group = CHUNK // LANES
    for p in range(PLANES):
        for q in range(PER_PLANE):
            value = [gas_ref[plane_rows(q * group + t, p), :] for t in range(group)]
            parts_ref[(p + 1) * PER_PLANE + q] = parts_of(jnp.concatenate(value, axis=1))
    none = jnp.zeros(parts_ref.shape[1:], jnp.bfloat16)
    for q in range(PER_PLANE):
        parts_ref[q] = none
        parts_ref[(PLANES + 1) * PER_PLANE + q] = none
    table_copy.wait()
    gather(table, 0, PAIRS, UNROLL, cell_ref, lambda c: parts_ref[c], inner_ref)
    for side in (0, 1):
        send(sent.at[0], got.at[side], send_sem.at[0], recv_sem.at[side], above).wait_recv()
        for q in range(PER_PLANE):
            outer_ref[side * PER_PLANE + q] = parts_of(got[side, :, q * CHUNK : (q + 1) * CHUNK])
    for each in copies:
        each.wait_send()


def halo(cells, gas_rows):
    vmem = pl.BlockSpec(memory_space=pltpu.VMEM)
    dma = pltpu.SemaphoreType.DMA
    chunks = (PLANES + 2) * PER_PLANE
    parts = (3 * FIELDS, CHUNK)
    return pl.pallas_call(
        halo_kernel,
        out_shape=(
            jax.ShapeDtypeStruct((PAIRS + 1, FIELDS, BLOCK), jnp.float32),
            jax.ShapeDtypeStruct((2 * PER_PLANE,) + parts, jnp.bfloat16),
            jax.ShapeDtypeStruct((ROWS, LANES), jnp.int32),
        ),
        in_specs=[vmem, vmem],
        out_specs=(vmem, vmem, vmem),
        scratch_shapes=[
            pltpu.VMEM((chunks,) + parts, jnp.bfloat16),
            pltpu.VMEM((2, FIELDS, TILES * LANES), jnp.float32),
            pltpu.VMEM((2, FIELDS, TILES * LANES), jnp.float32),
            pltpu.SMEM((ROWS, LANES), jnp.int32),
            dma, dma((2,)), dma((2,)),
        ],
        compiler_params=pltpu.CompilerParams(
            collective_id=1, has_side_effects=True, vmem_limit_bytes=16 << 20
        ),
        name="halo",
    )(cells, gas_rows)


def advance(table, count_at, steam_ref, inner_ref, outer_ref, record_ref, shares_ref, cell_ref, next_ref, terms, slots):
    def held(c):
        return outer_ref[within(jnp.where(c < PER_PLANE, c, c - PLANES * PER_PLANE), 2 * PER_PLANE - 1)]

    blocks = cell_ref.shape[0]
    gather(table, EDGE_BLOCK, EDGES, UNROLL, cell_ref, held, slots)
    lane = lax.broadcasted_iota(jnp.int32, (1, BLOCK), 1)
    species = lax.broadcasted_iota(jnp.int32, (steam_ref.shape[0], BLOCK), 0)
    steam = jnp.zeros(species.shape, jnp.float32)
    for k in range(steam_ref.shape[0]):
        steam = jnp.where(species == k, steam_ref[k], steam)

    def step(n, carry):
        for k in range(STEP):
            b = n * STEP + k
            cols = pl.ds(pl.multiple_of(b * BLOCK, BLOCK), BLOCK)
            gas = inner_ref[within(table[ENDS, b], PAIRS)] + slots[within(table[EDGE_ENDS, b], EDGES)]
            record = record_ref[:, cols]
            alive = lane < count_at[b]
            gas_velocity, gas_heat, vapour = gas[0:3], gas[3:4], gas[4:]
            velocity, heat, weight = record[0:3], record[3:4], record[4:5]
            slip = gas_velocity - velocity
            slip = slip * slip
            slip = slip[0:1] + slip[1:2] + slip[2:3]
            log_weight = jnp.log(weight)
            factor = drag_rate * jnp.exp(log_weight * (-2.0 / 3.0))
            factor = factor * (1.0 + 0.15 * jnp.exp(0.3435 * jnp.log(slip + 1.0)))
            moved = (velocity + factor * gas_velocity) / (1.0 + factor)
            surface = shares_ref[:, cols] * steam * jnp.exp(2.0 * (heat - 0.75))
            rates = evap_rate * weight * (surface - vapour)
            lost = jnp.sum(rates, axis=0, keepdims=True)
            exchange = warming_speed * (gas_heat - heat) * jnp.exp(log_weight * (1.0 / 3.0))
            warmed = heat + (exchange - latent_boiling_energy * lost) / weight
            scale = jnp.where(alive, volume_inverse, 0.0)
            terms[b, 0:3] = (weight * (velocity - moved) + lost * moved) * scale
            terms[b, 3:4] = (vapour_heat * lost - exchange) * scale
            terms[b, 4:16] = rates * scale
            next_ref[0:3, cols] = jnp.where(alive, moved, velocity)
            next_ref[3:4, cols] = jnp.where(alive, warmed, heat)
            next_ref[4:5, cols] = jnp.where(alive, weight - lost, weight)
        return carry

    lax.fori_loop(0, blocks // STEP, step, 0)


def scatter(table, cell_ref, terms_ref, edge, slots):
    row = chunk_rows()

    def step(n, carry):
        total, before = carry
        for k in range(UNROLL):
            i = n * UNROLL + k
            b = within(table[0, i], cell_ref.shape[0] - 1)
            c = table[1, i]
            picked = chosen(row, cell_ref[pl.ds(b, 1), :], c)
            part = lax.dot_general(
                parts_of(terms_ref[b]), picked, (((1,), (1,)), ((), ())),
                preferred_element_type=jnp.float32,
            )
            total = joined(part) + total * jnp.where(c == before, 1.0, 0.0)
            slots[i] = total
            before = c
        return total, before

    none = jnp.zeros((FIELDS, CHUNK), jnp.float32)
    lax.fori_loop(0, PAIRS // UNROLL, step, (none, -2))
    slots[PAIRS] = none

    fold_row = lax.broadcasted_iota(jnp.int32, (CHUNK, LANES), 0)
    fold_lane = lax.broadcasted_iota(jnp.int32, (CHUNK, LANES), 1)
    fold = jnp.where(lax.shift_right_logical(fold_row, 1) == fold_lane, 1.0, 0.0).astype(jnp.bfloat16)

    def mass(value):
        kept = jnp.sum(value[4:], axis=0, keepdims=True)
        return [joined(jnp.dot(parts_of(kept), fold, preferred_element_type=jnp.float32))]

    own, low, high = [], [], []
    for q in range(PER_PLANE):
        cols = slice(q * CHUNK, (q + 1) * CHUNK)
        below = slots[within(table[LAST, q], PAIRS)]
        above = slots[within(table[LAST, (PLANES + 1) * PER_PLANE + q], PAIRS)]
        edge[0, :, cols] = below
        edge[1, :, cols] = above
        inside = None
        for p in range(PLANES):
            value = slots[within(table[LAST, (p + 1) * PER_PLANE + q], PAIRS)]
            inside = value if inside is None else inside + value
        own += mass(inside)
        low += mass(below)
        high += mass(above)
    return tuple(0.25 * jnp.concatenate(rows, axis=0) for rows in (own, low, high))


def place_rows(table, slots, base_ref):
    group = CHUNK // LANES
    for q in range(PER_PLANE):
        for p in range(PLANES):
            value = slots[within(table[LAST, (p + 1) * PER_PLANE + q], PAIRS)]
            for t in range(group):
                base_ref[plane_rows(q * group + t, p), :] = value[:, t * LANES : (t + 1) * LANES]


def spread_kernel(
    table, count_at, steam_ref, inner_ref, parts_ref, record_ref, shares_ref, cell_ref,
    next_ref, base_ref, halo_ref, grid_ref, own_ref, outer_ref, edge_ref, terms, edge_slots, slots, got,
    pair_send, pair_recv, edge_send, edge_recv, line_send, line_recv,
    minor_send, minor_recv, major_send, major_recv, core_send, core_recv,
):
    slabs = 2 * RING * LINE
    slab = lax.axis_index("slab")
    cross = lax.axis_index("cross")
    core = lax.rem(cross, 2)
    z = lax.rem(slab, LINE)
    x = lax.rem(lax.div(slab, LINE), RING)
    y = lax.div(cross, 2) * 2 + lax.div(slab, RING * LINE)
    odd = lax.rem(slab, 2)
    sign = 2 * odd - 1
    pair = lax.div(slab, 2)
    line_pair = lax.div(z, 2)
    major = core * x + (1 - core) * y
    minor = core * y + (1 - core) * x

    def near(by):
        return (lax.rem(slab + by + slabs, slabs), cross)

    def place(at_x, at_y, at_z):
        return (lax.rem(at_y, 2) * (RING * LINE) + at_x * LINE + at_z, lax.div(at_y, 2) * 2 + core)

    def in_line(by):
        return lax.rem(z + by + LINE, LINE)

    def minor_peer(other):
        return place(core * x + (1 - core) * other, core * other + (1 - core) * y, z)

    def major_peer(other):
        return place(core * other + (1 - core) * x, core * y + (1 - core) * other, z)

    def turn(own, by):
        return lax.rem(own + by, RING)

    copy = send

    other_core = (slab, cross + 1 - 2 * core)
    line_from = [sign * k for k in (1, 3, 5, 7)] + [-sign * k for k in (2, 4, 6)]
    low = lax.rem(2 * pair - 1 + slabs, slabs)
    high = lax.rem(2 * pair + 2, slabs)

    barrier = pltpu.get_barrier_semaphore()
    sources = [near(-sign), (low, cross), (high, cross), near(-1), near(1)]
    sources += [place(x, y, in_line(by)) for by in line_from]
    sources += [minor_peer(turn(minor, by)) for by in (1, 2, 3)]
    sources += [major_peer(turn(major, by)) for by in (1, 2, 3)]
    sources += [other_core]
    for device in sources:
        pl.semaphore_signal(barrier, inc=1, device_id=device, device_id_type=pl.DeviceIdType.MESH)
    advance(
        table, count_at, steam_ref, inner_ref, parts_ref, record_ref, shares_ref, cell_ref,
        next_ref, terms, edge_slots,
    )
    own, low_tile, high_tile = scatter(table, cell_ref, terms, edge_ref, slots)
    own_ref[...] = own + jnp.where(odd == 1, low_tile, high_tile)
    outer_ref[...] = jnp.where(odd == 1, high_tile, low_tile)
    pl.semaphore_wait(barrier, len(sources))

    copies = [
        copy(own_ref, got.at[0], pair_send.at[0], pair_recv.at[0], near(-sign)),
        copy(outer_ref, got.at[2 - odd], pair_send.at[1], pair_recv.at[2 - odd], near(sign)),
        copy(outer_ref, got.at[2 - odd], pair_send.at[2], pair_recv.at[2 - odd], near(2 * sign)),
    ]
    for each in copies:
        each.start()
    for slot in range(3):
        copy(own_ref, got.at[slot], pair_send.at[slot], pair_recv.at[slot], near(1)).wait_recv()
    grid_ref[core, major, minor, line_pair] = (own_ref[...] + got[0]) + (got[1] + got[2])
    edges = [
        copy(edge_ref.at[0], halo_ref.at[1], edge_send.at[0], edge_recv.at[1], near(-1)),
        copy(edge_ref.at[1], halo_ref.at[0], edge_send.at[1], edge_recv.at[0], near(1)),
    ]
    tile = grid_ref.at[core, major, minor, line_pair]
    for k in range(1, 8):
        each = copy(tile, tile, line_send.at[k - 1], line_recv.at[line_pair], place(x, y, in_line(sign * k)))
        each.start()
        copies.append(each)
    tiles = [line_pair] + [lax.div(in_line(sign * k if k % 2 else -sign * k), 2) for k in range(1, 8)]

    def go(src, dst, send_sem, recv_sem, device):
        each = copy(src, dst, send_sem, recv_sem, device)
        each.start()
        copies.append(each)

    def to_minors(k):
        t = tiles[k]
        src = grid_ref.at[core, major, minor, t]
        if k:
            copy(src, src, line_send.at[0], line_recv.at[t], near(1)).wait_recv()
        for by in (1, 2, 3):
            go(src, src, minor_send.at[by - 1, k], minor_recv.at[minor, t], minor_peer(turn(minor, by)))

    def to_majors(k):
        t = tiles[k]
        for by in (1, 2, 3):
            src = grid_ref.at[core, major, turn(minor, by), t]
            copy(src, src, minor_send.at[0, k], minor_recv.at[turn(minor, by), t], near(1)).wait_recv()
        src = grid_ref.at[core, major, :, t]
        for by in (1, 2, 3):
            go(src, src, major_send.at[by - 1, k], major_recv.at[major, t], major_peer(turn(major, by)))
        go(src, src, core_send.at[0, k], core_recv.at[major, t], other_core)

    def to_core(k):
        t = tiles[k]
        for by in (1, 2, 3):
            src = grid_ref.at[core, turn(major, by), :, t]
            copy(src, src, major_send.at[0, k], major_recv.at[turn(major, by), t], near(1)).wait_recv()
            go(src, src, core_send.at[by, k], core_recv.at[turn(major, by), t], other_core)

    for step in range(8 + LAG_MINOR + LAG_MAJOR):
        if step < 8:
            to_minors(step)
        if step == 0:
            for each in edges:
                each.start()
            place_rows(table, slots, base_ref)
        if 0 <= step - LAG_MINOR < 8:
            to_majors(step - LAG_MINOR)
        if 0 <= step - LAG_MINOR - LAG_MAJOR < 8:
            to_core(step - LAG_MINOR - LAG_MAJOR)
    for by in range(RING):
        for k in range(8):
            src = grid_ref.at[1 - core, by, :, k]
            copy(src, src, core_send.at[0, k], core_recv.at[by, k], other_core).wait_recv()
    for slot in range(2):
        copy(edge_ref.at[0], halo_ref.at[slot], edge_send.at[0], edge_recv.at[slot], near(1)).wait_recv()
    for each in copies + edges:
        each.wait_send()


def spread(table, block_counts, steam, inner, parts, record, shares, cells):
    dma = pltpu.SemaphoreType.DMA
    vmem = pl.BlockSpec(memory_space=pltpu.VMEM)
    smem = pl.BlockSpec(memory_space=pltpu.SMEM)
    side = (2, FIELDS, TILES * LANES)
    return pl.pallas_call(
        spread_kernel,
        out_shape=(
            jax.ShapeDtypeStruct(record.shape, jnp.float32),
            jax.ShapeDtypeStruct((FIELDS * TILES * PLANES, LANES), jnp.float32),
            jax.ShapeDtypeStruct(side, jnp.float32),
            jax.ShapeDtypeStruct((2, RING, RING, LINE // 2, ROWS, LANES), jnp.float32),
        ),
        in_specs=[smem] * 3 + [vmem] * 5,
        out_specs=(vmem,) * 4,
        scratch_shapes=[
            pltpu.VMEM((ROWS, LANES), jnp.float32),
            pltpu.VMEM((ROWS, LANES), jnp.float32),
            pltpu.VMEM(side, jnp.float32),
            pltpu.VMEM((cells.shape[0], FIELDS, BLOCK), jnp.float32),
            pltpu.VMEM((EDGES + 1, FIELDS, BLOCK), jnp.float32),
            pltpu.VMEM((PAIRS + 1, FIELDS, CHUNK), jnp.float32),
            pltpu.VMEM((3, ROWS, LANES), jnp.float32),
            dma((3,)), dma((3,)), dma((2,)), dma((2,)), dma((7,)), dma((LINE // 2,)),
            dma((3, 8)), dma((RING, 8)), dma((3, 8)), dma((RING, 8)), dma((RING, 8)), dma((RING, 8)),
        ],
        compiler_params=pltpu.CompilerParams(
            collective_id=0, has_side_effects=True, vmem_limit_bytes=16 << 20
        ),
        name="spread",
    )(table, block_counts, steam, inner, parts, record, shares, cells)


def finish_kernel(moved_ref, base_ref, halo_ref, grid_ref, next_ref, fine_ref, out_ref, fine, source, even, uneven, flat, result, next_sem, fine_sem, out_sem):
    next_copy = pltpu.make_async_copy(moved_ref, next_ref, next_sem)
    next_copy.start()
    sub = lax.broadcasted_iota(jnp.int32, (ROWS, LANES), 0)
    lane = lax.broadcasted_iota(jnp.int32, (ROWS, LANES), 1)
    first = sub == 0
    last = sub == ROWS - 1
    for f in range(FIELDS):
        for t in range(TILES):
            cols = slice(t * LANES, (t + 1) * LANES)
            rows = slice((f * TILES + t) * PLANES, (f * TILES + t + 1) * PLANES)
            low = jnp.broadcast_to(halo_ref[0, f : f + 1, cols], (PLANES, LANES))
            high = jnp.broadcast_to(halo_ref[1, f : f + 1, cols], (PLANES, LANES))
            fine[rows, :] = base_ref[rows, :] + jnp.where(first, low, jnp.where(last, high, 0.0))
    fine_copy = pltpu.make_async_copy(fine, fine_ref, fine_sem)
    fine_copy.start()

    wide = COARSE // 2
    none = jnp.zeros((wide, LANES), jnp.float32)
    for held in (even, uneven):
        held[0] = none
        held[COARSE + 1] = none
    for plane in range(COARSE):
        y_lo, x, j = plane // 32, (plane // 8) % RING, plane % 8
        for c in range(RING):
            y = (c // 2) * 2 + y_lo
            at = grid_ref[0, y, x, j] if c % 2 == 0 else grid_ref[1, x, y, j]
            value = at * (1.0 / 6.0)
            source[plane, c * ROWS : (c + 1) * ROWS, :] = value
            even[plane + 1, c * ROWS : (c + 1) * ROWS, :] = value

    half = LANES // 2
    depth = lax.rem(lane, half)
    upper = jnp.where(depth < half - 1, 1.0, 0.0)
    lower = jnp.where(depth > 0, 1.0, 0.0)
    left = lane < half
    blank = jnp.zeros((ROWS, LANES), jnp.float32)

    def relaxed(src, plane):
        mid = [src[plane + 1, c * ROWS : (c + 1) * ROWS, :] for c in range(RING)]
        turned = [pltpu.roll(value, half, 1) for value in mid]
        down = [blank] + [pltpu.roll(value, 1, 0) for value in turned]
        up = [pltpu.roll(value, ROWS - 1, 0) for value in turned] + [blank]
        for c in range(RING):
            tile = slice(c * ROWS, (c + 1) * ROWS)
            before = jnp.where(first, down[c], down[c + 1])
            after = jnp.where(last, up[c + 1], up[c])
            total = turned[c] + jnp.where(left, before, after)
            total += pltpu.roll(mid[c], LANES - 1, 1) * upper
            total += pltpu.roll(mid[c], 1, 1) * lower
            total += src[plane, tile, :] + src[plane + 2, tile, :]
            yield tile, total * (1.0 / 6.0) + source[plane, tile, :]

    def sweep(src, dst):
        def some(n, carry):
            for k in range(SPAN):
                plane = n * SPAN + k
                for tile, value in relaxed(src, plane):
                    dst[plane + 1, tile, :] = value
            return carry

        lax.fori_loop(0, COARSE // SPAN, some, 0)

    sweep(even, uneven)
    sweep(uneven, even)
    copies = []
    for group in range(COARSE // ROWS):
        for k in range(ROWS):
            plane = group * ROWS + k
            for tile, value in relaxed(even, plane):
                flat[plane * wide + tile.start : plane * wide + tile.stop, :] = value
        rows = slice(group * ROWS, (group + 1) * ROWS)
        for r in range(wide):
            value = flat[pl.ds(group * ROWS * wide + r, ROWS, stride=wide), :]
            result[rows, r * LANES : (r + 1) * LANES] = value
        each = pltpu.make_async_copy(result.at[rows], out_ref.at[rows], out_sem.at[group])
        each.start()
        copies.append(each)
    for each in copies:
        each.wait()
    fine_copy.wait()
    next_copy.wait()


def finish(moved, base, halo_sum, grid):
    wide = COARSE // 2
    vmem = pl.BlockSpec(memory_space=pltpu.VMEM)
    hbm = pl.BlockSpec(memory_space=pl.ANY)
    dma = pltpu.SemaphoreType.DMA
    return pl.pallas_call(
        finish_kernel,
        out_shape=(
            jax.ShapeDtypeStruct(moved.shape, jnp.float32),
            jax.ShapeDtypeStruct(base.shape, jnp.float32),
            jax.ShapeDtypeStruct((COARSE, COARSE * COARSE), jnp.float32),
        ),
        in_specs=[vmem] * 4,
        out_specs=(hbm, hbm, hbm),
        scratch_shapes=[
            pltpu.VMEM(base.shape, jnp.float32),
            pltpu.VMEM((COARSE, wide, LANES), jnp.float32),
            pltpu.VMEM((COARSE + 2, wide, LANES), jnp.float32),
            pltpu.VMEM((COARSE + 2, wide, LANES), jnp.float32),
            pltpu.VMEM((COARSE * wide, LANES), jnp.float32),
            pltpu.VMEM((COARSE, COARSE * COARSE), jnp.float32),
            dma, dma, dma((COARSE // ROWS,)),
        ],
        compiler_params=pltpu.CompilerParams(vmem_limit_bytes=16 << 20),
        name="finish",
    )(moved, base, halo_sum, grid)


def body(gas_state, parcel_record, condensed_shares, surface_steam_factor, fine_cell, block_counts):
    rows = gas_state.reshape(FIELDS, PLANES, TILES, LANES).transpose(0, 2, 1, 3).reshape(-1, LANES)
    cells = fine_cell.reshape(-1, BLOCK)
    inner, outer, table = halo(cells, rows)
    moved, base, halo_sum, grid = spread(
        table, block_counts, surface_steam_factor, inner, outer, parcel_record, condensed_shares, cells
    )
    parcel_next, fine_rows, correction = finish(moved, base, halo_sum, grid)
    fine_source = fine_rows.reshape(FIELDS, TILES, PLANES, LANES).transpose(0, 2, 1, 3).reshape(gas_state.shape)
    return (parcel_next, fine_source, correction)


def solution(mesh):
    in_specs = (
        P(None, "slab", "cross"),
        P(None, ("slab", "cross")),
        P(None, ("slab", "cross")),
        P(),
        P(("slab", "cross")),
        P(("slab", "cross")),
    )
    out_specs = (P(None, ("slab", "cross")), P(None, "slab", "cross"), P())
    return jax.shard_map(body, mesh=mesh, in_specs=in_specs, out_specs=out_specs, check_vma=False)
```
